256 devices in a mesh: tmpl: 2 (over core), row: 128 (over x, y, z).
Axes of the slice: x: 4, y: 4, z: 8, core: 2. Of those that a mesh axis runs over, the one named last changes fastest.
Arguments:
- pair_maps: bfloat16 [2, 2048, 2048, 64], P('tmpl', 'row'), may hold values from -6 to 6
- crop_tiles: int32 [2, 8], P('tmpl'), may hold values from 0 to 15, as said below
- full_length: int32 [1], replicated, may hold values from 1536 to 2048
- proj_weight: bfloat16 [2, 64, 320], replicated, may hold values from -0.75 to 0.75
- out_weight: bfloat16 [2, 64, 64], replicated, may hold values from -0.75 to 0.75
- final_weight: bfloat16 [64, 128], replicated, may hold values from -0.75 to 0.75
Outputs:
- embedding: bfloat16 [128, 1024, 1024], P(None, 'row')
The draws below stay inside these ranges and needn't reach their ends.
Inputs may be any that keep to these rules, and one draw needn't show every extreme that they name: Each row of crop_tiles names 8 different tiles of the 16, in increasing order; its last 4 entries are the tiles 16 - 8 // 2 to 15.
All inputs are finite; a program needn't handle non-finite values.
Results may differ from the reference program's by a relative error of at most 0.014.
Values may be sent and summed in bfloat16 or wider, within the bound.
No kernel may reach another device: no remote copies, remote signals or barrier semaphores. Data moves between devices by JAX's collectives and lax.ppermute only.
A program may use at most 64 MiB of HBM per device.

```python
import jax
import jax.numpy as jnp
from jax import lax

CH = 64
CZ = 128
CROP = 1024
TILE = 128
NLAYER = 2
FULL = 2048
TEMPLATES = 2
NTILES = 16
NCROP = 8


def draw_crop_tiles(key, part):
    keys = jax.random.split(jax.random.fold_in(key, 17), TEMPLATES)
    tail_count = NCROP // 2
    head_pool = NTILES - tail_count
    tail_tiles = (jnp.arange(tail_count, dtype=jnp.int32) + head_pool).astype(jnp.int32)

    def one_template(single_key):
        order = jax.random.permutation(single_key, head_pool)
        head_tiles = jnp.sort(order[:NCROP - tail_count]).astype(jnp.int32)
        return jnp.concatenate([head_tiles, tail_tiles]).astype(jnp.int32)
    return jax.vmap(one_template)(keys)


def shard_levels(key, dims, cuts, smallest, top_value):
    gain, own = 1.0, jax.random.fold_in(key, 6)
    for dim, shards_of in cuts:
        steps = jnp.exp(jax.random.uniform(jax.random.fold_in(own, dim), (shards_of,), jnp.float32, smallest / len(cuts), top_value / len(cuts)))
        gain = gain * jnp.repeat(steps, dims[dim] // shards_of).reshape([-1 if axis == dim else 1 for axis in range(len(dims))])
    return gain


def gaussian(rng, dims, scale, bound, cuts=(), held_as=jnp.bfloat16):
    values = jax.random.normal(rng, dims, jnp.float32) * scale
    if len(cuts) > 0:
        values = shard_levels(rng, dims, cuts, -0.22, 0.18) * values
    return jnp.clip(values, min=-bound, max=bound).astype(held_as)


def setup_inputs(seed: int = 0) -> dict:
    streams_of = jax.random.split(jax.random.key(seed), 7)
    pair_maps = gaussian(streams_of[0], (TEMPLATES, FULL, FULL, CH), 1.0, 6.0, ((0, 2), (1, 128)))
    crop_tiles = draw_crop_tiles(jax.random.fold_in(streams_of[6], 71), 0)
    full_length = jax.random.randint(streams_of[2], (1,), FULL - CROP // 2, FULL + 1).astype(jnp.int32)
    proj_weight = gaussian(streams_of[3], (NLAYER, CH, 5 * CH), CH ** -0.5, 0.75)
    out_weight = gaussian(streams_of[4], (NLAYER, CH, CH), CH ** -0.5, 0.75)
    final_weight = gaussian(streams_of[5], (CH, CZ), CH ** -0.5, 0.75)
    return {"pair_maps": pair_maps, "crop_tiles": crop_tiles, "full_length": full_length, "proj_weight": proj_weight, "out_weight": out_weight, "final_weight": final_weight}


EPSILON = 1e-05

def channel_norm(values, axis_pos):
    center = values - lax.optimization_barrier(jnp.mean(values, axis=axis_pos, keepdims=True))
    spread = lax.optimization_barrier(jnp.mean(center * center, axis=axis_pos, keepdims=True))
    return center * lax.rsqrt(spread + EPSILON)

def outgoing_layer(current, usable, w_proj, w_out):
    normed_in = channel_norm(current.astype(jnp.float32), -1).astype(jnp.bfloat16)
    projected = jnp.dot(normed_in.reshape(-1, CH), w_proj, preferred_element_type=jnp.float32).reshape(CROP, CROP, 5 * CH)
    pair_mask = (usable[:, None] * usable[None, :])[:, :, None]
    left_proj = (jax.nn.sigmoid(projected[..., :CH]) * projected[..., CH:2 * CH] * pair_mask).astype(jnp.bfloat16)
    right_proj = (jax.nn.sigmoid(projected[..., 2 * CH:3 * CH]) * projected[..., 3 * CH:4 * CH] * pair_mask).astype(jnp.bfloat16)
    gate_vals = jax.nn.sigmoid(projected[..., 4 * CH:])
    left_first = jnp.transpose(left_proj, (2, 0, 1)).astype(jnp.float32)
    right_first = jnp.transpose(right_proj, (2, 0, 1)).astype(jnp.float32)
    products = jnp.einsum('cik,cjk->cij', left_first, right_first).astype(jnp.bfloat16)
    products = jnp.transpose(products, (1, 2, 0))
    normed_out = channel_norm(products.astype(jnp.float32), -1).astype(jnp.bfloat16)
    update = jnp.dot(normed_out.reshape(-1, CH), w_out, preferred_element_type=jnp.float32).reshape(CROP, CROP, CH)
    return (current.astype(jnp.float32) + gate_vals * update).astype(jnp.bfloat16)

def reference(pair_maps, crop_tiles, full_length, proj_weight, out_weight, final_weight):
    total = jnp.zeros((CROP, CROP, CH), jnp.float32)
    steps_crop = jnp.arange(CROP, dtype=jnp.int32)
    for template_idx in range(TEMPLATES):
        crop_ids = crop_tiles[template_idx].astype(jnp.int32)
        position = crop_ids[steps_crop // TILE] * TILE + steps_crop % TILE
        usable = (position < full_length[0]).astype(jnp.float32)
        full_map = pair_maps[template_idx].reshape(NTILES, TILE, FULL, CH)[crop_ids]
        full_map = full_map.reshape(CROP, NTILES, TILE, CH)[:, crop_ids]
        current = full_map.reshape(CROP, CROP, CH)
        for layer_idx in range(NLAYER):
            current = outgoing_layer(current, usable, proj_weight[layer_idx], out_weight[layer_idx])
        total = total + channel_norm(current.astype(jnp.float32), -1)
    mean_pair = total / TEMPLATES
    hidden = jnp.maximum(mean_pair, 0.0).astype(jnp.bfloat16)
    result = jnp.dot(hidden.reshape(-1, CH), final_weight, preferred_element_type=jnp.float32).reshape(CROP, CROP, CZ)
    return jnp.transpose(result, (2, 1, 0)).astype(jnp.bfloat16)
```

```python
import jax
import jax.numpy as jnp
from jax import lax
from jax.experimental import pallas as pl
from jax.experimental.pallas import tpu as pltpu
from jax.sharding import PartitionSpec as P

CH = 64
CZ = 128
CROP = 1024
TILE = 128
NLAYER = 2
FULL = 2048
ROWS = 8
EPSILON = 1e-05
BF = jnp.bfloat16
F32 = jnp.float32

PLANE = [[s * 8 + z for s in range(16)] for z in range(8)]
SAME_X0 = [
    [(x1 * 2 + x0) * 32 + y * 8 + z for x1 in range(2) for y in range(4) for z in range(8)]
    for x0 in range(2)
]
BY_Z = [[s * 8 + z for z in range(8) for s in range(16)]]
X0_PAIRS = [(r, r ^ 32) for r in range(128)]
CORES = [(0, 1), (1, 0)]
VMEM_LIMIT = 56 * 1024 * 1024


def iota(shape, dim):
    return lax.broadcasted_iota(jnp.int32, shape, dim)


def onehot(mask):
    return jnp.where(mask, 1.0, 0.0).astype(BF)


def dot(a, b):
    return jnp.dot(a, b, preferred_element_type=F32)


def dot_nt(a, b):
    return lax.dot_general(a, b, (((1,), (1,)), ((), ())), preferred_element_type=F32)


def dot_tn(a, b):
    return lax.dot_general(a, b, (((0,), (0,)), ((), ())), preferred_element_type=F32)


def lane_token(lane):
    return (
        (lane % 8) * 128
        + ((lane // 8) % 8) * 16
        + ((lane // 256) % 2) * 8
        + (lane // 512) * 4
        + ((lane // 64) % 4)
    )


def weights_kernel(proj_ref, out_ref, final_ref, wp_ref, wo_ref, wf_ref, prow_ref, q_ref, pj_ref, sel_ref):
    core = lax.axis_index("tmpl")
    spread = onehot(iota((CH, 512), 0) == iota((CH, 512), 1) // 8)
    repeat = onehot(iota((512, CH), 0) // 8 == iota((512, CH), 1))
    diag = iota((512, 512), 0) % 8 == iota((512, 512), 1) % 8
    for layer in range(NLAYER):
        for group in range(5):
            w = proj_ref[layer, :, group * CH : (group + 1) * CH]
            wide = dot_tn(w, spread).astype(BF)
            big = dot(repeat, wide)
            wp_ref[layer, group * 512 : (group + 1) * 512, :] = jnp.where(diag, big, 0.0).astype(BF)
        wide = dot_tn(out_ref[layer], spread).astype(BF)
        wo_ref[layer] = jnp.where(diag, dot(repeat, wide), 0.0).astype(BF)
    down = onehot(iota((512, CZ), 0) % CZ == iota((512, CZ), 1))
    across = onehot(iota((CH, 256), 0) == iota((CH, 256), 1) % CH)
    tall = dot_nt(down, final_ref[...]).astype(BF)
    block = iota((512, 256), 0) // CZ == iota((512, 256), 1) // CH
    wf_ref[...] = jnp.where(block, dot(tall, across), 0.0).astype(BF)
    r0, c0 = iota((512, 512), 0), iota((512, 512), 1)
    prow_ref[...] = onehot((r0 // 8 == c0 % CH) & (r0 % 8 == c0 // CH))
    half = (r0 // 256) ^ core
    sel_ref[...] = onehot((r0 % CH == c0 // 8) & (half * 4 + (r0 // CH) % 4 == c0 % 8))
    r1, c1 = iota((CROP, CROP), 0), iota((CROP, CROP), 1)
    token = lane_token(c1)
    q_ref[...] = onehot(r1 == token)
    dest = r1 // 8
    pj_ref[...] = onehot(((dest % 16) * 8 + dest // 16) * 8 + r1 % 8 == token)


def make_weights(proj_weight, out_weight, final_weight):
    shapes = [
        (NLAYER, 2560, 512), (NLAYER, 512, 512), (512, 256), (512, 512),
        (CROP, CROP), (CROP, CROP), (512, 512),
    ]
    return pl.pallas_call(
        weights_kernel,
        out_shape=[jax.ShapeDtypeStruct(shape, BF) for shape in shapes],
        compiler_params=pltpu.CompilerParams(vmem_limit_bytes=VMEM_LIMIT),
        cost_estimate=pl.CostEstimate(flops=2 * 10**9, bytes_accessed=12 * 2**20, transcendentals=0),
        name="weights",
    )(proj_weight, out_weight, final_weight)


def crop_kernel(crop_ref, x_ref, o_ref):
    del crop_ref
    o_ref[...] = x_ref[...]


def crop_columns(crop_tiles, pair):
    return pl.pallas_call(
        crop_kernel,
        grid_spec=pltpu.PrefetchScalarGridSpec(
            num_scalar_prefetch=1,
            grid=(8,),
            in_specs=[pl.BlockSpec((16, CH, TILE), lambda a, crop: (0, 0, crop[0, a]))],
            out_specs=pl.BlockSpec((16, CH, TILE), lambda a, crop: (0, 0, a)),
        ),
        out_shape=jax.ShapeDtypeStruct((16, CH, CROP), BF),
        name="crop",
    )(crop_tiles, pair)


def norm_channels(values):
    rows, lanes = values.shape
    cube = values.reshape(CH, ROWS, lanes)
    center = cube - (jnp.sum(cube, axis=0, keepdims=True) * (1.0 / CH))
    spread = jnp.sum(center * center, axis=0, keepdims=True) * (1.0 / CH)
    return (center * lax.rsqrt(spread + EPSILON)).reshape(rows, lanes)


def sigmoid(values):
    return 0.5 * jnp.tanh(0.5 * values) + 0.5


def pair_mask(crop_ref, length_ref, lanes, start):
    chip = lax.axis_index("row")
    inside = (chip % 8) * 16 + chip // 8
    length = length_ref[0]
    lane = iota((ROWS, lanes), 1) + start
    row = iota((ROWS, lanes), 0)
    token = lane_token(lane)
    col_pos = jnp.zeros((ROWS, lanes), jnp.int32)
    row_pos = jnp.zeros((ROWS, lanes), jnp.int32)
    for a in range(8):
        base = crop_ref[0, a] * TILE
        col_pos = jnp.where(lane % 8 == a, base, col_pos)
        row_pos = jnp.where(row == a, base, row_pos)
    col_pos = col_pos + token % TILE
    row_pos = row_pos + inside
    return jnp.where((col_pos < length) & (row_pos < length), 1.0, 0.0)


def project(current, wp, mask, left_ref, right_ref, gate_ref):
    lanes = current.shape[1]
    normed = norm_channels(current).astype(BF)
    wide = jnp.broadcast_to(mask[None], (CH, ROWS, lanes)).reshape(512, lanes)
    gate_a = dot(wp[0:512], normed)
    value_a = dot(wp[512:1024], normed)
    left_ref[...] = (sigmoid(gate_a) * value_a * wide).astype(BF)
    gate_b = dot(wp[1024:1536], normed)
    value_b = dot(wp[1536:2048], normed)
    right_ref[...] = (sigmoid(gate_b) * value_b * wide).astype(BF)
    gate_ref[...] = sigmoid(dot(wp[2048:2560], normed))


BLOCK = 256
STEPS = CROP // BLOCK


def first_kernel(crop_ref, length_ref, got_ref, prow_ref, q_ref, wp_ref, cur_ref, left_ref, right_ref, gate_ref, rows_ref):
    step = pl.program_id(0)

    @pl.when(step == 0)
    def _():
        parts = jnp.concatenate([got_ref[crop_ref[0, a]] for a in range(8)], axis=0)
        rows_ref[...] = dot(prow_ref[...], parts).astype(BF)

    current = dot(rows_ref[...], q_ref[...])
    cur_ref[...] = current.astype(BF)
    mask = pair_mask(crop_ref, length_ref, BLOCK, step * BLOCK)
    project(current, wp_ref[0], mask, left_ref, right_ref, gate_ref)


def full(shape):
    return pl.BlockSpec(shape, lambda step, crop, length: (0,) * len(shape), pipeline_mode=pl.Buffered(1))


def lanes_of(rows):
    return pl.BlockSpec((rows, BLOCK), lambda step, crop, length: (0, step))


def layer_weight(rows, layer):
    return pl.BlockSpec((1, rows, 512), lambda step, crop, length: (layer, 0, 0), pipeline_mode=pl.Buffered(1))


STATE = [
    jax.ShapeDtypeStruct((512, CROP), BF), jax.ShapeDtypeStruct((512, CROP), BF),
    jax.ShapeDtypeStruct((512, CROP), BF), jax.ShapeDtypeStruct((512, CROP), F32),
]


def first_projection(crop_tiles, full_length, got, prow, q, wp):
    return pl.pallas_call(
        first_kernel,
        grid_spec=pltpu.PrefetchScalarGridSpec(
            num_scalar_prefetch=2,
            grid=(STEPS,),
            in_specs=[full((16, CH, CROP)), full((512, 512)), lanes_of(CROP), layer_weight(2560, 0)],
            out_specs=[lanes_of(512)] * 4,
            scratch_shapes=[pltpu.VMEM((512, CROP), BF)],
        ),
        out_shape=STATE,
        compiler_params=pltpu.CompilerParams(vmem_limit_bytes=VMEM_LIMIT),
        name="first",
    )(crop_tiles, full_length, got, prow, q, wp)


def update(back_ref, cur_ref, gate_ref, wo):
    normed = norm_channels(back_ref[...].astype(F32)).astype(BF)
    change = dot(wo, normed)
    return (cur_ref[...].astype(F32) + gate_ref[...] * change).astype(BF)


def middle_kernel(crop_ref, length_ref, back_ref, cur_ref, gate_ref, wo_ref, wp_ref, next_ref, left_ref, right_ref, gate_out_ref):
    step = pl.program_id(0)
    current = update(back_ref, cur_ref, gate_ref, wo_ref[0])
    next_ref[...] = current
    mask = pair_mask(crop_ref, length_ref, BLOCK, step * BLOCK)
    project(current.astype(F32), wp_ref[0], mask, left_ref, right_ref, gate_out_ref)


def middle_layer(crop_tiles, full_length, back, current, gate, wo, wp, layer):
    return pl.pallas_call(
        middle_kernel,
        grid_spec=pltpu.PrefetchScalarGridSpec(
            num_scalar_prefetch=2,
            grid=(STEPS,),
            in_specs=[lanes_of(512)] * 3 + [layer_weight(512, layer), layer_weight(2560, layer + 1)],
            out_specs=[lanes_of(512)] * 4,
        ),
        out_shape=STATE,
        compiler_params=pltpu.CompilerParams(vmem_limit_bytes=VMEM_LIMIT),
        name="middle",
    )(crop_tiles, full_length, back, current, gate, wo, wp)


def last_kernel(back_ref, cur_ref, gate_ref, wo_ref, sel_ref, pj_ref, mine_ref, other_ref, total_ref):
    step = pl.program_id(0)
    current = update(back_ref, cur_ref, gate_ref, wo_ref[0])
    normed = norm_channels(current.astype(F32)).astype(BF)
    chosen = dot(sel_ref[...], normed).astype(BF)
    part = dot_nt(pj_ref[...], chosen)

    @pl.when(step == 0)
    def _():
        total_ref[...] = part

    @pl.when(step > 0)
    def _():
        total_ref[...] += part

    @pl.when(step == STEPS - 1)
    def _():
        mine_ref[...] = total_ref[:, :256].astype(BF)
        other_ref[...] = total_ref[:, 256:].astype(BF)


def last_layer(back, current, gate, wo, sel, pj, layer):
    lanes = pl.BlockSpec((512, BLOCK), lambda step: (0, step))
    half = pl.BlockSpec((CROP, 256), lambda step: (0, 0))
    return pl.pallas_call(
        last_kernel,
        grid=(STEPS,),
        in_specs=[lanes] * 3
        + [
            pl.BlockSpec((1, 512, 512), lambda step: (layer, 0, 0)),
            pl.BlockSpec((512, 512), lambda step: (0, 0)),
            pl.BlockSpec((CROP, BLOCK), lambda step: (0, step)),
        ],
        out_specs=[half, half],
        out_shape=[jax.ShapeDtypeStruct((CROP, 256), BF)] * 2,
        scratch_shapes=[pltpu.VMEM((CROP, 512), F32)],
        compiler_params=pltpu.CompilerParams(vmem_limit_bytes=VMEM_LIMIT),
        name="last",
    )(back, current, gate, wo, sel, pj)


def products_kernel(left_ref, own_ref, peer_ref, out_ref):
    x0 = (lax.axis_index("row") // 32) % 2
    left = left_ref[...]
    own = pl.multiple_of(x0 * 512, 512)
    peer = pl.multiple_of(512 - x0 * 512, 512)
    out_ref[:, pl.ds(own, 512)] = dot_nt(left, own_ref[...]).astype(BF)
    out_ref[:, pl.ds(peer, 512)] = dot_nt(left, peer_ref[...]).astype(BF)


def triangle_products(left, own, peer):
    return pl.pallas_call(
        products_kernel,
        out_shape=jax.ShapeDtypeStruct((512, CROP), BF),
        compiler_params=pltpu.CompilerParams(vmem_limit_bytes=VMEM_LIMIT),
        name="products",
    )(left, own, peer)


def hidden_kernel(mine_ref, peer_ref, out_ref):
    total = mine_ref[...].astype(F32) + peer_ref[...].astype(F32)
    out_ref[...] = jnp.maximum(total * 0.5, 0.0).astype(BF)


def hidden_features(mine, peer):
    return pl.pallas_call(
        hidden_kernel, out_shape=jax.ShapeDtypeStruct((CROP, 256), BF), name="hidden"
    )(mine, peer)


def final_kernel(mine_ref, peer_ref, wf_ref, out_ref, tall0_ref, tall1_ref, wide_ref):
    core = lax.axis_index("tmpl")
    wf = wf_ref[...]
    for source, ref in enumerate((mine_ref, peer_ref)):
        half = core if source == 0 else 1 - core
        tall0_ref[...] = ref[:, :128].astype(F32)
        tall1_ref[...] = ref[:, 128:].astype(F32)
        for j in range(8):
            rows = jnp.concatenate(
                [tall0_ref[pl.ds(j, 128, stride=8), :], tall1_ref[pl.ds(j, 128, stride=8), :]], axis=1
            ).astype(BF)
            result = dot_nt(wf, rows)
            for a in range(4):
                wide_ref[half * 4 + a, pl.ds(j, CZ, stride=8), :] = result[a * CZ : (a + 1) * CZ]
    for a in range(8):
        out_ref[:, a * TILE : (a + 1) * TILE] = wide_ref[a].astype(BF)


def final_projection(mine, peer, wf):
    return pl.pallas_call(
        final_kernel,
        out_shape=jax.ShapeDtypeStruct((CZ * 8, CROP), BF),
        scratch_shapes=[
            pltpu.VMEM((CROP, 128), F32), pltpu.VMEM((CROP, 128), F32), pltpu.VMEM((8, CZ * 8, TILE), F32)
        ],
        compiler_params=pltpu.CompilerParams(vmem_limit_bytes=VMEM_LIMIT),
        name="final",
    )(mine, peer, wf)


def exchange(values, groups, count):
    cube = values.reshape(count, -1, values.shape[-1])
    moved = lax.all_to_all(cube, "row", 0, 0, axis_index_groups=groups, tiled=True)
    return moved.reshape(values.shape)


def on_device(pair_maps, crop_tiles, full_length, proj_weight, out_weight, final_weight):
    wp, wo, wf, prow, q, pj, sel = make_weights(proj_weight, out_weight, final_weight)
    pair = jnp.transpose(pair_maps[0], (0, 2, 1))
    cropped = crop_columns(crop_tiles, pair)
    got = lax.all_to_all(cropped, "row", 0, 0, axis_index_groups=PLANE, tiled=True)
    current, left, right, gate = first_projection(crop_tiles, full_length, got, prow, q, wp)
    for layer in range(NLAYER):
        right_own = exchange(right, SAME_X0, CH)
        left_own = exchange(left, SAME_X0, CH)
        right_peer = lax.ppermute(right_own, "row", X0_PAIRS)
        products = triangle_products(left_own, right_own, right_peer)
        back = exchange(products, SAME_X0, CH)
        if layer + 1 < NLAYER:
            current, left, right, gate = middle_layer(
                crop_tiles, full_length, back, current, gate, wo, wp, layer
            )
    mine, other = last_layer(back, current, gate, wo, sel, pj, NLAYER - 1)
    hidden = hidden_features(mine, lax.ppermute(other, "tmpl", CORES))
    moved = exchange(hidden, BY_Z, 128)
    result = final_projection(moved, lax.ppermute(moved, "tmpl", CORES), wf)
    return result.reshape(CZ, 8, CROP)


def solution(mesh):
    placed = (P("tmpl", "row", None, None), P("tmpl", None), P(), P(), P(), P())
    return jax.shard_map(
        on_device, mesh=mesh, in_specs=placed, out_specs=P(None, "row", None), check_vma=False
    )
```

```python
import functools

import jax
import jax.numpy as jnp
from jax import lax
from jax.experimental import pallas as pl
from jax.experimental.pallas import tpu as pltpu
from jax.sharding import PartitionSpec as P

CH = 64
CZ = 128
CROP = 1024
TILE = 128
NLAYER = 2
FULL = 2048
ROWS = 8
EPSILON = 1e-05
BF = jnp.bfloat16
F32 = jnp.float32

PLANE = [[s * 8 + z for s in range(16)] for z in range(8)]
SAME_X0 = [
    [(x1 * 2 + x0) * 32 + y * 8 + z for x1 in range(2) for y in range(4) for z in range(8)]
    for x0 in range(2)
]
BY_Z = [[s * 8 + z for z in range(8) for s in range(16)]]
X0_PAIRS = [(r, r ^ 32) for r in range(128)]
CORES = [(0, 1), (1, 0)]
VMEM_LIMIT = 56 * 1024 * 1024


def iota(shape, dim):
    return lax.broadcasted_iota(jnp.int32, shape, dim)


def onehot(mask):
    return jnp.where(mask, 1.0, 0.0).astype(BF)


def dot(a, b):
    return jnp.dot(a, b, preferred_element_type=F32)


def dot_nt(a, b):
    return lax.dot_general(a, b, (((1,), (1,)), ((), ())), preferred_element_type=F32)


def dot_tn(a, b):
    return lax.dot_general(a, b, (((0,), (0,)), ((), ())), preferred_element_type=F32)


def lane_token(lane):
    x0 = (lax.axis_index("row") // 32) % 2
    return (
        (lane % 8) * 128
        + ((lane // 8) % 8) * 16
        + ((lane // 256) % 2) * 8
        + ((lane // 512) ^ x0) * 4
        + ((lane // 64) % 4)
    )


def weights_kernel(proj_ref, out_ref, final_ref, wp_ref, wo_ref, wf_ref, prow_ref, q_ref, pj_ref, sel_ref):
    core = lax.axis_index("tmpl")
    spread = onehot(iota((CH, 512), 0) == iota((CH, 512), 1) // 8)
    repeat = onehot(iota((512, CH), 0) // 8 == iota((512, CH), 1))
    diag = iota((512, 512), 0) % 8 == iota((512, 512), 1) % 8
    for layer in range(NLAYER):
        for group in range(5):
            w = proj_ref[layer, :, group * CH : (group + 1) * CH]
            wide = dot_tn(w, spread).astype(BF)
            big = dot(repeat, wide)
            wp_ref[layer, group * 512 : (group + 1) * 512, :] = jnp.where(diag, big, 0.0).astype(BF)
        wide = dot_tn(out_ref[layer], spread).astype(BF)
        wo_ref[layer] = jnp.where(diag, dot(repeat, wide), 0.0).astype(BF)
    down = onehot(iota((512, CZ), 0) % CZ == iota((512, CZ), 1))
    across = onehot(iota((CH, 256), 0) == iota((CH, 256), 1) % CH)
    tall = dot_nt(down, final_ref[...]).astype(BF)
    block = iota((512, 256), 0) // CZ == iota((512, 256), 1) // CH
    wf_ref[...] = jnp.where(block, dot(tall, across), 0.0).astype(BF)
    r0, c0 = iota((512, 512), 0), iota((512, 512), 1)
    prow_ref[...] = onehot((r0 // 8 == c0 % CH) & (r0 % 8 == c0 // CH))
    half = (r0 // 256) ^ core
    sel_ref[...] = onehot((r0 % CH == c0 // 8) & (half * 4 + (r0 // CH) % 4 == c0 % 8))
    r1, c1 = iota((CROP, CROP), 0), iota((CROP, CROP), 1)
    token = lane_token(c1)
    q_ref[...] = onehot(r1 == token)
    dest = r1 // 8
    pj_ref[...] = onehot(((dest % 16) * 8 + dest // 16) * 8 + r1 % 8 == token)


def make_weights(proj_weight, out_weight, final_weight):
    shapes = [
        (NLAYER, 2560, 512), (NLAYER, 512, 512), (512, 256), (512, 512),
        (CROP, CROP), (CROP, CROP), (512, 512),
    ]
    return pl.pallas_call(
        weights_kernel,
        out_shape=[jax.ShapeDtypeStruct(shape, BF) for shape in shapes],
        compiler_params=pltpu.CompilerParams(vmem_limit_bytes=VMEM_LIMIT),
        cost_estimate=pl.CostEstimate(flops=2 * 10**9, bytes_accessed=12 * 2**20, transcendentals=0),
        name="weights",
    )(proj_weight, out_weight, final_weight)


def crop_kernel(crop_ref, x_ref, o_ref):
    for a in range(8):
        start = pl.multiple_of(crop_ref[0, a] * TILE, TILE)
        o_ref[:, :, a * TILE : (a + 1) * TILE] = x_ref[:, :, pl.ds(start, TILE)]


def crop_columns(crop_tiles, pair):
    return pl.pallas_call(
        crop_kernel,
        grid_spec=pltpu.PrefetchScalarGridSpec(
            num_scalar_prefetch=1,
            grid=(8,),
            in_specs=[pl.BlockSpec((2, CH, FULL), lambda m, crop: (m, 0, 0))],
            out_specs=pl.BlockSpec((2, CH, CROP), lambda m, crop: (m, 0, 0)),
        ),
        out_shape=jax.ShapeDtypeStruct((16, CH, CROP), BF),
        name="crop",
    )(crop_tiles, pair)


def norm_channels(values):
    rows, lanes = values.shape
    cube = values.reshape(CH, ROWS, lanes)
    center = cube - (jnp.sum(cube, axis=0, keepdims=True) * (1.0 / CH))
    spread = jnp.sum(center * center, axis=0, keepdims=True) * (1.0 / CH)
    return (center * lax.rsqrt(spread + EPSILON)).reshape(rows, lanes)


def sigmoid(values):
    return 0.5 * jnp.tanh(0.5 * values) + 0.5


def pair_mask(crop_ref, length_ref, lanes, start):
    chip = lax.axis_index("row")
    inside = (chip % 8) * 16 + chip // 8
    length = length_ref[0]
    lane = iota((ROWS, lanes), 1) + start
    row = iota((ROWS, lanes), 0)
    token = lane_token(lane)
    col_pos = jnp.zeros((ROWS, lanes), jnp.int32)
    row_pos = jnp.zeros((ROWS, lanes), jnp.int32)
    for a in range(8):
        base = crop_ref[0, a] * TILE
        col_pos = jnp.where(lane % 8 == a, base, col_pos)
        row_pos = jnp.where(row == a, base, row_pos)
    col_pos = col_pos + token % TILE
    row_pos = row_pos + inside
    return jnp.where((col_pos < length) & (row_pos < length), 1.0, 0.0)


def project(current, wp, mask, both_ref, gate_ref):
    lanes = current.shape[1]
    normed = norm_channels(current).astype(BF)
    wide = jnp.broadcast_to(mask[None], (CH, ROWS, lanes)).reshape(512, lanes)
    gate_a = dot(wp[0:512], normed)
    value_a = dot(wp[512:1024], normed)
    both_ref[:, :lanes] = (sigmoid(gate_a) * value_a * wide).astype(BF)
    gate_b = dot(wp[1024:1536], normed)
    value_b = dot(wp[1536:2048], normed)
    both_ref[:, lanes:] = (sigmoid(gate_b) * value_b * wide).astype(BF)
    gate_ref[...] = sigmoid(dot(wp[2048:2560], normed))


BLOCK = 256
STEPS = CROP // BLOCK
HALF_STEPS = STEPS // 2
BOTH = jax.ShapeDtypeStruct((512, 2 * CROP), BF)


def first_kernel(crop_ref, length_ref, got_ref, prow_ref, q_ref, wp_ref, cur_ref, both_ref, gate_ref, rows_ref):
    step = pl.program_id(0)

    @pl.when(step == 0)
    def _():
        parts = jnp.concatenate([got_ref[crop_ref[0, a]] for a in range(8)], axis=0)
        rows_ref[...] = dot(prow_ref[...], parts).astype(BF)

    current = dot(rows_ref[...], q_ref[...])
    cur_ref[...] = current.astype(BF)
    mask = pair_mask(crop_ref, length_ref, BLOCK, step * BLOCK)
    project(current, wp_ref[0], mask, both_ref, gate_ref)


def full(shape):
    return pl.BlockSpec(shape, lambda step, *_: (0,) * len(shape), pipeline_mode=pl.Buffered(1))


def lanes_of(rows, lanes=BLOCK, offset=0):
    return pl.BlockSpec((rows, lanes), lambda step, *_: (0, step + offset))


def layer_weight(rows, layer):
    return pl.BlockSpec((1, rows, 512), lambda step, *_: (layer, 0, 0), pipeline_mode=pl.Buffered(1))


def first_projection(crop_tiles, full_length, got, prow, q, wp):
    return pl.pallas_call(
        first_kernel,
        grid_spec=pltpu.PrefetchScalarGridSpec(
            num_scalar_prefetch=2,
            grid=(STEPS,),
            in_specs=[full((16, CH, CROP)), full((512, 512)), lanes_of(CROP), layer_weight(2560, 0)],
            out_specs=[lanes_of(512), lanes_of(512, 2 * BLOCK), lanes_of(512)],
            scratch_shapes=[pltpu.VMEM((512, CROP), BF)],
        ),
        out_shape=[jax.ShapeDtypeStruct((512, CROP), BF), BOTH, jax.ShapeDtypeStruct((512, CROP), F32)],
        compiler_params=pltpu.CompilerParams(vmem_limit_bytes=VMEM_LIMIT),
        name="first",
    )(crop_tiles, full_length, got, prow, q, wp)


def update(back_ref, cur_ref, gate_ref, wo):
    normed = norm_channels(back_ref[...].astype(F32)).astype(BF)
    change = dot(wo, normed)
    return (cur_ref[...].astype(F32) + gate_ref[...] * change).astype(BF)


def middle_kernel(half, *refs):
    crop_ref, length_ref, back_ref, cur_ref, gate_ref, wo_ref, wp_ref = refs[:7]
    next_ref, both_ref, gate_out_ref = refs[-3:]
    current = update(back_ref, cur_ref, gate_ref, wo_ref[0])
    next_ref[...] = current
    start = half * 512 + pl.program_id(0) * BLOCK
    mask = pair_mask(crop_ref, length_ref, BLOCK, start)
    project(current.astype(F32), wp_ref[0], mask, both_ref, gate_out_ref)


def middle_half(half, crop_tiles, full_length, back, current, gate, wo, wp, layer, both):
    offset = half * HALF_STEPS
    aliased = [] if both is None else [both]
    return pl.pallas_call(
        functools.partial(middle_kernel, half),
        grid_spec=pltpu.PrefetchScalarGridSpec(
            num_scalar_prefetch=2,
            grid=(HALF_STEPS,),
            in_specs=[
                lanes_of(512), lanes_of(512, offset=offset), lanes_of(512, offset=offset),
                layer_weight(512, layer), layer_weight(2560, layer + 1),
            ]
            + [pl.BlockSpec(memory_space=pl.ANY)] * len(aliased),
            out_specs=[lanes_of(512), lanes_of(512, 2 * BLOCK, offset), lanes_of(512)],
        ),
        out_shape=[jax.ShapeDtypeStruct((512, 512), BF), BOTH, jax.ShapeDtypeStruct((512, 512), F32)],
        input_output_aliases={7: 1} if aliased else {},
        compiler_params=pltpu.CompilerParams(vmem_limit_bytes=VMEM_LIMIT),
        name="middle" + str(half),
    )(crop_tiles, full_length, back, current, gate, wo, wp, *aliased)


def chosen_rows(back_ref, cur_ref, gate_ref, wo_ref, sel_ref):
    current = update(back_ref, cur_ref, gate_ref, wo_ref[0])
    normed = norm_channels(current.astype(F32)).astype(BF)
    return dot(sel_ref[...], normed).astype(BF)


def last_own_kernel(back_ref, cur_ref, gate_ref, wo_ref, sel_ref, chosen_ref):
    chosen_ref[...] = chosen_rows(back_ref, cur_ref, gate_ref, wo_ref, sel_ref)


def last_peer_kernel(back_ref, cur_ref, gate_ref, wo_ref, sel_ref, own_ref, pj_ref, mine_ref, other_ref, part_ref):
    step = pl.program_id(0)
    part_ref[step] = chosen_rows(back_ref, cur_ref, gate_ref, wo_ref, sel_ref)

    @pl.when(step == HALF_STEPS - 1)
    def _():
        chosen = jnp.concatenate([own_ref[...]] + [part_ref[k] for k in range(HALF_STEPS)], axis=1)
        mine_ref[...] = dot_nt(pj_ref[...], chosen[:256]).astype(BF)
        other_ref[...] = dot_nt(pj_ref[...], chosen[256:]).astype(BF)


def last_own(back, current, gate, wo, sel, layer):
    return pl.pallas_call(
        last_own_kernel,
        grid=(HALF_STEPS,),
        in_specs=[lanes_of(512)] * 3 + [layer_weight(512, layer), full((512, 512))],
        out_specs=lanes_of(512),
        out_shape=jax.ShapeDtypeStruct((512, 512), BF),
        compiler_params=pltpu.CompilerParams(vmem_limit_bytes=VMEM_LIMIT),
        name="last_own",
    )(back, current, gate, wo, sel)


def last_peer(back, current, gate, wo, sel, own, pj, layer):
    return pl.pallas_call(
        last_peer_kernel,
        grid=(HALF_STEPS,),
        in_specs=[lanes_of(512)] * 3
        + [layer_weight(512, layer), full((512, 512)), full((512, 512)), full((CROP, CROP))],
        out_specs=[full((CROP, 256))] * 2,
        out_shape=[jax.ShapeDtypeStruct((CROP, 256), BF)] * 2,
        scratch_shapes=[pltpu.VMEM((HALF_STEPS, 512, BLOCK), BF)],
        compiler_params=pltpu.CompilerParams(vmem_limit_bytes=VMEM_LIMIT),
        name="last_peer",
    )(back, current, gate, wo, sel, own, pj)


def lane_blocks(both_ref, which, order):
    starts = [(2 * block + which) * BLOCK for block in order]
    return jnp.concatenate([both_ref[:, start : start + BLOCK] for start in starts], axis=1)


def own_products_kernel(both_ref, out_ref, right_ref):
    right = lane_blocks(both_ref, 1, range(STEPS))
    right_ref[...] = right
    out_ref[...] = dot_nt(lane_blocks(both_ref, 0, range(STEPS)), right).astype(BF)


def own_products(both):
    return pl.pallas_call(
        own_products_kernel,
        out_shape=[jax.ShapeDtypeStruct((512, 512), BF), jax.ShapeDtypeStruct((512, CROP), BF)],
        compiler_params=pltpu.CompilerParams(vmem_limit_bytes=VMEM_LIMIT),
        cost_estimate=pl.CostEstimate(flops=2**29, bytes_accessed=4 * 2**20, transcendentals=0),
        name="own_products",
    )(both)


def peer_products_kernel(both_ref, right_ref, out_ref):
    left = lane_blocks(both_ref, 0, [2, 3, 0, 1])
    out_ref[...] = dot_nt(left, right_ref[...]).astype(BF)


def peer_products(both, right):
    return pl.pallas_call(
        peer_products_kernel,
        out_shape=jax.ShapeDtypeStruct((512, 512), BF),
        compiler_params=pltpu.CompilerParams(vmem_limit_bytes=VMEM_LIMIT),
        cost_estimate=pl.CostEstimate(flops=2**29, bytes_accessed=4 * 2**20, transcendentals=0),
        name="peer_products",
    )(both, right)


def hidden_kernel(mine_ref, peer_ref, out_ref):
    total = mine_ref[...].astype(F32) + peer_ref[...].astype(F32)
    out_ref[...] = jnp.maximum(total * 0.5, 0.0).astype(BF)


def hidden_features(mine, peer):
    return pl.pallas_call(
        hidden_kernel, out_shape=jax.ShapeDtypeStruct((CROP, 256), BF), name="hidden"
    )(mine, peer)


def final_kernel(mine_ref, peer_ref, wf_ref, out_ref, tall0_ref, tall1_ref, wide_ref):
    core = lax.axis_index("tmpl")
    wf = wf_ref[...]
    for source, ref in enumerate((mine_ref, peer_ref)):
        half = core if source == 0 else 1 - core
        tall0_ref[...] = ref[:, :128].astype(F32)
        tall1_ref[...] = ref[:, 128:].astype(F32)
        for j in range(8):
            rows = jnp.concatenate(
                [tall0_ref[pl.ds(j, 128, stride=8), :], tall1_ref[pl.ds(j, 128, stride=8), :]], axis=1
            ).astype(BF)
            result = dot_nt(wf, rows)
            for a in range(4):
                wide_ref[half * 4 + a, pl.ds(j, CZ, stride=8), :] = result[a * CZ : (a + 1) * CZ]
    for a in range(8):
        out_ref[:, a * TILE : (a + 1) * TILE] = wide_ref[a].astype(BF)


def final_projection(mine, peer, wf):
    return pl.pallas_call(
        final_kernel,
        out_shape=jax.ShapeDtypeStruct((CZ * 8, CROP), BF),
        scratch_shapes=[
            pltpu.VMEM((CROP, 128), F32), pltpu.VMEM((CROP, 128), F32), pltpu.VMEM((8, CZ * 8, TILE), F32)
        ],
        compiler_params=pltpu.CompilerParams(vmem_limit_bytes=VMEM_LIMIT),
        name="final",
    )(mine, peer, wf)


def exchange(values, groups, count):
    cube = values.reshape(count, -1, values.shape[-1])
    moved = lax.all_to_all(cube, "row", 0, 0, axis_index_groups=groups, tiled=True)
    return moved.reshape(values.shape)


def on_device(pair_maps, crop_tiles, full_length, proj_weight, out_weight, final_weight):
    wp, wo, wf, prow, q, pj, sel = make_weights(proj_weight, out_weight, final_weight)
    pair = jnp.transpose(pair_maps[0], (0, 2, 1))
    cropped = crop_columns(crop_tiles, pair)
    got = lax.all_to_all(cropped, "row", 0, 0, axis_index_groups=PLANE, tiled=True)
    current, both, gate = first_projection(crop_tiles, full_length, got, prow, q, wp)
    currents, gates = (current, current), (gate, gate)
    for layer in range(NLAYER):
        gathered = exchange(both, SAME_X0, CH)
        products, right = own_products(gathered)
        back_own = exchange(products, SAME_X0, CH)
        right_peer = lax.ppermute(right, "row", X0_PAIRS)
        back_peer = exchange(peer_products(gathered, right_peer), SAME_X0, CH)
        if layer + 1 < NLAYER:
            shared = (wo, wp, layer)
            own, both, gate_own = middle_half(
                0, crop_tiles, full_length, back_own, currents[0], gates[0], *shared, None
            )
            peer, both, gate_peer = middle_half(
                1, crop_tiles, full_length, back_peer, currents[1], gates[1], *shared, both
            )
            currents, gates = (own, peer), (gate_own, gate_peer)
    chosen = last_own(back_own, currents[0], gates[0], wo, sel, NLAYER - 1)
    mine, other = last_peer(back_peer, currents[1], gates[1], wo, sel, chosen, pj, NLAYER - 1)
    hidden = hidden_features(mine, lax.ppermute(other, "tmpl", CORES))
    moved = exchange(hidden, BY_Z, 128)
    result = final_projection(moved, lax.ppermute(moved, "tmpl", CORES), wf)
    return result.reshape(CZ, 8, CROP)


def solution(mesh):
    placed = (P("tmpl", "row", None, None), P("tmpl", None), P(), P(), P(), P())
    return jax.shard_map(
        on_device, mesh=mesh, in_specs=placed, out_specs=P(None, "row", None), check_vma=False
    )
```

```python
import functools

import jax
import jax.numpy as jnp
from jax import lax
from jax.experimental import pallas as pl
from jax.experimental.pallas import tpu as pltpu
from jax.sharding import PartitionSpec as P

CH = 64
CZ = 128
CROP = 1024
TILE = 128
NLAYER = 2
FULL = 2048
ROWS = 8
EPSILON = 1e-05
BF = jnp.bfloat16
F32 = jnp.float32

PLANE = [[s * 8 + z for s in range(16)] for z in range(8)]
SAME_X0 = [
    [(x1 * 2 + x0) * 32 + y * 8 + z for x1 in range(2) for y in range(4) for z in range(8)]
    for x0 in range(2)
]
BY_Z = [[s * 8 + z for z in range(8) for s in range(16)]]
X0_PAIRS = [(r, r ^ 32) for r in range(128)]
CORES = [(0, 1), (1, 0)]
VMEM_LIMIT = 20 * 1024 * 1024


def iota(shape, dim):
    return lax.broadcasted_iota(jnp.int32, shape, dim)


def onehot(mask):
    return jnp.where(mask, 1.0, 0.0).astype(BF)


def dot(a, b):
    return jnp.dot(a, b, preferred_element_type=F32)


def dot_nt(a, b):
    return lax.dot_general(a, b, (((1,), (1,)), ((), ())), preferred_element_type=F32)


def dot_tn(a, b):
    return lax.dot_general(a, b, (((0,), (0,)), ((), ())), preferred_element_type=F32)


def lane_token(lane):
    x0 = (lax.axis_index("row") // 32) % 2
    return (
        (lane % 8) * 128
        + ((lane // 8) % 8) * 16
        + ((lane // 256) % 2) * 8
        + ((lane // 512) ^ x0) * 4
        + ((lane // 64) % 4)
    )


def weights_kernel(proj_ref, out_ref, final_ref, wp_ref, wo_ref, wf_ref, prow_ref, q_ref, pj_ref, sel_ref):
    core = lax.axis_index("tmpl")
    spread = onehot(iota((CH, 512), 0) == iota((CH, 512), 1) // 8)
    repeat = onehot(iota((512, CH), 0) // 8 == iota((512, CH), 1))
    diag = iota((512, 512), 0) % 8 == iota((512, 512), 1) % 8
    for layer in range(NLAYER):
        for group in range(5):
            w = proj_ref[layer, :, group * CH : (group + 1) * CH]
            wide = dot_tn(w, spread).astype(BF)
            big = dot(repeat, wide)
            wp_ref[layer, group * 512 : (group + 1) * 512, :] = jnp.where(diag, big, 0.0).astype(BF)
        wide = dot_tn(out_ref[layer], spread).astype(BF)
        wo_ref[layer] = jnp.where(diag, dot(repeat, wide), 0.0).astype(BF)
    down = onehot(iota((512, CZ), 0) % CZ == iota((512, CZ), 1))
    across = onehot(iota((CH, 256), 0) == iota((CH, 256), 1) % CH)
    tall = dot_nt(down, final_ref[...]).astype(BF)
    block = iota((512, 256), 0) // CZ == iota((512, 256), 1) // CH
    wf_ref[...] = jnp.where(block, dot(tall, across), 0.0).astype(BF)
    r0, c0 = iota((512, 512), 0), iota((512, 512), 1)
    prow_ref[...] = onehot((r0 // 8 == c0 % CH) & (r0 % 8 == c0 // CH))
    half = (r0 // 256) ^ core
    sel_ref[...] = onehot((r0 % CH == c0 // 8) & (half * 4 + (r0 // CH) % 4 == c0 % 8))
    r1, c1 = iota((CROP, CROP), 0), iota((CROP, CROP), 1)
    token = lane_token(c1)
    q_ref[...] = onehot(r1 == token)
    dest = r1 // 8
    pj_ref[...] = onehot(((dest % 16) * 8 + dest // 16) * 8 + r1 % 8 == token)


def make_weights(proj_weight, out_weight, final_weight):
    shapes = [
        (NLAYER, 2560, 512), (NLAYER, 512, 512), (512, 256), (512, 512),
        (CROP, CROP), (CROP, CROP), (512, 512),
    ]
    return pl.pallas_call(
        weights_kernel,
        out_shape=[jax.ShapeDtypeStruct(shape, BF) for shape in shapes],
        compiler_params=pltpu.CompilerParams(vmem_limit_bytes=48 * 1024 * 1024),
        cost_estimate=pl.CostEstimate(flops=2 * 10**9, bytes_accessed=12 * 2**20, transcendentals=0),
        name="weights",
    )(proj_weight, out_weight, final_weight)


def crop_kernel(crop_ref, x_ref, o_ref):
    for a in range(8):
        start = pl.multiple_of(crop_ref[0, a] * TILE, TILE)
        o_ref[:, :, a * TILE : (a + 1) * TILE] = x_ref[:, :, pl.ds(start, TILE)]


def crop_columns(crop_tiles, pair):
    return pl.pallas_call(
        crop_kernel,
        grid_spec=pltpu.PrefetchScalarGridSpec(
            num_scalar_prefetch=1,
            grid=(4,),
            in_specs=[pl.BlockSpec((4, CH, FULL), lambda m, crop: (m, 0, 0))],
            out_specs=pl.BlockSpec((4, CH, CROP), lambda m, crop: (m, 0, 0)),
        ),
        out_shape=jax.ShapeDtypeStruct((16, CH, CROP), BF),
        compiler_params=pltpu.CompilerParams(vmem_limit_bytes=VMEM_LIMIT),
        name="crop",
    )(crop_tiles, pair)


def norm_channels(values):
    rows, lanes = values.shape
    cube = values.reshape(CH, ROWS, lanes)
    center = cube - (jnp.sum(cube, axis=0, keepdims=True) * (1.0 / CH))
    spread = jnp.sum(center * center, axis=0, keepdims=True) * (1.0 / CH)
    return (center * lax.rsqrt(spread + EPSILON)).reshape(rows, lanes)


def sigmoid(values):
    return 0.5 * jnp.tanh(0.5 * values) + 0.5


def pair_mask(crop_ref, length_ref, lanes, start):
    chip = lax.axis_index("row")
    inside = (chip % 8) * 16 + chip // 8
    length = length_ref[0]
    lane = iota((ROWS, lanes), 1) + start
    row = iota((ROWS, lanes), 0)
    token = lane_token(lane)
    col_pos = jnp.zeros((ROWS, lanes), jnp.int32)
    row_pos = jnp.zeros((ROWS, lanes), jnp.int32)
    for a in range(8):
        base = crop_ref[0, a] * TILE
        col_pos = jnp.where(lane % 8 == a, base, col_pos)
        row_pos = jnp.where(row == a, base, row_pos)
    col_pos = col_pos + token % TILE
    row_pos = row_pos + inside
    return jnp.where((col_pos < length) & (row_pos < length), 1.0, 0.0)


def project(current, wp, mask, both_ref, gate_ref):
    lanes = current.shape[1]
    normed = norm_channels(current).astype(BF)
    wide = jnp.broadcast_to(mask[None], (CH, ROWS, lanes)).reshape(512, lanes)
    gate_a = dot(wp[0:512], normed)
    value_a = dot(wp[512:1024], normed)
    both_ref[:, :lanes] = (sigmoid(gate_a) * value_a * wide).astype(BF)
    gate_b = dot(wp[1024:1536], normed)
    value_b = dot(wp[1536:2048], normed)
    both_ref[:, lanes:] = (sigmoid(gate_b) * value_b * wide).astype(BF)
    gate_ref[...] = sigmoid(dot(wp[2048:2560], normed))


BLOCK = 256
STEPS = CROP // BLOCK
HALF_STEPS = STEPS // 2
BOTH = jax.ShapeDtypeStruct((512, 2 * CROP), BF)


def first_kernel(crop_ref, length_ref, got_ref, prow_ref, q_ref, wp_ref, cur_ref, both_ref, gate_ref, rows_ref):
    step = pl.program_id(0)

    @pl.when(step == 0)
    def _():
        parts = jnp.concatenate([got_ref[crop_ref[0, a]] for a in range(8)], axis=0)
        rows_ref[...] = dot(prow_ref[...], parts).astype(BF)

    current = dot(rows_ref[...], q_ref[...])
    cur_ref[...] = current.astype(BF)
    mask = pair_mask(crop_ref, length_ref, BLOCK, step * BLOCK)
    project(current, wp_ref[0], mask, both_ref, gate_ref)


def full(shape):
    return pl.BlockSpec(shape, lambda step, *_: (0,) * len(shape), pipeline_mode=pl.Buffered(1))


def lanes_of(rows, lanes=BLOCK, offset=0):
    return pl.BlockSpec((rows, lanes), lambda step, *_: (0, step + offset))


def layer_weight(rows, layer):
    return pl.BlockSpec((1, rows, 512), lambda step, *_: (layer, 0, 0), pipeline_mode=pl.Buffered(1))


def first_projection(crop_tiles, full_length, got, prow, q, wp):
    return pl.pallas_call(
        first_kernel,
        grid_spec=pltpu.PrefetchScalarGridSpec(
            num_scalar_prefetch=2,
            grid=(STEPS,),
            in_specs=[full((16, CH, CROP)), full((512, 512)), lanes_of(CROP), layer_weight(2560, 0)],
            out_specs=[lanes_of(512), lanes_of(512, 2 * BLOCK), lanes_of(512)],
            scratch_shapes=[pltpu.VMEM((512, CROP), BF)],
        ),
        out_shape=[jax.ShapeDtypeStruct((512, CROP), BF), BOTH, jax.ShapeDtypeStruct((512, CROP), F32)],
        compiler_params=pltpu.CompilerParams(vmem_limit_bytes=VMEM_LIMIT),
        name="first",
    )(crop_tiles, full_length, got, prow, q, wp)


def update(back_ref, cur_ref, gate_ref, wo):
    normed = norm_channels(back_ref[...].astype(F32)).astype(BF)
    change = dot(wo, normed)
    return (cur_ref[...].astype(F32) + gate_ref[...] * change).astype(BF)


def middle_kernel(half, *refs):
    crop_ref, length_ref, back_ref, cur_ref, gate_ref, wo_ref, wp_ref = refs[:7]
    next_ref, both_ref, gate_out_ref = refs[-3:]
    current = update(back_ref, cur_ref, gate_ref, wo_ref[0])
    next_ref[...] = current
    start = half * 512 + pl.program_id(0) * BLOCK
    mask = pair_mask(crop_ref, length_ref, BLOCK, start)
    project(current.astype(F32), wp_ref[0], mask, both_ref, gate_out_ref)


def middle_half(half, crop_tiles, full_length, back, current, gate, wo, wp, layer, both):
    offset = half * HALF_STEPS
    aliased = [] if both is None else [both]
    return pl.pallas_call(
        functools.partial(middle_kernel, half),
        grid_spec=pltpu.PrefetchScalarGridSpec(
            num_scalar_prefetch=2,
            grid=(HALF_STEPS,),
            in_specs=[
                lanes_of(512), lanes_of(512, offset=offset), lanes_of(512, offset=offset),
                layer_weight(512, layer), layer_weight(2560, layer + 1),
            ]
            + [pl.BlockSpec(memory_space=pl.ANY)] * len(aliased),
            out_specs=[lanes_of(512), lanes_of(512, 2 * BLOCK, offset), lanes_of(512)],
        ),
        out_shape=[jax.ShapeDtypeStruct((512, 512), BF), BOTH, jax.ShapeDtypeStruct((512, 512), F32)],
        input_output_aliases={7: 1} if aliased else {},
        compiler_params=pltpu.CompilerParams(vmem_limit_bytes=VMEM_LIMIT),
        name="middle" + str(half),
    )(crop_tiles, full_length, back, current, gate, wo, wp, *aliased)


def chosen_rows(back_ref, cur_ref, gate_ref, wo_ref, sel_ref):
    current = update(back_ref, cur_ref, gate_ref, wo_ref[0])
    normed = norm_channels(current.astype(F32)).astype(BF)
    return dot(sel_ref[...], normed).astype(BF)


def last_own_kernel(back_ref, cur_ref, gate_ref, wo_ref, sel_ref, chosen_ref):
    chosen_ref[...] = chosen_rows(back_ref, cur_ref, gate_ref, wo_ref, sel_ref)


def last_peer_kernel(back_ref, cur_ref, gate_ref, wo_ref, sel_ref, own_ref, pj_ref, mine_ref, other_ref, part_ref):
    step = pl.program_id(0)
    part_ref[step] = chosen_rows(back_ref, cur_ref, gate_ref, wo_ref, sel_ref)

    @pl.when(step == HALF_STEPS - 1)
    def _():
        chosen = jnp.concatenate([own_ref[...]] + [part_ref[k] for k in range(HALF_STEPS)], axis=1)
        mine_ref[...] = dot_nt(pj_ref[...], chosen[:256]).astype(BF)
        other_ref[...] = dot_nt(pj_ref[...], chosen[256:]).astype(BF)


def last_own(back, current, gate, wo, sel, layer):
    return pl.pallas_call(
        last_own_kernel,
        grid=(HALF_STEPS,),
        in_specs=[lanes_of(512)] * 3 + [layer_weight(512, layer), full((512, 512))],
        out_specs=lanes_of(512),
        out_shape=jax.ShapeDtypeStruct((512, 512), BF),
        compiler_params=pltpu.CompilerParams(vmem_limit_bytes=VMEM_LIMIT),
        name="last_own",
    )(back, current, gate, wo, sel)


def last_peer(back, current, gate, wo, sel, own, pj, layer):
    return pl.pallas_call(
        last_peer_kernel,
        grid=(HALF_STEPS,),
        in_specs=[lanes_of(512)] * 3
        + [layer_weight(512, layer), full((512, 512)), full((512, 512)), full((CROP, CROP))],
        out_specs=[full((CROP, 256))] * 2,
        out_shape=[jax.ShapeDtypeStruct((CROP, 256), BF)] * 2,
        scratch_shapes=[pltpu.VMEM((HALF_STEPS, 512, BLOCK), BF)],
        compiler_params=pltpu.CompilerParams(vmem_limit_bytes=VMEM_LIMIT),
        name="last_peer",
    )(back, current, gate, wo, sel, own, pj)


def lane_blocks(both_ref, which, order):
    starts = [(2 * block + which) * BLOCK for block in order]
    return jnp.concatenate([both_ref[:, start : start + BLOCK] for start in starts], axis=1)


def own_products_kernel(both_ref, out_ref, right_ref):
    right = lane_blocks(both_ref, 1, range(STEPS))
    right_ref[...] = right
    out_ref[...] = dot_nt(lane_blocks(both_ref, 0, range(STEPS)), right).astype(BF)


def own_products(both):
    return pl.pallas_call(
        own_products_kernel,
        out_shape=[jax.ShapeDtypeStruct((512, 512), BF), jax.ShapeDtypeStruct((512, CROP), BF)],
        compiler_params=pltpu.CompilerParams(vmem_limit_bytes=VMEM_LIMIT),
        cost_estimate=pl.CostEstimate(flops=2**29, bytes_accessed=4 * 2**20, transcendentals=0),
        name="own_products",
    )(both)


def peer_products_kernel(both_ref, right_ref, out_ref):
    left = lane_blocks(both_ref, 0, [2, 3, 0, 1])
    out_ref[...] = dot_nt(left, right_ref[...]).astype(BF)


def peer_products(both, right):
    return pl.pallas_call(
        peer_products_kernel,
        out_shape=jax.ShapeDtypeStruct((512, 512), BF),
        compiler_params=pltpu.CompilerParams(vmem_limit_bytes=VMEM_LIMIT),
        cost_estimate=pl.CostEstimate(flops=2**29, bytes_accessed=4 * 2**20, transcendentals=0),
        name="peer_products",
    )(both, right)


def hidden_kernel(mine_ref, peer_ref, out_ref):
    total = mine_ref[...].astype(F32) + peer_ref[...].astype(F32)
    out_ref[...] = jnp.maximum(total * 0.5, 0.0).astype(BF)


def hidden_features(mine, peer):
    return pl.pallas_call(
        hidden_kernel, out_shape=jax.ShapeDtypeStruct((CROP, 256), BF), name="hidden"
    )(mine, peer)


def final_kernel(mine_ref, peer_ref, wf_ref, out_ref, tall0_ref, tall1_ref, wide_ref):
    core = lax.axis_index("tmpl")
    wf = wf_ref[...]
    for source, ref in enumerate((mine_ref, peer_ref)):
        half = core if source == 0 else 1 - core
        tall0_ref[...] = ref[:, :128].astype(F32)
        tall1_ref[...] = ref[:, 128:].astype(F32)
        for j in range(8):
            rows = jnp.concatenate(
                [tall0_ref[pl.ds(j, 128, stride=8), :], tall1_ref[pl.ds(j, 128, stride=8), :]], axis=1
            ).astype(BF)
            result = dot_nt(wf, rows)
            for a in range(4):
                wide_ref[half * 4 + a, pl.ds(j, CZ, stride=8), :] = result[a * CZ : (a + 1) * CZ]
    for a in range(8):
        out_ref[:, a * TILE : (a + 1) * TILE] = wide_ref[a].astype(BF)


def final_projection(mine, peer, wf):
    return pl.pallas_call(
        final_kernel,
        out_shape=jax.ShapeDtypeStruct((CZ * 8, CROP), BF),
        scratch_shapes=[
            pltpu.VMEM((CROP, 128), F32), pltpu.VMEM((CROP, 128), F32), pltpu.VMEM((8, CZ * 8, TILE), F32)
        ],
        compiler_params=pltpu.CompilerParams(vmem_limit_bytes=VMEM_LIMIT),
        name="final",
    )(mine, peer, wf)


def exchange(values, groups, count):
    cube = values.reshape(count, -1, values.shape[-1])
    moved = lax.all_to_all(cube, "row", 0, 0, axis_index_groups=groups, tiled=True)
    return moved.reshape(values.shape)


def on_device(pair_maps, crop_tiles, full_length, proj_weight, out_weight, final_weight):
    wp, wo, wf, prow, q, pj, sel = make_weights(proj_weight, out_weight, final_weight)
    pair = jnp.transpose(pair_maps[0], (0, 2, 1))
    cropped = crop_columns(crop_tiles, pair)
    got = lax.all_to_all(cropped, "row", 0, 0, axis_index_groups=PLANE, tiled=True)
    current, both, gate = first_projection(crop_tiles, full_length, got, prow, q, wp)
    currents, gates = (current, current), (gate, gate)
    for layer in range(NLAYER):
        gathered = exchange(both, SAME_X0, CH)
        products, right = own_products(gathered)
        back_own = exchange(products, SAME_X0, CH)
        right_peer = lax.ppermute(right, "row", X0_PAIRS)
        back_peer = exchange(peer_products(gathered, right_peer), SAME_X0, CH)
        if layer + 1 < NLAYER:
            shared = (wo, wp, layer)
            own, both, gate_own = middle_half(
                0, crop_tiles, full_length, back_own, currents[0], gates[0], *shared, None
            )
            peer, both, gate_peer = middle_half(
                1, crop_tiles, full_length, back_peer, currents[1], gates[1], *shared, both
            )
            currents, gates = (own, peer), (gate_own, gate_peer)
    chosen = last_own(back_own, currents[0], gates[0], wo, sel, NLAYER - 1)
    mine, other = last_peer(back_peer, currents[1], gates[1], wo, sel, chosen, pj, NLAYER - 1)
    hidden = hidden_features(mine, lax.ppermute(other, "tmpl", CORES))
    moved = exchange(hidden, BY_Z, 128)
    result = final_projection(moved, lax.ppermute(moved, "tmpl", CORES), wf)
    return result.reshape(CZ, 8, CROP)


def solution(mesh):
    placed = (P("tmpl", "row", None, None), P("tmpl", None), P(), P(), P(), P())
    return jax.shard_map(
        on_device, mesh=mesh, in_specs=placed, out_specs=P(None, "row", None), check_vma=False
    )
```

```python
import functools

import jax
import jax.numpy as jnp
from jax import lax
from jax.experimental import pallas as pl
from jax.experimental.pallas import tpu as pltpu
from jax.sharding import PartitionSpec as P

CH = 64
CZ = 128
CROP = 1024
TILE = 128
NLAYER = 2
FULL = 2048
ROWS = 8
EPSILON = 1e-05
BF = jnp.bfloat16
F32 = jnp.float32

PLANE = [[s * 8 + z for s in range(16)] for z in range(8)]
SAME_X0 = [
    [(x1 * 2 + x0) * 32 + y * 8 + z for x1 in range(2) for y in range(4) for z in range(8)]
    for x0 in range(2)
]
BY_Z = [[s * 8 + z for z in range(8) for s in range(16)]]
X0_PAIRS = [(r, r ^ 32) for r in range(128)]
CORES = [(0, 1), (1, 0)]
VMEM_LIMIT = 20 * 1024 * 1024


def in_vmem(*arrays):
    return [pltpu.with_memory_space_constraint(array, pltpu.VMEM) for array in arrays]


def in_hbm(*arrays):
    return [pltpu.with_memory_space_constraint(array, pltpu.HBM) for array in arrays]


def iota(shape, dim):
    return lax.broadcasted_iota(jnp.int32, shape, dim)


def onehot(mask):
    return jnp.where(mask, 1.0, 0.0).astype(BF)


def dot(a, b):
    return jnp.dot(a, b, preferred_element_type=F32)


def dot_nt(a, b):
    return lax.dot_general(a, b, (((1,), (1,)), ((), ())), preferred_element_type=F32)


def dot_tn(a, b):
    return lax.dot_general(a, b, (((0,), (0,)), ((), ())), preferred_element_type=F32)


def lane_token(lane):
    x0 = (lax.axis_index("row") // 32) % 2
    return (
        (lane % 8) * 128
        + ((lane // 8) % 8) * 16
        + ((lane // 256) % 2) * 8
        + ((lane // 512) ^ x0) * 4
        + ((lane // 64) % 4)
    )


def weights_kernel(proj_ref, out_ref, final_ref, wp_ref, wu_ref, wf_ref, prow_ref, q_ref, pj_ref, sel_ref):
    core = lax.axis_index("tmpl")
    spread = onehot(iota((CH, 512), 0) == iota((CH, 512), 1) // 8)
    repeat = onehot(iota((512, CH), 0) // 8 == iota((512, CH), 1))
    diag = iota((512, 512), 0) % 8 == iota((512, 512), 1) % 8
    for layer in range(NLAYER):
        for group in range(5):
            w = proj_ref[layer, :, group * CH : (group + 1) * CH]
            wide = dot_tn(w, spread).astype(BF)
            big = dot(repeat, wide)
            big = jnp.where(diag, big, 0.0).astype(BF)
            if group < 4:
                wp_ref[layer, group * 512 : (group + 1) * 512, :] = big
            else:
                wu_ref[layer, :512, :] = big
        wide = dot_tn(out_ref[layer], spread).astype(BF)
        wu_ref[layer, 512:, :] = jnp.where(diag, dot(repeat, wide), 0.0).astype(BF)
    down = onehot(iota((512, CZ), 0) % CZ == iota((512, CZ), 1))
    across = onehot(iota((CH, 256), 0) == iota((CH, 256), 1) % CH)
    tall = dot_nt(down, final_ref[...]).astype(BF)
    block = iota((512, 256), 0) // CZ == iota((512, 256), 1) // CH
    wf_ref[...] = jnp.where(block, dot(tall, across), 0.0).astype(BF)
    r0, c0 = iota((512, 512), 0), iota((512, 512), 1)
    prow_ref[...] = onehot((r0 // 8 == c0 % CH) & (r0 % 8 == c0 // CH))
    half = (r0 // 256) ^ core
    sel_ref[...] = onehot((r0 % CH == c0 // 8) & (half * 4 + (r0 // CH) % 4 == c0 % 8))
    r1, c1 = iota((CROP, CROP), 0), iota((CROP, CROP), 1)
    token = lane_token(c1)
    q_ref[...] = onehot(r1 == token)
    dest = r1 // 8
    pj_ref[...] = onehot(((dest % 16) * 8 + dest // 16) * 8 + r1 % 8 == token)


def make_weights(proj_weight, out_weight, final_weight):
    shapes = [
        (NLAYER, 2048, 512), (NLAYER, 1024, 512), (512, 256), (512, 512),
        (CROP, CROP), (CROP, CROP), (512, 512),
    ]
    return pl.pallas_call(
        weights_kernel,
        out_shape=[pltpu.VMEM(shape, BF) if index in (1, 2, 6) else pltpu.HBM(shape, BF) for index, shape in enumerate(shapes)],
        compiler_params=pltpu.CompilerParams(vmem_limit_bytes=40 * 1024 * 1024),
        cost_estimate=pl.CostEstimate(flops=2 * 10**9, bytes_accessed=12 * 2**20, transcendentals=0),
        name="weights",
    )(proj_weight, out_weight, final_weight)


def crop_kernel(crop_ref, x_ref, o_ref):
    for a in range(8):
        start = pl.multiple_of(crop_ref[0, a] * TILE, TILE)
        o_ref[:, :, a * TILE : (a + 1) * TILE] = x_ref[:, :, pl.ds(start, TILE)]


def crop_columns(crop_tiles, pair):
    return pl.pallas_call(
        crop_kernel,
        grid_spec=pltpu.PrefetchScalarGridSpec(
            num_scalar_prefetch=1,
            grid=(4,),
            in_specs=[pl.BlockSpec((4, CH, FULL), lambda m, crop: (m, 0, 0))],
            out_specs=pl.BlockSpec((4, CH, CROP), lambda m, crop: (m, 0, 0)),
        ),
        out_shape=pltpu.HBM((16, CH, CROP), BF),
        compiler_params=pltpu.CompilerParams(vmem_limit_bytes=VMEM_LIMIT),
        name="crop",
    )(crop_tiles, *in_hbm(pair))


def norm_channels(values):
    rows, lanes = values.shape
    cube = values.reshape(CH, ROWS, lanes)
    center = cube - (jnp.sum(cube, axis=0, keepdims=True) * (1.0 / CH))
    spread = jnp.sum(center * center, axis=0, keepdims=True) * (1.0 / CH)
    return (center * lax.rsqrt(spread + EPSILON)).reshape(rows, lanes)


def sigmoid(values):
    return 0.5 * jnp.tanh(0.5 * values) + 0.5


def pair_mask(crop_ref, length_ref, lanes, start):
    chip = lax.axis_index("row")
    inside = (chip % 8) * 16 + chip // 8
    length = length_ref[0]
    lane = iota((ROWS, lanes), 1) + start
    row = iota((ROWS, lanes), 0)
    token = lane_token(lane)
    col_pos = jnp.zeros((ROWS, lanes), jnp.int32)
    row_pos = jnp.zeros((ROWS, lanes), jnp.int32)
    for a in range(8):
        base = crop_ref[0, a] * TILE
        col_pos = jnp.where(lane % 8 == a, base, col_pos)
        row_pos = jnp.where(row == a, base, row_pos)
    col_pos = col_pos + token % TILE
    row_pos = row_pos + inside
    return jnp.where((col_pos < length) & (row_pos < length), 1.0, 0.0)


def project(current, wp, mask, both_ref):
    lanes = current.shape[1]
    normed = norm_channels(current).astype(BF)
    wide = jnp.broadcast_to(mask[None], (CH, ROWS, lanes)).reshape(512, lanes)
    gate_a = dot(wp[0:512], normed)
    value_a = dot(wp[512:1024], normed)
    both_ref[:, :lanes] = (sigmoid(gate_a) * value_a * wide).astype(BF)
    gate_b = dot(wp[1024:1536], normed)
    value_b = dot(wp[1536:2048], normed)
    both_ref[:, lanes:] = (sigmoid(gate_b) * value_b * wide).astype(BF)


BLOCK = 256
ANYWHERE = pl.BlockSpec(memory_space=pl.ANY)
STEPS = CROP // BLOCK
HALF_STEPS = STEPS // 2
BOTH = pltpu.HBM((512, 2 * CROP), BF)


def when_first(step, action):
    @pl.when(step == 0)
    def _():
        action()


def first_kernel(crop_ref, length_ref, got_ref, prow_ref, q_ref, wp_hbm, cur_ref, both_ref, rows_ref, wp_ref, sem):
    step = pl.program_id(0)
    load = pltpu.make_async_copy(wp_hbm.at[0], wp_ref, sem)

    @pl.when(step == 0)
    def _():
        load.start()
        parts = jnp.concatenate([got_ref[crop_ref[0, a]] for a in range(8)], axis=0)
        rows_ref[...] = dot(prow_ref[...], parts).astype(BF)

    current = dot(rows_ref[...], q_ref[...])
    cur_ref[...] = current.astype(BF)
    mask = pair_mask(crop_ref, length_ref, BLOCK, step * BLOCK)
    when_first(step, load.wait)
    project(current, wp_ref, mask, both_ref)


def full(shape):
    return pl.BlockSpec(shape, lambda step, *_: (0,) * len(shape), pipeline_mode=pl.Buffered(1))


def lanes_of(rows, lanes=BLOCK, offset=0):
    return pl.BlockSpec((rows, lanes), lambda step, *_: (0, step + offset))


def layer_weight(rows, layer):
    return pl.BlockSpec((1, rows, 512), lambda step, *_: (layer, 0, 0), pipeline_mode=pl.Buffered(1))


def first_projection(crop_tiles, full_length, got, prow, q, wp):
    return pl.pallas_call(
        first_kernel,
        grid_spec=pltpu.PrefetchScalarGridSpec(
            num_scalar_prefetch=2,
            grid=(STEPS,),
            in_specs=[full((16, CH, CROP)), full((512, 512)), lanes_of(CROP), ANYWHERE],
            out_specs=[lanes_of(512), lanes_of(512, 2 * BLOCK)],
            scratch_shapes=[pltpu.VMEM((512, CROP), BF), pltpu.VMEM((2048, 512), BF), pltpu.SemaphoreType.DMA],
        ),
        out_shape=[pltpu.HBM((512, CROP), BF), BOTH],
        compiler_params=pltpu.CompilerParams(vmem_limit_bytes=VMEM_LIMIT),
        name="first",
    )(crop_tiles, full_length, *in_hbm(got, prow, q, wp))


def update(back_ref, cur_ref, wu):
    current = cur_ref[...].astype(F32)
    gate = sigmoid(dot(wu[:512], norm_channels(current).astype(BF)))
    normed = norm_channels(back_ref[...].astype(F32)).astype(BF)
    return (current + gate * dot(wu[512:], normed)).astype(BF)


def middle_kernel(half, layer, *refs):
    crop_ref, length_ref, back_ref, cur_ref, wu_ref, wp_hbm = refs[:6]
    next_ref, both_ref, wp_ref, sem = refs[-4:]
    step = pl.program_id(0)
    load = pltpu.make_async_copy(wp_hbm.at[layer + 1], wp_ref, sem)
    when_first(step, load.start)
    current = update(back_ref, cur_ref, wu_ref[0])
    next_ref[...] = current
    start = half * 512 + step * BLOCK
    mask = pair_mask(crop_ref, length_ref, BLOCK, start)
    when_first(step, load.wait)
    project(current.astype(F32), wp_ref, mask, both_ref)


def middle_half(half, crop_tiles, full_length, back, current, wu, wp, layer, both):
    offset = half * HALF_STEPS
    aliased = [] if both is None else [both]
    return pl.pallas_call(
        functools.partial(middle_kernel, half, layer),
        grid_spec=pltpu.PrefetchScalarGridSpec(
            num_scalar_prefetch=2,
            grid=(HALF_STEPS,),
            in_specs=[
                lanes_of(512), lanes_of(512, offset=offset),
                layer_weight(1024, layer), ANYWHERE,
            ]
            + [ANYWHERE] * len(aliased),
            out_specs=[lanes_of(512), lanes_of(512, 2 * BLOCK, offset)],
            scratch_shapes=[pltpu.VMEM((2048, 512), BF), pltpu.SemaphoreType.DMA],
        ),
        out_shape=[pltpu.HBM((512, 512), BF), BOTH],
        input_output_aliases={6: 1} if aliased else {},
        compiler_params=pltpu.CompilerParams(vmem_limit_bytes=VMEM_LIMIT),
        name="middle" + str(half),
    )(crop_tiles, full_length, *in_hbm(back, current), *in_vmem(wu), *in_hbm(wp), *aliased)


def chosen_rows(back_ref, cur_ref, wu_ref, sel_ref):
    current = update(back_ref, cur_ref, wu_ref[0])
    normed = norm_channels(current.astype(F32)).astype(BF)
    return dot(sel_ref[...], normed).astype(BF)


def last_own_kernel(back_ref, cur_ref, wu_ref, sel_ref, chosen_ref):
    chosen_ref[...] = chosen_rows(back_ref, cur_ref, wu_ref, sel_ref)


def last_peer_kernel(back_ref, cur_ref, wu_ref, sel_ref, own_ref, pj_hbm, mine_ref, other_ref, part_ref, pj_ref, sem):
    step = pl.program_id(0)
    load = pltpu.make_async_copy(pj_hbm, pj_ref, sem)
    when_first(step, load.start)
    part_ref[step] = chosen_rows(back_ref, cur_ref, wu_ref, sel_ref)

    @pl.when(step == HALF_STEPS - 1)
    def _():
        load.wait()
        chosen = jnp.concatenate([own_ref[...]] + [part_ref[k] for k in range(HALF_STEPS)], axis=1)
        mine_ref[...] = dot_nt(pj_ref[...], chosen[:256]).astype(BF)
        other_ref[...] = dot_nt(pj_ref[...], chosen[256:]).astype(BF)


def last_own(back, current, wu, sel, layer):
    return pl.pallas_call(
        last_own_kernel,
        grid=(HALF_STEPS,),
        in_specs=[lanes_of(512)] * 2 + [layer_weight(1024, layer), full((512, 512))],
        out_specs=lanes_of(512),
        out_shape=pltpu.HBM((512, 512), BF),
        compiler_params=pltpu.CompilerParams(vmem_limit_bytes=VMEM_LIMIT),
        name="last_own",
    )(*in_hbm(back, current), *in_vmem(wu, sel))


def last_peer(back, current, wu, sel, own, pj, layer):
    return pl.pallas_call(
        last_peer_kernel,
        grid=(HALF_STEPS,),
        in_specs=[lanes_of(512)] * 2
        + [layer_weight(1024, layer), full((512, 512)), full((512, 512)), ANYWHERE],
        out_specs=[full((CROP, 256))] * 2,
        out_shape=[jax.ShapeDtypeStruct((CROP, 256), BF)] * 2,
        scratch_shapes=[
            pltpu.VMEM((HALF_STEPS, 512, BLOCK), BF), pltpu.VMEM((CROP, CROP), BF), pltpu.SemaphoreType.DMA,
        ],
        compiler_params=pltpu.CompilerParams(vmem_limit_bytes=VMEM_LIMIT),
        name="last_peer",
    )(*in_hbm(back, current), *in_vmem(wu, sel), *in_hbm(own, pj))


def own_products_kernel(both_ref, out_ref, right_ref, sum_ref):
    step = pl.program_id(0)
    right = both_ref[:, BLOCK:]
    right_ref[...] = right
    part = dot_nt(both_ref[:, :BLOCK], right)
    add_products(step, part, out_ref, sum_ref)


def add_products(step, part, out_ref, sum_ref):
    @pl.when(step == 0)
    def _():
        sum_ref[...] = part

    @pl.when((step > 0) & (step < STEPS - 1))
    def _():
        sum_ref[...] += part

    @pl.when(step == STEPS - 1)
    def _():
        out_ref[...] = (sum_ref[...] + part).astype(BF)


def own_products(both):
    return pl.pallas_call(
        own_products_kernel,
        grid=(STEPS,),
        in_specs=[lanes_of(512, 2 * BLOCK)],
        out_specs=[full((512, 512)), lanes_of(512)],
        out_shape=[pltpu.HBM((512, 512), BF), pltpu.HBM((512, CROP), BF)],
        scratch_shapes=[pltpu.VMEM((512, 512), F32)],
        compiler_params=pltpu.CompilerParams(vmem_limit_bytes=VMEM_LIMIT),
        cost_estimate=pl.CostEstimate(flops=2**29, bytes_accessed=4 * 2**20, transcendentals=0),
        name="own_products",
    )(*in_hbm(both))


def peer_products_kernel(left_ref, right_ref, out_ref, sum_ref):
    add_products(pl.program_id(0), dot_nt(left_ref[...], right_ref[...]), out_ref, sum_ref)


def peer_products(both, right):
    return pl.pallas_call(
        peer_products_kernel,
        grid=(STEPS,),
        in_specs=[
            pl.BlockSpec((512, BLOCK), lambda step: (0, ((step + HALF_STEPS) % STEPS) * 2)),
            lanes_of(512),
        ],
        out_specs=full((512, 512)),
        out_shape=pltpu.HBM((512, 512), BF),
        scratch_shapes=[pltpu.VMEM((512, 512), F32)],
        compiler_params=pltpu.CompilerParams(vmem_limit_bytes=VMEM_LIMIT),
        cost_estimate=pl.CostEstimate(flops=2**29, bytes_accessed=4 * 2**20, transcendentals=0),
        name="peer_products",
    )(*in_hbm(both, right))


def hidden_features(mine, peer):
    total = mine.astype(F32) + peer.astype(F32)
    return jnp.maximum(total * 0.5, 0.0).astype(BF)


def final_kernel(mine_ref, peer_ref, wf_ref, out_ref, tall0_ref, tall1_ref, wide_ref):
    core = lax.axis_index("tmpl")
    wf = wf_ref[...]
    for source, ref in enumerate((mine_ref, peer_ref)):
        half = core if source == 0 else 1 - core
        tall0_ref[...] = ref[:, :128].astype(F32)
        tall1_ref[...] = ref[:, 128:].astype(F32)
        for j in range(8):
            rows = jnp.concatenate(
                [tall0_ref[pl.ds(j, 128, stride=8), :], tall1_ref[pl.ds(j, 128, stride=8), :]], axis=1
            ).astype(BF)
            result = dot_nt(wf, rows)
            for a in range(4):
                wide_ref[half * 4 + a, pl.ds(j, CZ, stride=8), :] = result[a * CZ : (a + 1) * CZ]
    for a in range(8):
        out_ref[:, a * TILE : (a + 1) * TILE] = wide_ref[a].astype(BF)


def final_projection(mine, peer, wf):
    return pl.pallas_call(
        final_kernel,
        out_shape=jax.ShapeDtypeStruct((CZ * 8, CROP), BF),
        scratch_shapes=[
            pltpu.VMEM((CROP, 128), F32), pltpu.VMEM((CROP, 128), F32), pltpu.VMEM((8, CZ * 8, TILE), F32)
        ],
        compiler_params=pltpu.CompilerParams(vmem_limit_bytes=VMEM_LIMIT),
        name="final",
    )(mine, peer, wf)


def exchange(values, groups, count):
    cube = values.reshape(count, -1, values.shape[-1])
    moved = lax.all_to_all(cube, "row", 0, 0, axis_index_groups=groups, tiled=True)
    return moved.reshape(values.shape)


def on_device(pair_maps, crop_tiles, full_length, proj_weight, out_weight, final_weight):
    wp, wu, wf, prow, q, pj, sel = make_weights(proj_weight, out_weight, final_weight)
    pair = jnp.transpose(pair_maps[0], (0, 2, 1))
    cropped = crop_columns(crop_tiles, pair)
    got = lax.all_to_all(cropped, "row", 0, 0, axis_index_groups=PLANE, tiled=True)
    current, both = first_projection(crop_tiles, full_length, got, prow, q, wp)
    currents = (current, current)
    for layer in range(NLAYER):
        gathered = exchange(both, SAME_X0, CH)
        products, right = own_products(gathered)
        back_own = exchange(products, SAME_X0, CH)
        right_peer = lax.ppermute(right, "row", X0_PAIRS)
        back_peer = exchange(peer_products(gathered, right_peer), SAME_X0, CH)
        if layer + 1 < NLAYER:
            scalars, weights = (crop_tiles, full_length), (wu, wp, layer)
            own, both = middle_half(0, *scalars, back_own, currents[0], *weights, None)
            peer, both = middle_half(1, *scalars, back_peer, currents[1], *weights, both)
            currents = (own, peer)
    chosen = last_own(back_own, currents[0], wu, sel, NLAYER - 1)
    mine, other = last_peer(back_peer, currents[1], wu, sel, chosen, pj, NLAYER - 1)
    hidden = hidden_features(mine, lax.ppermute(other, "tmpl", CORES))
    moved = exchange(hidden, BY_Z, 128)
    result = final_projection(moved, lax.ppermute(moved, "tmpl", CORES), wf)
    return result.reshape(CZ, 8, CROP)


def solution(mesh):
    placed = (P("tmpl", "row", None, None), P("tmpl", None), P(), P(), P(), P())
    return jax.shard_map(
        on_device, mesh=mesh, in_specs=placed, out_specs=P(None, "row", None), check_vma=False
    )
```

```python
import functools

import jax
import jax.numpy as jnp
from jax import lax
from jax.experimental import pallas as pl
from jax.experimental.pallas import tpu as pltpu
from jax.sharding import PartitionSpec as P

CH = 64
CZ = 128
CROP = 1024
TILE = 128
NLAYER = 2
FULL = 2048
ROWS = 8
EPSILON = 1e-05
BF = jnp.bfloat16
F32 = jnp.float32

PLANE = [[s * 8 + z for s in range(16)] for z in range(8)]
SAME_X0 = [
    [(x1 * 2 + x0) * 32 + y * 8 + z for x1 in range(2) for y in range(4) for z in range(8)]
    for x0 in range(2)
]
BY_Z = [[s * 8 + z for z in range(8) for s in range(16)]]
X0_PAIRS = [(r, r ^ 32) for r in range(128)]
CORES = [(0, 1), (1, 0)]
VMEM_LIMIT = 20 * 1024 * 1024


def in_vmem(*arrays):
    return [pltpu.with_memory_space_constraint(array, pltpu.VMEM) for array in arrays]


def in_hbm(*arrays):
    return [pltpu.with_memory_space_constraint(array, pltpu.HBM) for array in arrays]


def iota(shape, dim):
    return lax.broadcasted_iota(jnp.int32, shape, dim)


def onehot(mask):
    return jnp.where(mask, 1.0, 0.0).astype(BF)


def dot(a, b):
    return jnp.dot(a, b, preferred_element_type=F32)


def dot_nt(a, b):
    return lax.dot_general(a, b, (((1,), (1,)), ((), ())), preferred_element_type=F32)


def dot_tn(a, b):
    return lax.dot_general(a, b, (((0,), (0,)), ((), ())), preferred_element_type=F32)


def lane_token(lane):
    x0 = (lax.axis_index("row") // 32) % 2
    return (
        (lane % 8) * 128
        + ((lane // 8) % 8) * 16
        + ((lane // 256) % 2) * 8
        + ((lane // 512) ^ x0) * 4
        + ((lane // 64) % 4)
    )


def weights_kernel(builder, *refs):
    count = len(WEIGHT_SHAPES)
    outs, scratch, sems = refs[-2 * count - 1 : -count - 1], refs[-count - 1 : -1], refs[-1]

    @pl.when(lax.axis_index("tmpl") == builder)
    def _():
        build_weights(builder, *refs[:3], *scratch)
        copies = [pltpu.make_async_copy(scratch[k], outs[k], sems.at[k]) for k in range(count)]
        for copy in copies:
            copy.start()
        for copy in copies:
            copy.wait()


def build_weights(core, proj_ref, out_ref, final_ref, wp_ref, wu_ref, wf_ref, prow_ref, q_ref, pj_ref, sel_ref):
    spread = onehot(iota((CH, 512), 0) == iota((CH, 512), 1) // 8)
    repeat = onehot(iota((512, CH), 0) // 8 == iota((512, CH), 1))
    diag = iota((512, 512), 0) % 8 == iota((512, 512), 1) % 8
    for layer in range(NLAYER):
        for group in range(5):
            w = proj_ref[layer, :, group * CH : (group + 1) * CH]
            wide = dot_tn(w, spread).astype(BF)
            big = dot(repeat, wide)
            big = jnp.where(diag, big, 0.0).astype(BF)
            if group < 4:
                wp_ref[layer, group * 512 : (group + 1) * 512, :] = big
            else:
                wu_ref[layer, :512, :] = big
        wide = dot_tn(out_ref[layer], spread).astype(BF)
        wu_ref[layer, 512:, :] = jnp.where(diag, dot(repeat, wide), 0.0).astype(BF)
    down = onehot(iota((512, CZ), 0) % CZ == iota((512, CZ), 1))
    across = onehot(iota((CH, 256), 0) == iota((CH, 256), 1) % CH)
    tall = dot_nt(down, final_ref[...]).astype(BF)
    block = iota((512, 256), 0) // CZ == iota((512, 256), 1) // CH
    wf_ref[...] = jnp.where(block, dot(tall, across), 0.0).astype(BF)
    r0, c0 = iota((512, 512), 0), iota((512, 512), 1)
    prow_ref[...] = onehot((r0 // 8 == c0 % CH) & (r0 % 8 == c0 // CH))
    half = (r0 // 256) ^ core
    sel_ref[...] = onehot((r0 % CH == c0 // 8) & (half * 4 + (r0 // CH) % 4 == c0 % 8))
    r1, c1 = iota((CROP, CROP), 0), iota((CROP, CROP), 1)
    token = lane_token(c1)
    q_ref[...] = onehot(r1 == token)
    dest = r1 // 8
    pj_ref[...] = onehot(((dest % 16) * 8 + dest // 16) * 8 + r1 % 8 == token)


WEIGHT_SHAPES = [
    (NLAYER, 2048, 512), (NLAYER, 1024, 512), (512, 256), (512, 512), (CROP, CROP), (CROP, CROP), (512, 512),
]


def make_weights(builder, params, earlier=()):
    count = len(WEIGHT_SHAPES)
    anywhere = pl.BlockSpec(memory_space=pl.ANY)
    in_vmem_specs = [pl.BlockSpec(memory_space=pltpu.VMEM)] * 3
    return pl.pallas_call(
        functools.partial(weights_kernel, builder),
        in_specs=in_vmem_specs + [anywhere] * len(earlier),
        out_specs=[anywhere] * count,
        out_shape=[pltpu.HBM(shape, BF) for shape in WEIGHT_SHAPES],
        scratch_shapes=[pltpu.VMEM(shape, BF) for shape in WEIGHT_SHAPES] + [pltpu.SemaphoreType.DMA((count,))],
        input_output_aliases={3 + k: k for k in range(len(earlier))},
        compiler_params=pltpu.CompilerParams(vmem_limit_bytes=48 * 1024 * 1024),
        cost_estimate=pl.CostEstimate(flops=2 * 10**9, bytes_accessed=12 * 2**20, transcendentals=0),
        name="weights" + str(builder),
    )(*params, *earlier)


def crop_kernel(crop_ref, x_ref, after_ref, o_ref):
    del after_ref
    for a in range(8):
        start = pl.multiple_of(crop_ref[0, a] * TILE, TILE)
        o_ref[:, :, a * TILE : (a + 1) * TILE] = x_ref[:, :, pl.ds(start, TILE)]


def crop_columns(crop_tiles, pair, after):
    return pl.pallas_call(
        crop_kernel,
        grid_spec=pltpu.PrefetchScalarGridSpec(
            num_scalar_prefetch=1,
            grid=(4,),
            in_specs=[pl.BlockSpec((4, CH, FULL), lambda m, crop: (m, 0, 0)), pl.BlockSpec(memory_space=pl.ANY)],
            out_specs=pl.BlockSpec((4, CH, CROP), lambda m, crop: (m, 0, 0)),
        ),
        out_shape=pltpu.HBM((16, CH, CROP), BF),
        compiler_params=pltpu.CompilerParams(vmem_limit_bytes=VMEM_LIMIT),
        name="crop",
    )(crop_tiles, *in_hbm(pair), after)


def norm_channels(values):
    rows, lanes = values.shape
    cube = values.reshape(CH, ROWS, lanes)
    center = cube - (jnp.sum(cube, axis=0, keepdims=True) * (1.0 / CH))
    spread = jnp.sum(center * center, axis=0, keepdims=True) * (1.0 / CH)
    return (center * lax.rsqrt(spread + EPSILON)).reshape(rows, lanes)


def sigmoid(values):
    return 0.5 * jnp.tanh(0.5 * values) + 0.5


def pair_mask(crop_ref, length_ref, lanes, start):
    chip = lax.axis_index("row")
    inside = (chip % 8) * 16 + chip // 8
    length = length_ref[0]
    lane = iota((ROWS, lanes), 1) + start
    row = iota((ROWS, lanes), 0)
    token = lane_token(lane)
    col_pos = jnp.zeros((ROWS, lanes), jnp.int32)
    row_pos = jnp.zeros((ROWS, lanes), jnp.int32)
    for a in range(8):
        base = crop_ref[0, a] * TILE
        col_pos = jnp.where(lane % 8 == a, base, col_pos)
        row_pos = jnp.where(row == a, base, row_pos)
    col_pos = col_pos + token % TILE
    row_pos = row_pos + inside
    return jnp.where((col_pos < length) & (row_pos < length), 1.0, 0.0)


def project(current, wp, mask, both_ref):
    lanes = current.shape[1]
    normed = norm_channels(current).astype(BF)
    wide = jnp.broadcast_to(mask[None], (CH, ROWS, lanes)).reshape(512, lanes)
    gate_a = dot(wp[0:512], normed)
    value_a = dot(wp[512:1024], normed)
    both_ref[:, :lanes] = (sigmoid(gate_a) * value_a * wide).astype(BF)
    gate_b = dot(wp[1024:1536], normed)
    value_b = dot(wp[1536:2048], normed)
    both_ref[:, lanes:] = (sigmoid(gate_b) * value_b * wide).astype(BF)


BLOCK = 256
ANYWHERE = pl.BlockSpec(memory_space=pl.ANY)
STEPS = CROP // BLOCK
HALF_STEPS = STEPS // 2
BOTH = pltpu.HBM((512, 2 * CROP), BF)


def when_first(step, action):
    @pl.when(step == 0)
    def _():
        action()


def first_kernel(crop_ref, length_ref, got_ref, prow_ref, q_ref, wp_hbm, cur_ref, both_ref, rows_ref, wp_ref, sem):
    step = pl.program_id(0)
    load = pltpu.make_async_copy(wp_hbm.at[0], wp_ref, sem)

    @pl.when(step == 0)
    def _():
        load.start()
        parts = jnp.concatenate([got_ref[crop_ref[0, a]] for a in range(8)], axis=0)
        rows_ref[...] = dot(prow_ref[...], parts).astype(BF)

    current = dot(rows_ref[...], q_ref[...])
    cur_ref[...] = current.astype(BF)
    mask = pair_mask(crop_ref, length_ref, BLOCK, step * BLOCK)
    when_first(step, load.wait)
    project(current, wp_ref, mask, both_ref)


def full(shape):
    return pl.BlockSpec(shape, lambda step, *_: (0,) * len(shape), pipeline_mode=pl.Buffered(1))


def lanes_of(rows, lanes=BLOCK, offset=0):
    return pl.BlockSpec((rows, lanes), lambda step, *_: (0, step + offset))


def layer_weight(rows, layer):
    return pl.BlockSpec((1, rows, 512), lambda step, *_: (layer, 0, 0), pipeline_mode=pl.Buffered(1))


def first_projection(crop_tiles, full_length, got, prow, q, wp):
    return pl.pallas_call(
        first_kernel,
        grid_spec=pltpu.PrefetchScalarGridSpec(
            num_scalar_prefetch=2,
            grid=(STEPS,),
            in_specs=[full((16, CH, CROP)), full((512, 512)), lanes_of(CROP), ANYWHERE],
            out_specs=[lanes_of(512), lanes_of(512, 2 * BLOCK)],
            scratch_shapes=[pltpu.VMEM((512, CROP), BF), pltpu.VMEM((2048, 512), BF), pltpu.SemaphoreType.DMA],
        ),
        out_shape=[pltpu.HBM((512, CROP), BF), BOTH],
        compiler_params=pltpu.CompilerParams(vmem_limit_bytes=VMEM_LIMIT),
        name="first",
    )(crop_tiles, full_length, got, *in_hbm(prow, q, wp))


def update(back_ref, cur_ref, wu):
    current = cur_ref[...].astype(F32)
    gate = sigmoid(dot(wu[:512], norm_channels(current).astype(BF)))
    normed = norm_channels(back_ref[...].astype(F32)).astype(BF)
    return (current + gate * dot(wu[512:], normed)).astype(BF)


def middle_kernel(half, layer, *refs):
    crop_ref, length_ref, back_ref, cur_ref, wu_ref, wp_hbm = refs[:6]
    next_ref, both_ref, wp_ref, sem = refs[-4:]
    step = pl.program_id(0)
    load = pltpu.make_async_copy(wp_hbm.at[layer + 1], wp_ref, sem)
    when_first(step, load.start)
    current = update(back_ref, cur_ref, wu_ref[0])
    next_ref[...] = current
    start = half * 512 + step * BLOCK
    mask = pair_mask(crop_ref, length_ref, BLOCK, start)
    when_first(step, load.wait)
    project(current.astype(F32), wp_ref, mask, both_ref)


def middle_half(half, crop_tiles, full_length, back, current, wu, wp, layer, both):
    offset = half * HALF_STEPS
    aliased = [] if both is None else [both]
    return pl.pallas_call(
        functools.partial(middle_kernel, half, layer),
        grid_spec=pltpu.PrefetchScalarGridSpec(
            num_scalar_prefetch=2,
            grid=(HALF_STEPS,),
            in_specs=[
                lanes_of(512), lanes_of(512, offset=offset),
                layer_weight(1024, layer), ANYWHERE,
            ]
            + [ANYWHERE] * len(aliased),
            out_specs=[lanes_of(512), lanes_of(512, 2 * BLOCK, offset)],
            scratch_shapes=[pltpu.VMEM((2048, 512), BF), pltpu.SemaphoreType.DMA],
        ),
        out_shape=[pltpu.HBM((512, 512), BF), BOTH],
        input_output_aliases={6: 1} if aliased else {},
        compiler_params=pltpu.CompilerParams(vmem_limit_bytes=VMEM_LIMIT),
        name="middle" + str(half),
    )(crop_tiles, full_length, back, *in_hbm(current), *in_vmem(wu), *in_hbm(wp), *aliased)


def chosen_rows(back_ref, cur_ref, wu_ref, sel_ref):
    current = update(back_ref, cur_ref, wu_ref[0])
    normed = norm_channels(current.astype(F32)).astype(BF)
    return dot(sel_ref[...], normed).astype(BF)


def last_own_kernel(back_ref, cur_ref, wu_ref, sel_ref, chosen_ref):
    chosen_ref[...] = chosen_rows(back_ref, cur_ref, wu_ref, sel_ref)


def last_peer_kernel(back_ref, cur_ref, wu_ref, sel_ref, own_ref, pj_hbm, mine_ref, other_ref, part_ref, pj_ref, sem):
    step = pl.program_id(0)
    load = pltpu.make_async_copy(pj_hbm, pj_ref, sem)
    when_first(step, load.start)
    part_ref[step] = chosen_rows(back_ref, cur_ref, wu_ref, sel_ref)

    @pl.when(step == HALF_STEPS - 1)
    def _():
        load.wait()
        chosen = jnp.concatenate([own_ref[...]] + [part_ref[k] for k in range(HALF_STEPS)], axis=1)
        mine_ref[...] = dot_nt(pj_ref[...], chosen[:256]).astype(BF)
        other_ref[...] = dot_nt(pj_ref[...], chosen[256:]).astype(BF)


def last_own(back, current, wu, sel, layer):
    return pl.pallas_call(
        last_own_kernel,
        grid=(HALF_STEPS,),
        in_specs=[lanes_of(512)] * 2 + [layer_weight(1024, layer), full((512, 512))],
        out_specs=lanes_of(512),
        out_shape=pltpu.HBM((512, 512), BF),
        compiler_params=pltpu.CompilerParams(vmem_limit_bytes=VMEM_LIMIT),
        name="last_own",
    )(back, *in_hbm(current), *in_vmem(wu, sel))


def last_peer(back, current, wu, sel, own, pj, layer):
    return pl.pallas_call(
        last_peer_kernel,
        grid=(HALF_STEPS,),
        in_specs=[lanes_of(512)] * 2
        + [layer_weight(1024, layer), full((512, 512)), full((512, 512)), ANYWHERE],
        out_specs=[full((CROP, 256))] * 2,
        out_shape=[jax.ShapeDtypeStruct((CROP, 256), BF)] * 2,
        scratch_shapes=[
            pltpu.VMEM((HALF_STEPS, 512, BLOCK), BF), pltpu.VMEM((CROP, CROP), BF), pltpu.SemaphoreType.DMA,
        ],
        compiler_params=pltpu.CompilerParams(vmem_limit_bytes=VMEM_LIMIT),
        name="last_peer",
    )(back, *in_hbm(current), *in_vmem(wu, sel), *in_hbm(own, pj))


def lane_blocks(both_ref, which, order):
    starts = [(2 * block + which) * BLOCK for block in order]
    return jnp.concatenate([both_ref[:, start : start + BLOCK] for start in starts], axis=1)


def own_products_kernel(both_ref, out_ref, right_ref):
    right = lane_blocks(both_ref, 1, range(STEPS))
    right_ref[...] = right
    out_ref[...] = dot_nt(lane_blocks(both_ref, 0, range(STEPS)), right).astype(BF)


def own_products(both):
    return pl.pallas_call(
        own_products_kernel,
        out_shape=[pltpu.HBM((512, 512), BF), pltpu.HBM((512, CROP), BF)],
        compiler_params=pltpu.CompilerParams(vmem_limit_bytes=VMEM_LIMIT),
        cost_estimate=pl.CostEstimate(flops=2**29, bytes_accessed=4 * 2**20, transcendentals=0),
        name="own_products",
    )(both)


def peer_products_kernel(both_ref, right_ref, out_ref):
    left = lane_blocks(both_ref, 0, [2, 3, 0, 1])
    out_ref[...] = dot_nt(left, right_ref[...]).astype(BF)


def peer_products(both, right):
    return pl.pallas_call(
        peer_products_kernel,
        out_shape=pltpu.HBM((512, 512), BF),
        compiler_params=pltpu.CompilerParams(vmem_limit_bytes=VMEM_LIMIT),
        cost_estimate=pl.CostEstimate(flops=2**29, bytes_accessed=4 * 2**20, transcendentals=0),
        name="peer_products",
    )(both, right)


def hidden_features(mine, peer):
    total = mine.astype(F32) + peer.astype(F32)
    return jnp.maximum(total * 0.5, 0.0).astype(BF)


def final_kernel(mine_ref, peer_ref, wf_ref, out_ref, tall0_ref, tall1_ref, wide_ref):
    core = lax.axis_index("tmpl")
    wf = wf_ref[...]
    for source, ref in enumerate((mine_ref, peer_ref)):
        half = core if source == 0 else 1 - core
        tall0_ref[...] = ref[:, :128].astype(F32)
        tall1_ref[...] = ref[:, 128:].astype(F32)
        for j in range(8):
            rows = jnp.concatenate(
                [tall0_ref[pl.ds(j, 128, stride=8), :], tall1_ref[pl.ds(j, 128, stride=8), :]], axis=1
            ).astype(BF)
            result = dot_nt(wf, rows)
            for a in range(4):
                wide_ref[half * 4 + a, pl.ds(j, CZ, stride=8), :] = result[a * CZ : (a + 1) * CZ]
    for a in range(8):
        out_ref[:, a * TILE : (a + 1) * TILE] = wide_ref[a].astype(BF)


def final_projection(mine, peer, wf):
    return pl.pallas_call(
        final_kernel,
        out_shape=jax.ShapeDtypeStruct((CZ * 8, CROP), BF),
        scratch_shapes=[
            pltpu.VMEM((CROP, 128), F32), pltpu.VMEM((CROP, 128), F32), pltpu.VMEM((8, CZ * 8, TILE), F32)
        ],
        compiler_params=pltpu.CompilerParams(vmem_limit_bytes=VMEM_LIMIT),
        name="final",
    )(mine, peer, wf)


def exchange(values, groups, count):
    cube = values.reshape(count, -1, values.shape[-1])
    moved = lax.all_to_all(cube, "row", 0, 0, axis_index_groups=groups, tiled=True)
    return moved.reshape(values.shape)


def on_device(pair_maps, crop_tiles, full_length, proj_weight, out_weight, final_weight):
    params = (proj_weight, out_weight, final_weight)
    early = make_weights(1, params)
    pair = jnp.transpose(pair_maps[0], (0, 2, 1))
    cropped = crop_columns(crop_tiles, pair, early[2])
    got = lax.all_to_all(cropped, "row", 0, 0, axis_index_groups=PLANE, tiled=True)
    wp, wu, wf, prow, q, pj, sel = make_weights(0, params, early)
    current, both = first_projection(crop_tiles, full_length, got, prow, q, wp)
    currents = (current, current)
    for layer in range(NLAYER):
        gathered = exchange(both, SAME_X0, CH)
        products, right = own_products(gathered)
        back_own = exchange(products, SAME_X0, CH)
        right_peer = lax.ppermute(right, "row", X0_PAIRS)
        back_peer = exchange(peer_products(gathered, right_peer), SAME_X0, CH)
        if layer + 1 < NLAYER:
            scalars, weights = (crop_tiles, full_length), (wu, wp, layer)
            own, both = middle_half(0, *scalars, back_own, currents[0], *weights, None)
            peer, both = middle_half(1, *scalars, back_peer, currents[1], *weights, both)
            currents = (own, peer)
    chosen = last_own(back_own, currents[0], wu, sel, NLAYER - 1)
    mine, other = last_peer(back_peer, currents[1], wu, sel, chosen, pj, NLAYER - 1)
    hidden = hidden_features(mine, lax.ppermute(other, "tmpl", CORES))
    moved = exchange(hidden, BY_Z, 128)
    result = final_projection(moved, lax.ppermute(moved, "tmpl", CORES), wf)
    return result.reshape(CZ, 8, CROP)


def solution(mesh):
    placed = (P("tmpl", "row", None, None), P("tmpl", None), P(), P(), P(), P())
    return jax.shard_map(
        on_device, mesh=mesh, in_specs=placed, out_specs=P(None, "row", None), check_vma=False
    )
```

```python
import functools

import jax
import jax.numpy as jnp
from jax import lax
from jax.experimental import pallas as pl
from jax.experimental.pallas import tpu as pltpu
from jax.sharding import PartitionSpec as P

CH = 64
CZ = 128
CROP = 1024
TILE = 128
NLAYER = 2
FULL = 2048
ROWS = 8
EPSILON = 1e-05
BF = jnp.bfloat16
F32 = jnp.float32

PLANE = [[s * 8 + z for s in range(16)] for z in range(8)]
SAME_X0 = [
    [(x1 * 2 + x0) * 32 + y * 8 + z for x1 in range(2) for y in range(4) for z in range(8)]
    for x0 in range(2)
]
BY_Z = [[s * 8 + z for z in range(8) for s in range(16)]]
X0_PAIRS = [(r, r ^ 32) for r in range(128)]
CORES = [(0, 1), (1, 0)]
VMEM_LIMIT = 20 * 1024 * 1024


def in_vmem(*arrays):
    return [pltpu.with_memory_space_constraint(array, pltpu.VMEM) for array in arrays]


def in_hbm(*arrays):
    return [pltpu.with_memory_space_constraint(array, pltpu.HBM) for array in arrays]


def iota(shape, dim):
    return lax.broadcasted_iota(jnp.int32, shape, dim)


def onehot(mask):
    return jnp.where(mask, 1.0, 0.0).astype(BF)


def dot(a, b):
    return jnp.dot(a, b, preferred_element_type=F32)


def dot_nt(a, b):
    return lax.dot_general(a, b, (((1,), (1,)), ((), ())), preferred_element_type=F32)


def dot_tn(a, b):
    return lax.dot_general(a, b, (((0,), (0,)), ((), ())), preferred_element_type=F32)


def lane_token(lane):
    x0 = (lax.axis_index("row") // 32) % 2
    return (
        (lane % 8) * 128
        + ((lane // 8) % 8) * 16
        + ((lane // 256) % 2) * 8
        + ((lane // 512) ^ x0) * 4
        + ((lane // 64) % 4)
    )


def tables_kernel(final_ref, wf_ref, prow_ref, q_ref, pj_ref):
    down = onehot(iota((512, CZ), 0) % CZ == iota((512, CZ), 1))
    across = onehot(iota((CH, 256), 0) == iota((CH, 256), 1) % CH)
    tall = dot_nt(down, final_ref[...]).astype(BF)
    block = iota((512, 256), 0) // CZ == iota((512, 256), 1) // CH
    wf_ref[...] = jnp.where(block, dot(tall, across), 0.0).astype(BF)
    r0, c0 = iota((512, 512), 0), iota((512, 512), 1)
    prow_ref[...] = onehot((r0 // 8 == c0 % CH) & (r0 % 8 == c0 // CH))
    r1, c1 = iota((CROP, CROP), 0), iota((CROP, CROP), 1)
    token = lane_token(c1)
    q_ref[...] = onehot(r1 == token)
    dest = r1 // 8
    pj_ref[...] = onehot(((dest % 16) * 8 + dest // 16) * 8 + r1 % 8 == token)


def make_tables(final_weight):
    return pl.pallas_call(
        tables_kernel,
        out_shape=[
            pltpu.VMEM((512, 256), BF), pltpu.VMEM((512, 512), BF),
            pltpu.HBM((CROP, CROP), BF), pltpu.HBM((CROP, CROP), BF),
        ],
        compiler_params=pltpu.CompilerParams(vmem_limit_bytes=40 * 1024 * 1024),
        cost_estimate=pl.CostEstimate(flops=10**9, bytes_accessed=6 * 2**20, transcendentals=0),
        name="tables",
    )(final_weight)


def crop_kernel(crop_ref, x_ref, o_ref):
    for a in range(8):
        start = pl.multiple_of(crop_ref[0, a] * TILE, TILE)
        o_ref[:, :, a * TILE : (a + 1) * TILE] = x_ref[:, :, pl.ds(start, TILE)]


def crop_columns(crop_tiles, pair):
    return pl.pallas_call(
        crop_kernel,
        grid_spec=pltpu.PrefetchScalarGridSpec(
            num_scalar_prefetch=1,
            grid=(4,),
            in_specs=[pl.BlockSpec((4, CH, FULL), lambda m, crop: (m, 0, 0))],
            out_specs=pl.BlockSpec((4, CH, CROP), lambda m, crop: (m, 0, 0)),
        ),
        out_shape=pltpu.HBM((16, CH, CROP), BF),
        compiler_params=pltpu.CompilerParams(vmem_limit_bytes=VMEM_LIMIT),
        name="crop",
    )(crop_tiles, *in_hbm(pair))


def norm_channels(values):
    center = values - jnp.sum(values, axis=0, keepdims=True) * (1.0 / CH)
    spread = jnp.sum(center * center, axis=0, keepdims=True) * (1.0 / CH)
    return center * lax.rsqrt(spread + EPSILON)


def sigmoid(values):
    return 0.5 * jnp.tanh(0.5 * values) + 0.5


def side_by_side(values):
    return jnp.concatenate([values[a * CH : (a + 1) * CH] for a in range(ROWS)], axis=1)


def stacked(values):
    lanes = values.shape[1] // ROWS
    return jnp.concatenate([values[:, a * lanes : (a + 1) * lanes] for a in range(ROWS)], axis=0)


def pair_mask(crop_ref, length_ref, lanes, start):
    chip = lax.axis_index("row")
    inside = (chip % 8) * 16 + chip // 8
    length = length_ref[0]
    lane = iota((1, lanes), 1) + start
    position = lane_token(lane) % TILE
    for a in range(ROWS):
        position = position + jnp.where(lane % 8 == a, crop_ref[0, a] * TILE, 0)
    parts = []
    for a in range(ROWS):
        row_position = crop_ref[0, a] * TILE + inside
        parts.append(jnp.where((position < length) & (row_position < length), 1.0, 0.0))
    return jnp.concatenate(parts, axis=1)


def project(current, w, prow, mask, both_ref):
    values = dot_tn(w[:, : 4 * CH], norm_channels(current).astype(BF))
    lanes = both_ref.shape[1] // 2
    for side in range(2):
        gate = values[side * 128 : side * 128 + CH]
        value = values[side * 128 + CH : side * 128 + 2 * CH]
        factor = (sigmoid(gate) * value * mask).astype(BF)
        both_ref[:, side * lanes : (side + 1) * lanes] = dot(prow, stacked(factor)).astype(BF)


BLOCK = 256
ANYWHERE = pl.BlockSpec(memory_space=pl.ANY)
STEPS = CROP // BLOCK
HALF_STEPS = STEPS // 2
BOTH = pltpu.HBM((512, 2 * CROP), BF)


def first_kernel(crop_ref, length_ref, got_ref, prow_ref, q_ref, w_ref, cur_ref, both_ref):
    step = pl.program_id(0)
    parts = jnp.concatenate([got_ref[crop_ref[0, a]] for a in range(ROWS)], axis=0)
    current = dot(parts, q_ref[...])
    cur_ref[...] = current.astype(BF)
    mask = pair_mask(crop_ref, length_ref, BLOCK, step * BLOCK)
    project(side_by_side(current), w_ref[0], prow_ref[...], mask, both_ref)


def full(shape):
    return pl.BlockSpec(shape, lambda step, *_: (0,) * len(shape), pipeline_mode=pl.Buffered(1))


def lanes_of(rows, lanes=BLOCK, offset=0):
    return pl.BlockSpec((rows, lanes), lambda step, *_: (0, step + offset))


def layer_weight(columns, layer):
    return pl.BlockSpec((1, CH, columns), lambda step, *_: (layer, 0, 0), pipeline_mode=pl.Buffered(1))


def first_projection(crop_tiles, full_length, got, prow, q, proj_weight):
    return pl.pallas_call(
        first_kernel,
        grid_spec=pltpu.PrefetchScalarGridSpec(
            num_scalar_prefetch=2,
            grid=(STEPS,),
            in_specs=[full((16, CH, CROP)), full((512, 512)), lanes_of(CROP), layer_weight(320, 0)],
            out_specs=[lanes_of(512), lanes_of(512, 2 * BLOCK)],
        ),
        out_shape=[pltpu.HBM((512, CROP), BF), BOTH],
        compiler_params=pltpu.CompilerParams(vmem_limit_bytes=VMEM_LIMIT),
        name="first",
    )(crop_tiles, full_length, got, *in_vmem(prow), *in_hbm(q), proj_weight)


def update(back_ref, cur_ref, prow, w_proj, w_out):
    current = side_by_side(cur_ref[...].astype(F32))
    gate = sigmoid(dot_tn(w_proj[:, 4 * CH :], norm_channels(current).astype(BF)))
    products = side_by_side(dot_tn(prow, back_ref[...]))
    change = dot_tn(w_out, norm_channels(products).astype(BF))
    return (current + gate * change).astype(BF)


def middle_kernel(half, *refs):
    crop_ref, length_ref, back_ref, cur_ref, prow_ref, w_ref, w_out_ref, w_next_ref = refs[:8]
    next_ref, both_ref = refs[-2:]
    current = update(back_ref, cur_ref, prow_ref[...], w_ref[0], w_out_ref[0])
    next_ref[...] = stacked(current)
    mask = pair_mask(crop_ref, length_ref, BLOCK, half * 512 + pl.program_id(0) * BLOCK)
    project(current.astype(F32), w_next_ref[0], prow_ref[...], mask, both_ref)


def middle_half(half, crop_tiles, full_length, back, current, prow, proj_weight, out_weight, layer, both):
    offset = half * HALF_STEPS
    aliased = [] if both is None else [both]
    return pl.pallas_call(
        functools.partial(middle_kernel, half),
        grid_spec=pltpu.PrefetchScalarGridSpec(
            num_scalar_prefetch=2,
            grid=(HALF_STEPS,),
            in_specs=[
                lanes_of(512), lanes_of(512, offset=offset), full((512, 512)),
                layer_weight(320, layer), layer_weight(CH, layer), layer_weight(320, layer + 1),
            ]
            + [ANYWHERE] * len(aliased),
            out_specs=[lanes_of(512), lanes_of(512, 2 * BLOCK, offset)],
        ),
        out_shape=[pltpu.HBM((512, 512), BF), BOTH],
        input_output_aliases={8: 1} if aliased else {},
        compiler_params=pltpu.CompilerParams(vmem_limit_bytes=VMEM_LIMIT),
        name="middle" + str(half),
    )(
        crop_tiles, full_length, back, *in_hbm(current), *in_vmem(prow), proj_weight, out_weight, proj_weight,
        *aliased,
    )


def last_rows(back_ref, cur_ref, prow_ref, w_ref, w_out_ref):
    current = update(back_ref, cur_ref, prow_ref[...], w_ref[0], w_out_ref[0])
    return stacked(norm_channels(current.astype(F32)).astype(BF))


def last_own_kernel(back_ref, cur_ref, prow_ref, w_ref, w_out_ref, rows_ref):
    rows_ref[...] = last_rows(back_ref, cur_ref, prow_ref, w_ref, w_out_ref)


def last_peer_kernel(
    back_ref, cur_ref, prow_ref, w_ref, w_out_ref, own_hbm, pj_hbm, mine_ref, other_ref, rows_ref, pj_ref, sems
):
    step = pl.program_id(0)
    loads = [
        pltpu.make_async_copy(own_hbm, rows_ref.at[:, pl.ds(0, 512)], sems.at[0]),
        pltpu.make_async_copy(pj_hbm, pj_ref, sems.at[1]),
    ]

    @pl.when(step == 0)
    def _():
        for load in loads:
            load.start()

    lanes = pl.ds(pl.multiple_of(512 + step * BLOCK, BLOCK), BLOCK)
    rows_ref[:, lanes] = last_rows(back_ref, cur_ref, prow_ref, w_ref, w_out_ref)

    @pl.when(step == HALF_STEPS - 1)
    def _():
        for load in loads:
            load.wait()
        core = lax.axis_index("tmpl")
        pj = pj_ref[...]
        mine_ref[...] = dot_nt(pj, rows_ref[pl.ds(pl.multiple_of(core * 256, 256), 256), :]).astype(BF)
        other_ref[...] = dot_nt(pj, rows_ref[pl.ds(pl.multiple_of(256 - core * 256, 256), 256), :]).astype(BF)


def last_specs(layer):
    return [lanes_of(512)] * 2 + [full((512, 512)), layer_weight(320, layer), layer_weight(CH, layer)]


def last_own(back, current, prow, proj_weight, out_weight, layer):
    return pl.pallas_call(
        last_own_kernel,
        grid=(HALF_STEPS,),
        in_specs=last_specs(layer),
        out_specs=lanes_of(512),
        out_shape=pltpu.HBM((512, 512), BF),
        compiler_params=pltpu.CompilerParams(vmem_limit_bytes=VMEM_LIMIT),
        name="last_own",
    )(back, *in_hbm(current), *in_vmem(prow), proj_weight, out_weight)


def last_peer(back, current, prow, proj_weight, out_weight, own, pj, layer):
    return pl.pallas_call(
        last_peer_kernel,
        grid=(HALF_STEPS,),
        in_specs=last_specs(layer) + [ANYWHERE, ANYWHERE],
        out_specs=[full((CROP, 256))] * 2,
        out_shape=[jax.ShapeDtypeStruct((CROP, 256), BF)] * 2,
        scratch_shapes=[
            pltpu.VMEM((512, CROP), BF), pltpu.VMEM((CROP, CROP), BF), pltpu.SemaphoreType.DMA((2,)),
        ],
        compiler_params=pltpu.CompilerParams(vmem_limit_bytes=VMEM_LIMIT),
        name="last_peer",
    )(back, *in_hbm(current), *in_vmem(prow), proj_weight, out_weight, *in_hbm(own, pj))


def own_products_kernel(both_ref, out_ref, left_hbm, right_hbm, sems):
    copies = []
    for block in range(STEPS):
        for side, target in enumerate((left_hbm, right_hbm)):
            source = both_ref.at[:, pl.ds((2 * block + side) * BLOCK, BLOCK)]
            place = target.at[:, pl.ds(block * BLOCK, BLOCK)]
            copies.append(pltpu.make_async_copy(source, place, sems.at[2 * block + side]))
    for copy in copies:
        copy.start()
    starts = [2 * block * BLOCK for block in range(STEPS)]
    left = jnp.concatenate([both_ref[:, start : start + BLOCK] for start in starts], axis=1)
    right = jnp.concatenate([both_ref[:, start + BLOCK : start + 2 * BLOCK] for start in starts], axis=1)
    out_ref[...] = dot_nt(left, right).astype(BF)
    for copy in copies:
        copy.wait()


def own_products(both):
    return pl.pallas_call(
        own_products_kernel,
        out_specs=[pl.BlockSpec(memory_space=pltpu.VMEM), ANYWHERE, ANYWHERE],
        out_shape=[jax.ShapeDtypeStruct((512, 512), BF), pltpu.HBM((512, CROP), BF), pltpu.HBM((512, CROP), BF)],
        scratch_shapes=[pltpu.SemaphoreType.DMA((2 * STEPS,))],
        compiler_params=pltpu.CompilerParams(vmem_limit_bytes=VMEM_LIMIT),
        cost_estimate=pl.CostEstimate(flops=2**29, bytes_accessed=4 * 2**20, transcendentals=0),
        name="own_products",
    )(both)


def peer_products_kernel(left_ref, right_ref, out_ref):
    left = jnp.concatenate([left_ref[:, 512:], left_ref[:, :512]], axis=1)
    out_ref[...] = dot_nt(left, right_ref[...]).astype(BF)


def peer_products(left, right):
    return pl.pallas_call(
        peer_products_kernel,
        out_shape=pltpu.HBM((512, 512), BF),
        compiler_params=pltpu.CompilerParams(vmem_limit_bytes=VMEM_LIMIT),
        cost_estimate=pl.CostEstimate(flops=2**29, bytes_accessed=4 * 2**20, transcendentals=0),
        name="peer_products",
    )(left, right)


def hidden_features(mine, peer):
    total = mine.astype(F32) + peer.astype(F32)
    return jnp.maximum(total * 0.5, 0.0).astype(BF)


def final_kernel(mine_ref, peer_ref, wf_ref, out_ref, tall0_ref, tall1_ref, wide_ref):
    core = lax.axis_index("tmpl")
    wf = wf_ref[...]
    for source, ref in enumerate((mine_ref, peer_ref)):
        half = core if source == 0 else 1 - core
        tall0_ref[...] = ref[:, :128].astype(F32)
        tall1_ref[...] = ref[:, 128:].astype(F32)
        for j in range(8):
            rows = jnp.concatenate(
                [tall0_ref[pl.ds(j, 128, stride=8), :], tall1_ref[pl.ds(j, 128, stride=8), :]], axis=1
            ).astype(BF)
            result = dot_nt(wf, rows)
            for a in range(4):
                wide_ref[half * 4 + a, pl.ds(j, CZ, stride=8), :] = result[a * CZ : (a + 1) * CZ]
    for a in range(8):
        out_ref[:, a * TILE : (a + 1) * TILE] = wide_ref[a].astype(BF)


def final_projection(mine, peer, wf):
    return pl.pallas_call(
        final_kernel,
        out_shape=jax.ShapeDtypeStruct((CZ * 8, CROP), BF),
        scratch_shapes=[
            pltpu.VMEM((CROP, 128), F32), pltpu.VMEM((CROP, 128), F32), pltpu.VMEM((8, CZ * 8, TILE), F32)
        ],
        compiler_params=pltpu.CompilerParams(vmem_limit_bytes=VMEM_LIMIT),
        name="final",
    )(mine, peer, wf)


def exchange(values, groups, count):
    cube = values.reshape(count, -1, values.shape[-1])
    moved = lax.all_to_all(cube, "row", 0, 0, axis_index_groups=groups, tiled=True)
    return moved.reshape(values.shape)


def on_device(pair_maps, crop_tiles, full_length, proj_weight, out_weight, final_weight):
    wf, prow, q, pj = make_tables(final_weight)
    pair = jnp.transpose(pair_maps[0], (0, 2, 1))
    cropped = crop_columns(crop_tiles, pair)
    got = lax.all_to_all(cropped, "row", 0, 0, axis_index_groups=PLANE, tiled=True)
    current, both = first_projection(crop_tiles, full_length, got, prow, q, proj_weight)
    currents = (current, current)
    weights = (prow, proj_weight, out_weight)
    for layer in range(NLAYER):
        products, left, right = own_products(exchange(both, SAME_X0, CH))
        back_own = exchange(products, SAME_X0, CH)
        right_peer = lax.ppermute(right, "row", X0_PAIRS)
        back_peer = exchange(peer_products(left, right_peer), SAME_X0, CH)
        if layer + 1 < NLAYER:
            scalars = (crop_tiles, full_length)
            own, both = middle_half(0, *scalars, back_own, currents[0], *weights, layer, None)
            peer, both = middle_half(1, *scalars, back_peer, currents[1], *weights, layer, both)
            currents = (own, peer)
    rows = last_own(back_own, currents[0], *weights, NLAYER - 1)
    mine, other = last_peer(back_peer, currents[1], *weights, rows, pj, NLAYER - 1)
    hidden = hidden_features(mine, lax.ppermute(other, "tmpl", CORES))
    moved = exchange(hidden, BY_Z, 128)
    result = final_projection(moved, lax.ppermute(moved, "tmpl", CORES), wf)
    return result.reshape(CZ, 8, CROP)


def solution(mesh):
    placed = (P("tmpl", "row", None, None), P("tmpl", None), P(), P(), P(), P())
    return jax.shard_map(
        on_device, mesh=mesh, in_specs=placed, out_specs=P(None, "row", None), check_vma=False
    )
```

```python
import functools

import jax
import jax.numpy as jnp
from jax import lax
from jax.experimental import pallas as pl
from jax.experimental.pallas import tpu as pltpu
from jax.sharding import PartitionSpec as P

CH = 64
CZ = 128
CROP = 1024
TILE = 128
NLAYER = 2
FULL = 2048
ROWS = 8
EPSILON = 1e-05
BF = jnp.bfloat16
F32 = jnp.float32

PLANE = [[s * 8 + z for s in range(16)] for z in range(8)]
SAME_X0 = [
    [(x1 * 2 + x0) * 32 + y * 8 + z for x1 in range(2) for y in range(4) for z in range(8)]
    for x0 in range(2)
]
BY_Z = [[s * 8 + z for z in range(8) for s in range(16)]]
X0_PAIRS = [(r, r ^ 32) for r in range(128)]
CORES = [(0, 1), (1, 0)]
VMEM_LIMIT = 24 * 1024 * 1024


def in_vmem(*arrays):
    return [pltpu.with_memory_space_constraint(array, pltpu.VMEM) for array in arrays]


def in_hbm(*arrays):
    return [pltpu.with_memory_space_constraint(array, pltpu.HBM) for array in arrays]


def iota(shape, dim):
    return lax.broadcasted_iota(jnp.int32, shape, dim)


def onehot(mask):
    return jnp.where(mask, 1.0, 0.0).astype(BF)


def dot(a, b):
    return jnp.dot(a, b, preferred_element_type=F32)


def dot_nt(a, b):
    return lax.dot_general(a, b, (((1,), (1,)), ((), ())), preferred_element_type=F32)


def dot_tn(a, b):
    return lax.dot_general(a, b, (((0,), (0,)), ((), ())), preferred_element_type=F32)


def lane_token(lane):
    x0 = (lax.axis_index("row") // 32) % 2
    return (
        (lane % 8) * 128
        + ((lane // 8) % 8) * 16
        + ((lane // 256) % 2) * 8
        + ((lane // 512) ^ x0) * 4
        + ((lane // 64) % 4)
    )


def tables_kernel(final_ref, wf_ref, prow_ref, q_ref, pj_ref):
    down = onehot(iota((512, CZ), 0) % CZ == iota((512, CZ), 1))
    across = onehot(iota((CH, 256), 0) == iota((CH, 256), 1) % CH)
    tall = dot_nt(down, final_ref[...]).astype(BF)
    block = iota((512, 256), 0) // CZ == iota((512, 256), 1) // CH
    wf_ref[...] = jnp.where(block, dot(tall, across), 0.0).astype(BF)
    r0, c0 = iota((512, 512), 0), iota((512, 512), 1)
    prow_ref[...] = onehot((r0 // 8 == c0 % CH) & (r0 % 8 == c0 // CH))
    r1, c1 = iota((CROP, CROP), 0), iota((CROP, CROP), 1)
    token = lane_token(c1)
    q_ref[...] = onehot(r1 == token)
    dest = r1 // 8
    pj_ref[...] = onehot(((dest % 16) * 8 + dest // 16) * 8 + r1 % 8 == token)


def make_tables(final_weight):
    return pl.pallas_call(
        tables_kernel,
        out_shape=[
            pltpu.VMEM((512, 256), BF), pltpu.VMEM((512, 512), BF),
            pltpu.HBM((CROP, CROP), BF), pltpu.HBM((CROP, CROP), BF),
        ],
        compiler_params=pltpu.CompilerParams(vmem_limit_bytes=40 * 1024 * 1024),
        cost_estimate=pl.CostEstimate(flops=10**9, bytes_accessed=6 * 2**20, transcendentals=0),
        name="tables",
    )(final_weight)


CROP_CHUNKS = 4


def crop_kernel(crop_ref, x_hbm, o_hbm, rows_ref, in_sems, out_sems):
    size = 16 // CROP_CHUNKS
    loads, stores = [], []
    for chunk in range(CROP_CHUNKS):
        rows = pl.ds(chunk * size, size)
        for a in range(8):
            tile = pl.ds(pl.multiple_of(crop_ref[0, a] * TILE, TILE), TILE)
            load = pltpu.make_async_copy(
                x_hbm.at[rows, :, tile], rows_ref.at[rows, :, pl.ds(a * TILE, TILE)], in_sems.at[chunk * 8 + a]
            )
            load.start()
            loads.append(load)
    for chunk in range(CROP_CHUNKS):
        rows = pl.ds(chunk * size, size)
        for load in loads[chunk * 8 : chunk * 8 + 8]:
            load.wait()
        store = pltpu.make_async_copy(rows_ref.at[rows], o_hbm.at[rows], out_sems.at[chunk])
        store.start()
        stores.append(store)
    for store in stores:
        store.wait()


def crop_columns(crop_tiles, pair):
    return pl.pallas_call(
        crop_kernel,
        grid_spec=pltpu.PrefetchScalarGridSpec(
            num_scalar_prefetch=1,
            grid=(1,),
            in_specs=[pl.BlockSpec(memory_space=pl.ANY)],
            out_specs=pl.BlockSpec(memory_space=pl.ANY),
            scratch_shapes=[
                pltpu.VMEM((16, CH, CROP), BF),
                pltpu.SemaphoreType.DMA((8 * CROP_CHUNKS,)),
                pltpu.SemaphoreType.DMA((CROP_CHUNKS,)),
            ],
        ),
        out_shape=pltpu.HBM((16, CH, CROP), BF),
        compiler_params=pltpu.CompilerParams(vmem_limit_bytes=VMEM_LIMIT),
        name="crop",
    )(crop_tiles, *in_hbm(pair))


def norm_channels(values):
    center = values - jnp.sum(values, axis=0, keepdims=True) * (1.0 / CH)
    spread = jnp.sum(center * center, axis=0, keepdims=True) * (1.0 / CH)
    return center * lax.rsqrt(spread + EPSILON)


def sigmoid(values):
    return 0.5 * jnp.tanh(0.5 * values) + 0.5


def side_by_side(values):
    return jnp.concatenate([values[a * CH : (a + 1) * CH] for a in range(ROWS)], axis=1)


def stacked(values):
    lanes = values.shape[1] // ROWS
    return jnp.concatenate([values[:, a * lanes : (a + 1) * lanes] for a in range(ROWS)], axis=0)


def pair_mask(crop_ref, length_ref, lanes, start):
    chip = lax.axis_index("row")
    inside = (chip % 8) * 16 + chip // 8
    length = length_ref[0]
    lane = iota((1, lanes), 1) + start
    position = lane_token(lane) % TILE
    for a in range(ROWS):
        position = position + jnp.where(lane % 8 == a, crop_ref[0, a] * TILE, 0)
    parts = []
    for a in range(ROWS):
        row_position = crop_ref[0, a] * TILE + inside
        parts.append(jnp.where((position < length) & (row_position < length), 1.0, 0.0))
    return jnp.concatenate(parts, axis=1)


def project(current, w, prow, mask, both_ref):
    values = dot_tn(w[:, : 4 * CH], norm_channels(current).astype(BF))
    lanes = both_ref.shape[1] // 2
    for side in range(2):
        gate = values[side * 128 : side * 128 + CH]
        value = values[side * 128 + CH : side * 128 + 2 * CH]
        factor = (sigmoid(gate) * value * mask).astype(BF)
        both_ref[:, side * lanes : (side + 1) * lanes] = dot(prow, stacked(factor)).astype(BF)


BLOCK = 512
ANYWHERE = pl.BlockSpec(memory_space=pl.ANY)
RESIDENT = pl.BlockSpec(memory_space=pltpu.VMEM)
STEPS = CROP // BLOCK
HALF_STEPS = STEPS // 2
LAST_BLOCK = 256
LAST_STEPS = 512 // LAST_BLOCK
BOTH = pltpu.HBM((512, 2 * CROP), BF)


def first_kernel(crop_ref, length_ref, got_ref, prow_ref, q_ref, w_ref, cur_ref, both_ref):
    step = pl.program_id(0)
    parts = jnp.concatenate([got_ref[crop_ref[0, a]] for a in range(ROWS)], axis=0)
    current = dot(parts, q_ref[...])
    cur_ref[...] = current.astype(BF)
    mask = pair_mask(crop_ref, length_ref, BLOCK, step * BLOCK)
    project(side_by_side(current), w_ref[0], prow_ref[...], mask, both_ref)


def full(shape):
    return pl.BlockSpec(shape, lambda step, *_: (0,) * len(shape), pipeline_mode=pl.Buffered(1))


def lanes_of(rows, lanes=BLOCK, offset=0):
    return pl.BlockSpec((rows, lanes), lambda step, *_: (0, step + offset))


def layer_weight(columns, layer):
    return pl.BlockSpec((1, CH, columns), lambda step, *_: (layer, 0, 0), pipeline_mode=pl.Buffered(1))


def first_projection(crop_tiles, full_length, got, prow, q, proj_weight):
    return pl.pallas_call(
        first_kernel,
        grid_spec=pltpu.PrefetchScalarGridSpec(
            num_scalar_prefetch=2,
            grid=(STEPS,),
            in_specs=[RESIDENT, RESIDENT, lanes_of(CROP), layer_weight(320, 0)],
            out_specs=[lanes_of(512), lanes_of(512, 2 * BLOCK)],
        ),
        out_shape=[pltpu.HBM((512, CROP), BF), BOTH],
        compiler_params=pltpu.CompilerParams(vmem_limit_bytes=VMEM_LIMIT),
        name="first",
    )(crop_tiles, full_length, *in_vmem(got, prow), *in_hbm(q), proj_weight)


def update(back_ref, cur_ref, prow, w_proj, w_out):
    block = cur_ref.shape[1]
    current = side_by_side(cur_ref[...].astype(F32))
    gate = sigmoid(dot_tn(w_proj[:, 4 * CH :], norm_channels(current).astype(BF)))
    lanes = pl.ds(pl.multiple_of(pl.program_id(0) * block, block), block)
    products = side_by_side(dot_tn(prow, back_ref[:, lanes]))
    change = dot_tn(w_out, norm_channels(products).astype(BF))
    return (current + gate * change).astype(BF)


def middle_kernel(half, *refs):
    crop_ref, length_ref, back_ref, cur_ref, prow_ref, w_ref, w_out_ref, w_next_ref = refs[:8]
    next_ref, both_ref = refs[-2:]
    current = update(back_ref, cur_ref, prow_ref[...], w_ref[0], w_out_ref[0])
    next_ref[...] = stacked(current)
    mask = pair_mask(crop_ref, length_ref, BLOCK, half * 512 + pl.program_id(0) * BLOCK)
    project(current.astype(F32), w_next_ref[0], prow_ref[...], mask, both_ref)


def middle_half(half, crop_tiles, full_length, back, current, prow, proj_weight, out_weight, layer, both):
    offset = half * HALF_STEPS
    aliased = [] if both is None else [both]
    return pl.pallas_call(
        functools.partial(middle_kernel, half),
        grid_spec=pltpu.PrefetchScalarGridSpec(
            num_scalar_prefetch=2,
            grid=(HALF_STEPS,),
            in_specs=[
                RESIDENT, lanes_of(512, offset=offset), RESIDENT,
                layer_weight(320, layer), layer_weight(CH, layer), layer_weight(320, layer + 1),
            ]
            + [ANYWHERE] * len(aliased),
            out_specs=[lanes_of(512), lanes_of(512, 2 * BLOCK, offset)],
        ),
        out_shape=[pltpu.HBM((512, 512), BF), BOTH],
        input_output_aliases={8: 1} if aliased else {},
        compiler_params=pltpu.CompilerParams(vmem_limit_bytes=VMEM_LIMIT),
        name="middle" + str(half),
    )(
        crop_tiles, full_length, *in_vmem(back), *in_hbm(current), *in_vmem(prow), proj_weight, out_weight, proj_weight,
        *aliased,
    )


def last_rows(back_ref, cur_ref, prow_ref, w_ref, w_out_ref):
    current = update(back_ref, cur_ref, prow_ref[...], w_ref[0], w_out_ref[0])
    return stacked(norm_channels(current.astype(F32)).astype(BF))


def last_own_kernel(back_ref, cur_ref, prow_ref, w_ref, w_out_ref, rows_ref):
    rows_ref[...] = last_rows(back_ref, cur_ref, prow_ref, w_ref, w_out_ref)


def last_peer_kernel(
    back_ref, cur_ref, prow_ref, w_ref, w_out_ref, own_hbm, pj_hbm, mine_ref, other_ref, rows_ref, pj_ref, sems
):
    step = pl.program_id(0)
    loads = [
        pltpu.make_async_copy(own_hbm, rows_ref.at[:, pl.ds(0, 512)], sems.at[0]),
        pltpu.make_async_copy(pj_hbm, pj_ref, sems.at[1]),
    ]

    @pl.when(step == 0)
    def _():
        for load in loads:
            load.start()

    lanes = pl.ds(pl.multiple_of(512 + step * LAST_BLOCK, LAST_BLOCK), LAST_BLOCK)
    rows_ref[:, lanes] = last_rows(back_ref, cur_ref, prow_ref, w_ref, w_out_ref)

    @pl.when(step == LAST_STEPS - 1)
    def _():
        for load in loads:
            load.wait()
        core = lax.axis_index("tmpl")
        pj = pj_ref[...]
        mine_ref[...] = dot_nt(pj, rows_ref[pl.ds(pl.multiple_of(core * 256, 256), 256), :]).astype(BF)
        other_ref[...] = dot_nt(pj, rows_ref[pl.ds(pl.multiple_of(256 - core * 256, 256), 256), :]).astype(BF)


def last_specs(layer):
    return [RESIDENT, lanes_of(512, LAST_BLOCK), RESIDENT, layer_weight(320, layer), layer_weight(CH, layer)]


def last_own(back, current, prow, proj_weight, out_weight, layer):
    return pl.pallas_call(
        last_own_kernel,
        grid=(LAST_STEPS,),
        in_specs=last_specs(layer),
        out_specs=lanes_of(512, LAST_BLOCK),
        out_shape=pltpu.HBM((512, 512), BF),
        compiler_params=pltpu.CompilerParams(vmem_limit_bytes=VMEM_LIMIT),
        name="last_own",
    )(*in_vmem(back), *in_hbm(current), *in_vmem(prow), proj_weight, out_weight)


def last_peer(back, current, prow, proj_weight, out_weight, own, pj, layer):
    return pl.pallas_call(
        last_peer_kernel,
        grid=(LAST_STEPS,),
        in_specs=last_specs(layer) + [ANYWHERE, ANYWHERE],
        out_specs=[full((CROP, 256))] * 2,
        out_shape=[jax.ShapeDtypeStruct((CROP, 256), BF)] * 2,
        scratch_shapes=[
            pltpu.VMEM((512, CROP), BF), pltpu.VMEM((CROP, CROP), BF), pltpu.SemaphoreType.DMA((2,)),
        ],
        compiler_params=pltpu.CompilerParams(vmem_limit_bytes=VMEM_LIMIT),
        name="last_peer",
    )(*in_vmem(back), *in_hbm(current), *in_vmem(prow), proj_weight, out_weight, *in_hbm(own, pj))


def own_products_kernel(both_ref, out_ref, left_hbm, right_hbm, sems):
    copies = []
    for block in range(STEPS):
        for side, target in enumerate((left_hbm, right_hbm)):
            source = both_ref.at[:, pl.ds((2 * block + side) * BLOCK, BLOCK)]
            place = target.at[:, pl.ds(block * BLOCK, BLOCK)]
            copies.append(pltpu.make_async_copy(source, place, sems.at[2 * block + side]))
    for copy in copies:
        copy.start()
    starts = [2 * block * BLOCK for block in range(STEPS)]
    left = jnp.concatenate([both_ref[:, start : start + BLOCK] for start in starts], axis=1)
    right = jnp.concatenate([both_ref[:, start + BLOCK : start + 2 * BLOCK] for start in starts], axis=1)
    out_ref[...] = dot_nt(left, right).astype(BF)
    for copy in copies:
        copy.wait()


def own_products(both):
    return pl.pallas_call(
        own_products_kernel,
        out_specs=[pl.BlockSpec(memory_space=pltpu.VMEM), ANYWHERE, ANYWHERE],
        out_shape=[jax.ShapeDtypeStruct((512, 512), BF), pltpu.HBM((512, CROP), BF), pltpu.HBM((512, CROP), BF)],
        scratch_shapes=[pltpu.SemaphoreType.DMA((2 * STEPS,))],
        compiler_params=pltpu.CompilerParams(vmem_limit_bytes=VMEM_LIMIT),
        cost_estimate=pl.CostEstimate(flops=2**29, bytes_accessed=4 * 2**20, transcendentals=0),
        name="own_products",
    )(both)


def peer_products_kernel(left_ref, right_ref, out_ref):
    left = jnp.concatenate([left_ref[:, 512:], left_ref[:, :512]], axis=1)
    out_ref[...] = dot_nt(left, right_ref[...]).astype(BF)


def peer_products(left, right):
    return pl.pallas_call(
        peer_products_kernel,
        out_shape=pltpu.HBM((512, 512), BF),
        compiler_params=pltpu.CompilerParams(vmem_limit_bytes=VMEM_LIMIT),
        cost_estimate=pl.CostEstimate(flops=2**29, bytes_accessed=4 * 2**20, transcendentals=0),
        name="peer_products",
    )(left, right)


def hidden_features(mine, peer):
    total = mine.astype(F32) + peer.astype(F32)
    return jnp.maximum(total * 0.5, 0.0).astype(BF)


def final_kernel(mine_ref, peer_ref, wf_ref, out_ref, tall0_ref, tall1_ref, wide_ref):
    core = lax.axis_index("tmpl")
    wf = wf_ref[...]
    for source, ref in enumerate((mine_ref, peer_ref)):
        half = core if source == 0 else 1 - core
        tall0_ref[...] = ref[:, :128].astype(F32)
        tall1_ref[...] = ref[:, 128:].astype(F32)
        for j in range(8):
            rows = jnp.concatenate(
                [tall0_ref[pl.ds(j, 128, stride=8), :], tall1_ref[pl.ds(j, 128, stride=8), :]], axis=1
            ).astype(BF)
            result = dot_nt(wf, rows)
            for a in range(4):
                wide_ref[half * 4 + a, pl.ds(j, CZ, stride=8), :] = result[a * CZ : (a + 1) * CZ]
    for a in range(8):
        out_ref[:, a * TILE : (a + 1) * TILE] = wide_ref[a].astype(BF)


def final_projection(mine, peer, wf):
    return pl.pallas_call(
        final_kernel,
        out_shape=jax.ShapeDtypeStruct((CZ * 8, CROP), BF),
        scratch_shapes=[
            pltpu.VMEM((CROP, 128), F32), pltpu.VMEM((CROP, 128), F32), pltpu.VMEM((8, CZ * 8, TILE), F32)
        ],
        compiler_params=pltpu.CompilerParams(vmem_limit_bytes=VMEM_LIMIT),
        name="final",
    )(mine, peer, wf)


def exchange(values, groups, count):
    cube = values.reshape(count, -1, values.shape[-1])
    moved = lax.all_to_all(cube, "row", 0, 0, axis_index_groups=groups, tiled=True)
    return moved.reshape(values.shape)


def on_device(pair_maps, crop_tiles, full_length, proj_weight, out_weight, final_weight):
    wf, prow, q, pj = make_tables(final_weight)
    pair = jnp.transpose(pair_maps[0], (0, 2, 1))
    cropped = crop_columns(crop_tiles, pair)
    got = lax.all_to_all(cropped, "row", 0, 0, axis_index_groups=PLANE, tiled=True)
    current, both = first_projection(crop_tiles, full_length, got, prow, q, proj_weight)
    currents = (current, current)
    weights = (prow, proj_weight, out_weight)
    for layer in range(NLAYER):
        products, left, right = own_products(exchange(both, SAME_X0, CH))
        back_own = exchange(products, SAME_X0, CH)
        right_peer = lax.ppermute(right, "row", X0_PAIRS)
        back_peer = exchange(peer_products(left, right_peer), SAME_X0, CH)
        if layer + 1 < NLAYER:
            scalars = (crop_tiles, full_length)
            own, both = middle_half(0, *scalars, back_own, currents[0], *weights, layer, None)
            peer, both = middle_half(1, *scalars, back_peer, currents[1], *weights, layer, both)
            currents = (own, peer)
    rows = last_own(back_own, currents[0], *weights, NLAYER - 1)
    mine, other = last_peer(back_peer, currents[1], *weights, rows, pj, NLAYER - 1)
    hidden = hidden_features(mine, lax.ppermute(other, "tmpl", CORES))
    moved = exchange(hidden, BY_Z, 128)
    result = final_projection(moved, lax.ppermute(moved, "tmpl", CORES), wf)
    return result.reshape(CZ, 8, CROP)


def solution(mesh):
    placed = (P("tmpl", "row", None, None), P("tmpl", None), P(), P(), P(), P())
    return jax.shard_map(
        on_device, mesh=mesh, in_specs=placed, out_specs=P(None, "row", None), check_vma=False
    )
```

```python
import functools

import jax
import jax.numpy as jnp
from jax import lax
from jax.experimental import pallas as pl
from jax.experimental.pallas import tpu as pltpu
from jax.sharding import PartitionSpec as P

CH = 64
CZ = 128
CROP = 1024
TILE = 128
NLAYER = 2
FULL = 2048
ROWS = 8
EPSILON = 1e-05
BF = jnp.bfloat16
F32 = jnp.float32

PLANE = [[s * 8 + z for s in range(16)] for z in range(8)]
BOTH_AXES = ("tmpl", "row")
SAME_PART = [
    [(x1 * 2 + x0) * 32 + y * 8 + z for x1 in range(2) for y in range(4) for z in range(8)]
    for x0 in range(2)
] + [
    [128 + x * 32 + (y1 * 2 + y0) * 8 + z for x in range(4) for y1 in range(2) for z in range(8)]
    for y0 in range(2)
]
OTHER_PART = [(r, r ^ 32) for r in range(128)] + [(128 + r, 128 + (r ^ 8)) for r in range(128)]
BY_Z = [[s * 8 + z for z in range(8) for s in range(16)]]
CORES = [(0, 1), (1, 0)]
VMEM_LIMIT = 24 * 1024 * 1024


def in_vmem(*arrays):
    return [pltpu.with_memory_space_constraint(array, pltpu.VMEM) for array in arrays]


def in_hbm(*arrays):
    return [pltpu.with_memory_space_constraint(array, pltpu.HBM) for array in arrays]


def iota(shape, dim):
    return lax.broadcasted_iota(jnp.int32, shape, dim)


def onehot(mask):
    return jnp.where(mask, 1.0, 0.0).astype(BF)


def dot(a, b):
    return jnp.dot(a, b, preferred_element_type=F32)


def dot_nt(a, b):
    return lax.dot_general(a, b, (((1,), (1,)), ((), ())), preferred_element_type=F32)


def dot_tn(a, b):
    return lax.dot_general(a, b, (((0,), (0,)), ((), ())), preferred_element_type=F32)


def lane_token(lane):
    core, chip = lax.axis_index("tmpl"), lax.axis_index("row")
    part = jnp.where(core == 0, (chip // 32) % 2, (chip // 8) % 2)
    part = (lane // 512) ^ part
    group = (lane // 64) % 8
    by_x0 = (group // 4) * 8 + part * 4 + group % 4
    by_y0 = (group // 2) * 4 + (group % 2) * 2 + part
    return (lane % 8) * 128 + ((lane // 8) % 8) * 16 + jnp.where(core == 0, by_x0, by_y0)


def tables_kernel(final_ref, wf_ref, prow_ref, q_ref, pj_ref):
    down = onehot(iota((512, CZ), 0) % CZ == iota((512, CZ), 1))
    across = onehot(iota((CH, 256), 0) == iota((CH, 256), 1) % CH)
    tall = dot_nt(down, final_ref[...]).astype(BF)
    block = iota((512, 256), 0) // CZ == iota((512, 256), 1) // CH
    wf_ref[...] = jnp.where(block, dot(tall, across), 0.0).astype(BF)
    r0, c0 = iota((512, 512), 0), iota((512, 512), 1)
    prow_ref[...] = onehot((r0 // 8 == c0 % CH) & (r0 % 8 == c0 // CH))
    r1, c1 = iota((CROP, CROP), 0), iota((CROP, CROP), 1)
    token = lane_token(c1)
    q_ref[...] = onehot(r1 == token)
    dest = r1 // 8
    pj_ref[...] = onehot(((dest % 16) * 8 + dest // 16) * 8 + r1 % 8 == token)


def make_tables(final_weight):
    return pl.pallas_call(
        tables_kernel,
        out_shape=[
            pltpu.VMEM((512, 256), BF), pltpu.VMEM((512, 512), BF),
            pltpu.HBM((CROP, CROP), BF), pltpu.HBM((CROP, CROP), BF),
        ],
        compiler_params=pltpu.CompilerParams(vmem_limit_bytes=40 * 1024 * 1024),
        cost_estimate=pl.CostEstimate(flops=10**9, bytes_accessed=6 * 2**20, transcendentals=0),
        name="tables",
    )(final_weight)


CROP_CHUNKS = 4


def crop_kernel(crop_ref, x_hbm, o_hbm, rows_ref, in_sems, out_sems):
    size = 16 // CROP_CHUNKS
    loads, stores = [], []
    for chunk in range(CROP_CHUNKS):
        rows = pl.ds(chunk * size, size)
        for a in range(8):
            tile = pl.ds(pl.multiple_of(crop_ref[0, a] * TILE, TILE), TILE)
            load = pltpu.make_async_copy(
                x_hbm.at[rows, :, tile], rows_ref.at[rows, :, pl.ds(a * TILE, TILE)], in_sems.at[chunk * 8 + a]
            )
            load.start()
            loads.append(load)
    for chunk in range(CROP_CHUNKS):
        rows = pl.ds(chunk * size, size)
        for load in loads[chunk * 8 : chunk * 8 + 8]:
            load.wait()
        store = pltpu.make_async_copy(rows_ref.at[rows], o_hbm.at[rows], out_sems.at[chunk])
        store.start()
        stores.append(store)
    for store in stores:
        store.wait()


def crop_columns(crop_tiles, pair):
    return pl.pallas_call(
        crop_kernel,
        grid_spec=pltpu.PrefetchScalarGridSpec(
            num_scalar_prefetch=1,
            grid=(1,),
            in_specs=[pl.BlockSpec(memory_space=pl.ANY)],
            out_specs=pl.BlockSpec(memory_space=pl.ANY),
            scratch_shapes=[
                pltpu.VMEM((16, CH, CROP), BF),
                pltpu.SemaphoreType.DMA((8 * CROP_CHUNKS,)),
                pltpu.SemaphoreType.DMA((CROP_CHUNKS,)),
            ],
        ),
        out_shape=pltpu.HBM((16, CH, CROP), BF),
        compiler_params=pltpu.CompilerParams(vmem_limit_bytes=VMEM_LIMIT),
        name="crop",
    )(crop_tiles, *in_hbm(pair))


def norm_channels(values):
    center = values - jnp.sum(values, axis=0, keepdims=True) * (1.0 / CH)
    spread = jnp.sum(center * center, axis=0, keepdims=True) * (1.0 / CH)
    return center * lax.rsqrt(spread + EPSILON)


def sigmoid(values):
    return 0.5 * jnp.tanh(0.5 * values) + 0.5


def side_by_side(values):
    return jnp.concatenate([values[a * CH : (a + 1) * CH] for a in range(ROWS)], axis=1)


def stacked(values):
    lanes = values.shape[1] // ROWS
    return jnp.concatenate([values[:, a * lanes : (a + 1) * lanes] for a in range(ROWS)], axis=0)


def pair_mask(crop_ref, length_ref, lanes, start):
    chip = lax.axis_index("row")
    inside = (chip % 8) * 16 + chip // 8
    length = length_ref[0]
    lane = iota((1, lanes), 1) + start
    position = lane_token(lane) % TILE
    for a in range(ROWS):
        position = position + jnp.where(lane % 8 == a, crop_ref[0, a] * TILE, 0)
    parts = []
    for a in range(ROWS):
        row_position = crop_ref[0, a] * TILE + inside
        parts.append(jnp.where((position < length) & (row_position < length), 1.0, 0.0))
    return jnp.concatenate(parts, axis=1)


def project(current, w, prow, mask, both_ref):
    values = dot_tn(w[:, : 4 * CH], norm_channels(current).astype(BF))
    lanes = both_ref.shape[1] // 2
    for side in range(2):
        gate = values[side * 128 : side * 128 + CH]
        value = values[side * 128 + CH : side * 128 + 2 * CH]
        factor = (sigmoid(gate) * value * mask).astype(BF)
        both_ref[:, side * lanes : (side + 1) * lanes] = dot(prow, stacked(factor)).astype(BF)


BLOCK = 512
ANYWHERE = pl.BlockSpec(memory_space=pl.ANY)
RESIDENT = pl.BlockSpec(memory_space=pltpu.VMEM)
STEPS = CROP // BLOCK
HALF_STEPS = STEPS // 2
LAST_BLOCK = 256
LAST_STEPS = 512 // LAST_BLOCK
BOTH = pltpu.HBM((512, 2 * CROP), BF)


def first_kernel(crop_ref, length_ref, got_ref, prow_ref, q_ref, w_ref, cur_ref, both_ref):
    step = pl.program_id(0)
    parts = jnp.concatenate([got_ref[crop_ref[0, a]] for a in range(ROWS)], axis=0)
    current = dot(parts, q_ref[...])
    cur_ref[...] = current.astype(BF)
    mask = pair_mask(crop_ref, length_ref, BLOCK, step * BLOCK)
    project(side_by_side(current), w_ref[0], prow_ref[...], mask, both_ref)


def full(shape):
    return pl.BlockSpec(shape, lambda step, *_: (0,) * len(shape), pipeline_mode=pl.Buffered(1))


def lanes_of(rows, lanes=BLOCK, offset=0):
    return pl.BlockSpec((rows, lanes), lambda step, *_: (0, step + offset))


def layer_weight(columns, layer):
    return pl.BlockSpec((1, CH, columns), lambda step, *_: (layer, 0, 0), pipeline_mode=pl.Buffered(1))


def first_projection(crop_tiles, full_length, got, prow, q, proj_weight):
    return pl.pallas_call(
        first_kernel,
        grid_spec=pltpu.PrefetchScalarGridSpec(
            num_scalar_prefetch=2,
            grid=(STEPS,),
            in_specs=[RESIDENT, RESIDENT, lanes_of(CROP), layer_weight(320, 0)],
            out_specs=[lanes_of(512), lanes_of(512, 2 * BLOCK)],
        ),
        out_shape=[pltpu.HBM((512, CROP), BF), BOTH],
        compiler_params=pltpu.CompilerParams(vmem_limit_bytes=VMEM_LIMIT),
        name="first",
    )(crop_tiles, full_length, *in_vmem(got, prow), *in_hbm(q), proj_weight)


def update(back_ref, cur_ref, prow, w_proj, w_out):
    block = cur_ref.shape[1]
    current = side_by_side(cur_ref[...].astype(F32))
    gate = sigmoid(dot_tn(w_proj[:, 4 * CH :], norm_channels(current).astype(BF)))
    lanes = pl.ds(pl.multiple_of(pl.program_id(0) * block, block), block)
    products = side_by_side(dot_tn(prow, back_ref[:, lanes]))
    change = dot_tn(w_out, norm_channels(products).astype(BF))
    return (current + gate * change).astype(BF)


def middle_kernel(half, *refs):
    crop_ref, length_ref, back_ref, cur_ref, prow_ref, w_ref, w_out_ref, w_next_ref = refs[:8]
    next_ref, both_ref = refs[-2:]
    current = update(back_ref, cur_ref, prow_ref[...], w_ref[0], w_out_ref[0])
    next_ref[...] = stacked(current)
    mask = pair_mask(crop_ref, length_ref, BLOCK, half * 512 + pl.program_id(0) * BLOCK)
    project(current.astype(F32), w_next_ref[0], prow_ref[...], mask, both_ref)


def middle_half(half, crop_tiles, full_length, back, current, prow, proj_weight, out_weight, layer, both):
    offset = half * HALF_STEPS
    aliased = [] if both is None else [both]
    return pl.pallas_call(
        functools.partial(middle_kernel, half),
        grid_spec=pltpu.PrefetchScalarGridSpec(
            num_scalar_prefetch=2,
            grid=(HALF_STEPS,),
            in_specs=[
                RESIDENT, lanes_of(512, offset=offset), RESIDENT,
                layer_weight(320, layer), layer_weight(CH, layer), layer_weight(320, layer + 1),
            ]
            + [ANYWHERE] * len(aliased),
            out_specs=[lanes_of(512), lanes_of(512, 2 * BLOCK, offset)],
        ),
        out_shape=[pltpu.HBM((512, 512), BF), BOTH],
        input_output_aliases={8: 1} if aliased else {},
        compiler_params=pltpu.CompilerParams(vmem_limit_bytes=VMEM_LIMIT),
        name="middle" + str(half),
    )(
        crop_tiles, full_length, *in_vmem(back), *in_hbm(current), *in_vmem(prow), proj_weight, out_weight, proj_weight,
        *aliased,
    )


def last_rows(back_ref, cur_ref, prow_ref, w_ref, w_out_ref):
    current = update(back_ref, cur_ref, prow_ref[...], w_ref[0], w_out_ref[0])
    return stacked(norm_channels(current.astype(F32)).astype(BF))


def last_own_kernel(back_ref, cur_ref, prow_ref, w_ref, w_out_ref, rows_ref):
    rows_ref[...] = last_rows(back_ref, cur_ref, prow_ref, w_ref, w_out_ref)


def last_peer_kernel(
    back_ref, cur_ref, prow_ref, w_ref, w_out_ref, own_hbm, pj_hbm, mine_ref, other_ref, rows_ref, pj_ref, sems
):
    step = pl.program_id(0)
    loads = [
        pltpu.make_async_copy(own_hbm, rows_ref.at[:, pl.ds(0, 512)], sems.at[0]),
        pltpu.make_async_copy(pj_hbm, pj_ref, sems.at[1]),
    ]

    @pl.when(step == 0)
    def _():
        for load in loads:
            load.start()

    lanes = pl.ds(pl.multiple_of(512 + step * LAST_BLOCK, LAST_BLOCK), LAST_BLOCK)
    rows_ref[:, lanes] = last_rows(back_ref, cur_ref, prow_ref, w_ref, w_out_ref)

    @pl.when(step == LAST_STEPS - 1)
    def _():
        for load in loads:
            load.wait()
        core = lax.axis_index("tmpl")
        pj = pj_ref[...]
        mine_ref[...] = dot_nt(pj, rows_ref[pl.ds(pl.multiple_of(core * 256, 256), 256), :]).astype(BF)
        other_ref[...] = dot_nt(pj, rows_ref[pl.ds(pl.multiple_of(256 - core * 256, 256), 256), :]).astype(BF)


def last_specs(layer):
    return [RESIDENT, lanes_of(512, LAST_BLOCK), RESIDENT, layer_weight(320, layer), layer_weight(CH, layer)]


def last_own(back, current, prow, proj_weight, out_weight, layer):
    return pl.pallas_call(
        last_own_kernel,
        grid=(LAST_STEPS,),
        in_specs=last_specs(layer),
        out_specs=lanes_of(512, LAST_BLOCK),
        out_shape=pltpu.HBM((512, 512), BF),
        compiler_params=pltpu.CompilerParams(vmem_limit_bytes=VMEM_LIMIT),
        name="last_own",
    )(*in_vmem(back), *in_hbm(current), *in_vmem(prow), proj_weight, out_weight)


def last_peer(back, current, prow, proj_weight, out_weight, own, pj, layer):
    return pl.pallas_call(
        last_peer_kernel,
        grid=(LAST_STEPS,),
        in_specs=last_specs(layer) + [ANYWHERE, ANYWHERE],
        out_specs=[full((CROP, 256))] * 2,
        out_shape=[jax.ShapeDtypeStruct((CROP, 256), BF)] * 2,
        scratch_shapes=[
            pltpu.VMEM((512, CROP), BF), pltpu.VMEM((CROP, CROP), BF), pltpu.SemaphoreType.DMA((2,)),
        ],
        compiler_params=pltpu.CompilerParams(vmem_limit_bytes=VMEM_LIMIT),
        name="last_peer",
    )(*in_vmem(back), *in_hbm(current), *in_vmem(prow), proj_weight, out_weight, *in_hbm(own, pj))


def own_products_kernel(both_ref, out_ref, left_hbm, right_hbm, sems):
    copies = []
    for block in range(STEPS):
        for side, target in enumerate((left_hbm, right_hbm)):
            source = both_ref.at[:, pl.ds((2 * block + side) * BLOCK, BLOCK)]
            place = target.at[:, pl.ds(block * BLOCK, BLOCK)]
            copies.append(pltpu.make_async_copy(source, place, sems.at[2 * block + side]))
    for copy in copies:
        copy.start()
    starts = [2 * block * BLOCK for block in range(STEPS)]
    left = jnp.concatenate([both_ref[:, start : start + BLOCK] for start in starts], axis=1)
    right = jnp.concatenate([both_ref[:, start + BLOCK : start + 2 * BLOCK] for start in starts], axis=1)
    out_ref[...] = dot_nt(left, right).astype(BF)
    for copy in copies:
        copy.wait()


def own_products(both):
    return pl.pallas_call(
        own_products_kernel,
        out_specs=[pl.BlockSpec(memory_space=pltpu.VMEM), ANYWHERE, ANYWHERE],
        out_shape=[jax.ShapeDtypeStruct((512, 512), BF), pltpu.HBM((512, CROP), BF), pltpu.HBM((512, CROP), BF)],
        scratch_shapes=[pltpu.SemaphoreType.DMA((2 * STEPS,))],
        compiler_params=pltpu.CompilerParams(vmem_limit_bytes=VMEM_LIMIT),
        cost_estimate=pl.CostEstimate(flops=2**29, bytes_accessed=4 * 2**20, transcendentals=0),
        name="own_products",
    )(both)


def peer_products_kernel(left_ref, right_ref, out_ref):
    left = jnp.concatenate([left_ref[:, 512:], left_ref[:, :512]], axis=1)
    out_ref[...] = dot_nt(left, right_ref[...]).astype(BF)


def peer_products(left, right):
    return pl.pallas_call(
        peer_products_kernel,
        out_shape=pltpu.HBM((512, 512), BF),
        compiler_params=pltpu.CompilerParams(vmem_limit_bytes=VMEM_LIMIT),
        cost_estimate=pl.CostEstimate(flops=2**29, bytes_accessed=4 * 2**20, transcendentals=0),
        name="peer_products",
    )(left, right)


def hidden_features(mine, peer):
    total = mine.astype(F32) + peer.astype(F32)
    return jnp.maximum(total * 0.5, 0.0).astype(BF)


def final_kernel(mine_ref, peer_ref, wf_ref, out_ref, tall0_ref, tall1_ref, wide_ref):
    core = lax.axis_index("tmpl")
    wf = wf_ref[...]
    for source, ref in enumerate((mine_ref, peer_ref)):
        half = core if source == 0 else 1 - core
        tall0_ref[...] = ref[:, :128].astype(F32)
        tall1_ref[...] = ref[:, 128:].astype(F32)
        for j in range(8):
            rows = jnp.concatenate(
                [tall0_ref[pl.ds(j, 128, stride=8), :], tall1_ref[pl.ds(j, 128, stride=8), :]], axis=1
            ).astype(BF)
            result = dot_nt(wf, rows)
            for a in range(4):
                wide_ref[half * 4 + a, pl.ds(j, CZ, stride=8), :] = result[a * CZ : (a + 1) * CZ]
    for a in range(8):
        out_ref[:, a * TILE : (a + 1) * TILE] = wide_ref[a].astype(BF)


def final_projection(mine, peer, wf):
    return pl.pallas_call(
        final_kernel,
        out_shape=jax.ShapeDtypeStruct((CZ * 8, CROP), BF),
        scratch_shapes=[
            pltpu.VMEM((CROP, 128), F32), pltpu.VMEM((CROP, 128), F32), pltpu.VMEM((8, CZ * 8, TILE), F32)
        ],
        compiler_params=pltpu.CompilerParams(vmem_limit_bytes=VMEM_LIMIT),
        name="final",
    )(mine, peer, wf)


def exchange(values, axes, groups, count):
    cube = values.reshape(count, -1, values.shape[-1])
    moved = lax.all_to_all(cube, axes, 0, 0, axis_index_groups=groups, tiled=True)
    return moved.reshape(values.shape)


def on_device(pair_maps, crop_tiles, full_length, proj_weight, out_weight, final_weight):
    wf, prow, q, pj = make_tables(final_weight)
    pair = jnp.transpose(pair_maps[0], (0, 2, 1))
    cropped = crop_columns(crop_tiles, pair)
    got = lax.all_to_all(cropped, "row", 0, 0, axis_index_groups=PLANE, tiled=True)
    current, both = first_projection(crop_tiles, full_length, got, prow, q, proj_weight)
    currents = (current, current)
    weights = (prow, proj_weight, out_weight)
    for layer in range(NLAYER):
        products, left, right = own_products(exchange(both, BOTH_AXES, SAME_PART, CH))
        back_own = exchange(products, BOTH_AXES, SAME_PART, CH)
        right_peer = lax.ppermute(right, BOTH_AXES, OTHER_PART)
        back_peer = exchange(peer_products(left, right_peer), BOTH_AXES, SAME_PART, CH)
        if layer + 1 < NLAYER:
            scalars = (crop_tiles, full_length)
            own, both = middle_half(0, *scalars, back_own, currents[0], *weights, layer, None)
            peer, both = middle_half(1, *scalars, back_peer, currents[1], *weights, layer, both)
            currents = (own, peer)
    rows = last_own(back_own, currents[0], *weights, NLAYER - 1)
    mine, other = last_peer(back_peer, currents[1], *weights, rows, pj, NLAYER - 1)
    hidden = hidden_features(mine, lax.ppermute(other, "tmpl", CORES))
    moved = exchange(hidden, "row", BY_Z, 128)
    result = final_projection(moved, lax.ppermute(moved, "tmpl", CORES), wf)
    return result.reshape(CZ, 8, CROP)


def solution(mesh):
    placed = (P("tmpl", "row", None, None), P("tmpl", None), P(), P(), P(), P())
    return jax.shard_map(
        on_device, mesh=mesh, in_specs=placed, out_specs=P(None, "row", None), check_vma=False
    )
```

```python
import functools

import jax
import jax.numpy as jnp
from jax import lax
from jax.experimental import pallas as pl
from jax.experimental.pallas import tpu as pltpu
from jax.sharding import PartitionSpec as P

CH = 64
CZ = 128
CROP = 1024
TILE = 128
NLAYER = 2
FULL = 2048
ROWS = 8
EPSILON = 1e-05
BF = jnp.bfloat16
F32 = jnp.float32

PLANE = [[s * 8 + z for s in range(16)] for z in range(8)]
BOTH_AXES = ("tmpl", "row")
SAME_PART = [
    [t * 128 + s * 8 + ((7 - zi if part else zi) + 2 * t) % 8 for s in range(16) for zi in range(4)]
    for t in range(2)
    for part in range(2)
]
OTHER_PART = [
    (t * 128 + s * 8 + z, t * 128 + s * 8 + (7 + 4 * t - z) % 8) for t in range(2) for s in range(16) for z in range(8)
]
BY_Z = [[s * 8 + z for z in range(8) for s in range(16)]]
CORES = [(0, 1), (1, 0)]
VMEM_LIMIT = 24 * 1024 * 1024


def in_vmem(*arrays):
    return [pltpu.with_memory_space_constraint(array, pltpu.VMEM) for array in arrays]


def in_hbm(*arrays):
    return [pltpu.with_memory_space_constraint(array, pltpu.HBM) for array in arrays]


def iota(shape, dim):
    return lax.broadcasted_iota(jnp.int32, shape, dim)


def onehot(mask):
    return jnp.where(mask, 1.0, 0.0).astype(BF)


def dot(a, b):
    return jnp.dot(a, b, preferred_element_type=F32)


def dot_nt(a, b):
    return lax.dot_general(a, b, (((1,), (1,)), ((), ())), preferred_element_type=F32)


def dot_tn(a, b):
    return lax.dot_general(a, b, (((0,), (0,)), ((), ())), preferred_element_type=F32)


def lane_token(lane):
    core, chip = lax.axis_index("tmpl"), lax.axis_index("row")
    part = (lane // 512) ^ (((chip % 8 + 8 - 2 * core) % 8) // 4)
    place = (lane // 8) % 4
    z = (jnp.where(part == 0, place, 7 - place) + 2 * core) % 8
    return (lane % 8) * 128 + z * 16 + (lane // 32) % 16


def tables_kernel(final_ref, wf_ref, prow_ref, q_ref, pj_ref):
    down = onehot(iota((512, CZ), 0) % CZ == iota((512, CZ), 1))
    across = onehot(iota((CH, 256), 0) == iota((CH, 256), 1) % CH)
    tall = dot_nt(down, final_ref[...]).astype(BF)
    block = iota((512, 256), 0) // CZ == iota((512, 256), 1) // CH
    wf_ref[...] = jnp.where(block, dot(tall, across), 0.0).astype(BF)
    r0, c0 = iota((512, 512), 0), iota((512, 512), 1)
    prow_ref[...] = onehot((r0 // 8 == c0 % CH) & (r0 % 8 == c0 // CH))
    r1, c1 = iota((CROP, CROP), 0), iota((CROP, CROP), 1)
    token = lane_token(c1)
    q_ref[...] = onehot(r1 == token)
    dest = r1 // 8
    pj_ref[...] = onehot(((dest % 16) * 8 + dest // 16) * 8 + r1 % 8 == token)


def make_tables(final_weight):
    return pl.pallas_call(
        tables_kernel,
        out_shape=[
            pltpu.VMEM((512, 256), BF), pltpu.VMEM((512, 512), BF),
            pltpu.HBM((CROP, CROP), BF), pltpu.HBM((CROP, CROP), BF),
        ],
        compiler_params=pltpu.CompilerParams(vmem_limit_bytes=40 * 1024 * 1024),
        cost_estimate=pl.CostEstimate(flops=10**9, bytes_accessed=6 * 2**20, transcendentals=0),
        name="tables",
    )(final_weight)


CROP_CHUNKS = 4


def crop_kernel(crop_ref, x_hbm, o_hbm, rows_ref, in_sems, out_sems):
    size = 16 // CROP_CHUNKS
    loads, stores = [], []
    for chunk in range(CROP_CHUNKS):
        rows = pl.ds(chunk * size, size)
        for a in range(8):
            tile = pl.ds(pl.multiple_of(crop_ref[0, a] * TILE, TILE), TILE)
            load = pltpu.make_async_copy(
                x_hbm.at[rows, :, tile], rows_ref.at[rows, :, pl.ds(a * TILE, TILE)], in_sems.at[chunk * 8 + a]
            )
            load.start()
            loads.append(load)
    for chunk in range(CROP_CHUNKS):
        rows = pl.ds(chunk * size, size)
        for load in loads[chunk * 8 : chunk * 8 + 8]:
            load.wait()
        store = pltpu.make_async_copy(rows_ref.at[rows], o_hbm.at[rows], out_sems.at[chunk])
        store.start()
        stores.append(store)
    for store in stores:
        store.wait()


def crop_columns(crop_tiles, pair):
    return pl.pallas_call(
        crop_kernel,
        grid_spec=pltpu.PrefetchScalarGridSpec(
            num_scalar_prefetch=1,
            grid=(1,),
            in_specs=[pl.BlockSpec(memory_space=pl.ANY)],
            out_specs=pl.BlockSpec(memory_space=pl.ANY),
            scratch_shapes=[
                pltpu.VMEM((16, CH, CROP), BF),
                pltpu.SemaphoreType.DMA((8 * CROP_CHUNKS,)),
                pltpu.SemaphoreType.DMA((CROP_CHUNKS,)),
            ],
        ),
        out_shape=pltpu.HBM((16, CH, CROP), BF),
        compiler_params=pltpu.CompilerParams(vmem_limit_bytes=VMEM_LIMIT),
        name="crop",
    )(crop_tiles, *in_hbm(pair))


def norm_channels(values):
    center = values - jnp.sum(values, axis=0, keepdims=True) * (1.0 / CH)
    spread = jnp.sum(center * center, axis=0, keepdims=True) * (1.0 / CH)
    return center * lax.rsqrt(spread + EPSILON)


def sigmoid(values):
    return 0.5 * jnp.tanh(0.5 * values) + 0.5


def side_by_side(values):
    return jnp.concatenate([values[a * CH : (a + 1) * CH] for a in range(ROWS)], axis=1)


def stacked(values):
    lanes = values.shape[1] // ROWS
    return jnp.concatenate([values[:, a * lanes : (a + 1) * lanes] for a in range(ROWS)], axis=0)


def pair_mask(crop_ref, length_ref, lanes, start):
    chip = lax.axis_index("row")
    inside = (chip % 8) * 16 + chip // 8
    length = length_ref[0]
    lane = iota((1, lanes), 1) + start
    position = lane_token(lane) % TILE
    for a in range(ROWS):
        position = position + jnp.where(lane % 8 == a, crop_ref[0, a] * TILE, 0)
    parts = []
    for a in range(ROWS):
        row_position = crop_ref[0, a] * TILE + inside
        parts.append(jnp.where((position < length) & (row_position < length), 1.0, 0.0))
    return jnp.concatenate(parts, axis=1)


def project(current, w, prow, mask, both_ref):
    values = dot_tn(w[:, : 4 * CH], norm_channels(current).astype(BF))
    lanes = both_ref.shape[1] // 2
    for side in range(2):
        gate = values[side * 128 : side * 128 + CH]
        value = values[side * 128 + CH : side * 128 + 2 * CH]
        factor = (sigmoid(gate) * value * mask).astype(BF)
        both_ref[:, side * lanes : (side + 1) * lanes] = dot(prow, stacked(factor)).astype(BF)


BLOCK = 512
ANYWHERE = pl.BlockSpec(memory_space=pl.ANY)
RESIDENT = pl.BlockSpec(memory_space=pltpu.VMEM)
STEPS = CROP // BLOCK
HALF_STEPS = STEPS // 2
LAST_BLOCK = 256
LAST_STEPS = 512 // LAST_BLOCK
BOTH = pltpu.HBM((512, 2 * CROP), BF)


def first_kernel(crop_ref, length_ref, got_ref, prow_ref, q_ref, w_ref, cur_ref, both_ref):
    step = pl.program_id(0)
    parts = jnp.concatenate([got_ref[crop_ref[0, a]] for a in range(ROWS)], axis=0)
    current = dot(parts, q_ref[...])
    cur_ref[...] = current.astype(BF)
    mask = pair_mask(crop_ref, length_ref, BLOCK, step * BLOCK)
    project(side_by_side(current), w_ref[0], prow_ref[...], mask, both_ref)


def full(shape):
    return pl.BlockSpec(shape, lambda step, *_: (0,) * len(shape), pipeline_mode=pl.Buffered(1))


def lanes_of(rows, lanes=BLOCK, offset=0):
    return pl.BlockSpec((rows, lanes), lambda step, *_: (0, step + offset))


def layer_weight(columns, layer):
    return pl.BlockSpec((1, CH, columns), lambda step, *_: (layer, 0, 0), pipeline_mode=pl.Buffered(1))


def first_projection(crop_tiles, full_length, got, prow, q, proj_weight):
    return pl.pallas_call(
        first_kernel,
        grid_spec=pltpu.PrefetchScalarGridSpec(
            num_scalar_prefetch=2,
            grid=(STEPS,),
            in_specs=[RESIDENT, RESIDENT, lanes_of(CROP), layer_weight(320, 0)],
            out_specs=[lanes_of(512), lanes_of(512, 2 * BLOCK)],
        ),
        out_shape=[pltpu.HBM((512, CROP), BF), BOTH],
        compiler_params=pltpu.CompilerParams(vmem_limit_bytes=VMEM_LIMIT),
        name="first",
    )(crop_tiles, full_length, *in_vmem(got, prow), *in_hbm(q), proj_weight)


def update(back_ref, cur_ref, prow, w_proj, w_out):
    block = cur_ref.shape[1]
    current = side_by_side(cur_ref[...].astype(F32))
    gate = sigmoid(dot_tn(w_proj[:, 4 * CH :], norm_channels(current).astype(BF)))
    lanes = pl.ds(pl.multiple_of(pl.program_id(0) * block, block), block)
    products = side_by_side(dot_tn(prow, back_ref[:, lanes]))
    change = dot_tn(w_out, norm_channels(products).astype(BF))
    return (current + gate * change).astype(BF)


def middle_kernel(half, *refs):
    crop_ref, length_ref, back_ref, cur_ref, prow_ref, w_ref, w_out_ref, w_next_ref = refs[:8]
    next_ref, both_ref = refs[-2:]
    current = update(back_ref, cur_ref, prow_ref[...], w_ref[0], w_out_ref[0])
    next_ref[...] = stacked(current)
    mask = pair_mask(crop_ref, length_ref, BLOCK, half * 512 + pl.program_id(0) * BLOCK)
    project(current.astype(F32), w_next_ref[0], prow_ref[...], mask, both_ref)


def middle_half(half, crop_tiles, full_length, back, current, prow, proj_weight, out_weight, layer, both):
    offset = half * HALF_STEPS
    aliased = [] if both is None else [both]
    return pl.pallas_call(
        functools.partial(middle_kernel, half),
        grid_spec=pltpu.PrefetchScalarGridSpec(
            num_scalar_prefetch=2,
            grid=(HALF_STEPS,),
            in_specs=[
                RESIDENT, lanes_of(512, offset=offset), RESIDENT,
                layer_weight(320, layer), layer_weight(CH, layer), layer_weight(320, layer + 1),
            ]
            + [ANYWHERE] * len(aliased),
            out_specs=[lanes_of(512), lanes_of(512, 2 * BLOCK, offset)],
        ),
        out_shape=[pltpu.HBM((512, 512), BF), BOTH],
        input_output_aliases={8: 1} if aliased else {},
        compiler_params=pltpu.CompilerParams(vmem_limit_bytes=VMEM_LIMIT),
        name="middle" + str(half),
    )(
        crop_tiles, full_length, *in_vmem(back), *in_hbm(current), *in_vmem(prow), proj_weight, out_weight, proj_weight,
        *aliased,
    )


def last_rows(back_ref, cur_ref, prow_ref, w_ref, w_out_ref):
    current = update(back_ref, cur_ref, prow_ref[...], w_ref[0], w_out_ref[0])
    return stacked(norm_channels(current.astype(F32)).astype(BF))


def last_own_kernel(back_ref, cur_ref, prow_ref, w_ref, w_out_ref, rows_ref):
    rows_ref[...] = last_rows(back_ref, cur_ref, prow_ref, w_ref, w_out_ref)


def last_peer_kernel(
    back_ref, cur_ref, prow_ref, w_ref, w_out_ref, own_hbm, pj_hbm, mine_ref, other_ref, rows_ref, pj_ref, sems
):
    step = pl.program_id(0)
    loads = [
        pltpu.make_async_copy(own_hbm, rows_ref.at[:, pl.ds(0, 512)], sems.at[0]),
        pltpu.make_async_copy(pj_hbm, pj_ref, sems.at[1]),
    ]

    @pl.when(step == 0)
    def _():
        for load in loads:
            load.start()

    lanes = pl.ds(pl.multiple_of(512 + step * LAST_BLOCK, LAST_BLOCK), LAST_BLOCK)
    rows_ref[:, lanes] = last_rows(back_ref, cur_ref, prow_ref, w_ref, w_out_ref)

    @pl.when(step == LAST_STEPS - 1)
    def _():
        for load in loads:
            load.wait()
        core = lax.axis_index("tmpl")
        pj = pj_ref[...]
        mine_ref[...] = dot_nt(pj, rows_ref[pl.ds(pl.multiple_of(core * 256, 256), 256), :]).astype(BF)
        other_ref[...] = dot_nt(pj, rows_ref[pl.ds(pl.multiple_of(256 - core * 256, 256), 256), :]).astype(BF)


def last_specs(layer):
    return [RESIDENT, lanes_of(512, LAST_BLOCK), RESIDENT, layer_weight(320, layer), layer_weight(CH, layer)]


def last_own(back, current, prow, proj_weight, out_weight, layer):
    return pl.pallas_call(
        last_own_kernel,
        grid=(LAST_STEPS,),
        in_specs=last_specs(layer),
        out_specs=lanes_of(512, LAST_BLOCK),
        out_shape=pltpu.HBM((512, 512), BF),
        compiler_params=pltpu.CompilerParams(vmem_limit_bytes=VMEM_LIMIT),
        name="last_own",
    )(*in_vmem(back), *in_hbm(current), *in_vmem(prow), proj_weight, out_weight)


def last_peer(back, current, prow, proj_weight, out_weight, own, pj, layer):
    return pl.pallas_call(
        last_peer_kernel,
        grid=(LAST_STEPS,),
        in_specs=last_specs(layer) + [ANYWHERE, ANYWHERE],
        out_specs=[full((CROP, 256))] * 2,
        out_shape=[jax.ShapeDtypeStruct((CROP, 256), BF)] * 2,
        scratch_shapes=[
            pltpu.VMEM((512, CROP), BF), pltpu.VMEM((CROP, CROP), BF), pltpu.SemaphoreType.DMA((2,)),
        ],
        compiler_params=pltpu.CompilerParams(vmem_limit_bytes=VMEM_LIMIT),
        name="last_peer",
    )(*in_vmem(back), *in_hbm(current), *in_vmem(prow), proj_weight, out_weight, *in_hbm(own, pj))


def own_products_kernel(both_ref, out_ref, left_hbm, right_hbm, sems):
    copies = []
    for block in range(STEPS):
        for side, target in enumerate((left_hbm, right_hbm)):
            source = both_ref.at[:, pl.ds((2 * block + side) * BLOCK, BLOCK)]
            place = target.at[:, pl.ds(block * BLOCK, BLOCK)]
            copies.append(pltpu.make_async_copy(source, place, sems.at[2 * block + side]))
    for copy in copies:
        copy.start()
    starts = [2 * block * BLOCK for block in range(STEPS)]
    left = jnp.concatenate([both_ref[:, start : start + BLOCK] for start in starts], axis=1)
    right = jnp.concatenate([both_ref[:, start + BLOCK : start + 2 * BLOCK] for start in starts], axis=1)
    out_ref[...] = dot_nt(left, right).astype(BF)
    for copy in copies:
        copy.wait()


def own_products(both):
    return pl.pallas_call(
        own_products_kernel,
        out_specs=[pl.BlockSpec(memory_space=pltpu.VMEM), ANYWHERE, ANYWHERE],
        out_shape=[jax.ShapeDtypeStruct((512, 512), BF), pltpu.HBM((512, CROP), BF), pltpu.HBM((512, CROP), BF)],
        scratch_shapes=[pltpu.SemaphoreType.DMA((2 * STEPS,))],
        compiler_params=pltpu.CompilerParams(vmem_limit_bytes=VMEM_LIMIT),
        cost_estimate=pl.CostEstimate(flops=2**29, bytes_accessed=4 * 2**20, transcendentals=0),
        name="own_products",
    )(both)


def peer_products_kernel(left_ref, right_ref, out_ref):
    left = jnp.concatenate([left_ref[:, 512:], left_ref[:, :512]], axis=1)
    out_ref[...] = dot_nt(left, right_ref[...]).astype(BF)


def peer_products(left, right):
    return pl.pallas_call(
        peer_products_kernel,
        out_shape=pltpu.HBM((512, 512), BF),
        compiler_params=pltpu.CompilerParams(vmem_limit_bytes=VMEM_LIMIT),
        cost_estimate=pl.CostEstimate(flops=2**29, bytes_accessed=4 * 2**20, transcendentals=0),
        name="peer_products",
    )(left, right)


def hidden_features(mine, peer):
    total = mine.astype(F32) + peer.astype(F32)
    return jnp.maximum(total * 0.5, 0.0).astype(BF)


def final_kernel(mine_ref, peer_ref, wf_ref, out_ref, tall0_ref, tall1_ref, wide_ref):
    core = lax.axis_index("tmpl")
    wf = wf_ref[...]
    for source, ref in enumerate((mine_ref, peer_ref)):
        half = core if source == 0 else 1 - core
        tall0_ref[...] = ref[:, :128].astype(F32)
        tall1_ref[...] = ref[:, 128:].astype(F32)
        for j in range(8):
            rows = jnp.concatenate(
                [tall0_ref[pl.ds(j, 128, stride=8), :], tall1_ref[pl.ds(j, 128, stride=8), :]], axis=1
            ).astype(BF)
            result = dot_nt(wf, rows)
            for a in range(4):
                wide_ref[half * 4 + a, pl.ds(j, CZ, stride=8), :] = result[a * CZ : (a + 1) * CZ]
    for a in range(8):
        out_ref[:, a * TILE : (a + 1) * TILE] = wide_ref[a].astype(BF)


def final_projection(mine, peer, wf):
    return pl.pallas_call(
        final_kernel,
        out_shape=jax.ShapeDtypeStruct((CZ * 8, CROP), BF),
        scratch_shapes=[
            pltpu.VMEM((CROP, 128), F32), pltpu.VMEM((CROP, 128), F32), pltpu.VMEM((8, CZ * 8, TILE), F32)
        ],
        compiler_params=pltpu.CompilerParams(vmem_limit_bytes=VMEM_LIMIT),
        name="final",
    )(mine, peer, wf)


def exchange(values, axes, groups, count):
    cube = values.reshape(count, -1, values.shape[-1])
    moved = lax.all_to_all(cube, axes, 0, 0, axis_index_groups=groups, tiled=True)
    return moved.reshape(values.shape)


def on_device(pair_maps, crop_tiles, full_length, proj_weight, out_weight, final_weight):
    wf, prow, q, pj = make_tables(final_weight)
    pair = jnp.transpose(pair_maps[0], (0, 2, 1))
    cropped = crop_columns(crop_tiles, pair)
    got = lax.all_to_all(cropped, "row", 0, 0, axis_index_groups=PLANE, tiled=True)
    current, both = first_projection(crop_tiles, full_length, got, prow, q, proj_weight)
    currents = (current, current)
    weights = (prow, proj_weight, out_weight)
    for layer in range(NLAYER):
        products, left, right = own_products(exchange(both, BOTH_AXES, SAME_PART, CH))
        back_own = exchange(products, BOTH_AXES, SAME_PART, CH)
        right_peer = lax.ppermute(right, BOTH_AXES, OTHER_PART)
        back_peer = exchange(peer_products(left, right_peer), BOTH_AXES, SAME_PART, CH)
        if layer + 1 < NLAYER:
            scalars = (crop_tiles, full_length)
            own, both = middle_half(0, *scalars, back_own, currents[0], *weights, layer, None)
            peer, both = middle_half(1, *scalars, back_peer, currents[1], *weights, layer, both)
            currents = (own, peer)
    rows = last_own(back_own, currents[0], *weights, NLAYER - 1)
    mine, other = last_peer(back_peer, currents[1], *weights, rows, pj, NLAYER - 1)
    hidden = hidden_features(mine, lax.ppermute(other, "tmpl", CORES))
    moved = exchange(hidden, "row", BY_Z, 128)
    result = final_projection(moved, lax.ppermute(moved, "tmpl", CORES), wf)
    return result.reshape(CZ, 8, CROP)


def solution(mesh):
    placed = (P("tmpl", "row", None, None), P("tmpl", None), P(), P(), P(), P())
    return jax.shard_map(
        on_device, mesh=mesh, in_specs=placed, out_specs=P(None, "row", None), check_vma=False
    )
```

```python
import functools

import jax
import jax.numpy as jnp
from jax import lax
from jax.experimental import pallas as pl
from jax.experimental.pallas import tpu as pltpu
from jax.sharding import PartitionSpec as P

CH = 64
CZ = 128
CROP = 1024
TILE = 128
NLAYER = 2
FULL = 2048
ROWS = 8
EPSILON = 1e-05
BF = jnp.bfloat16
F32 = jnp.float32

PLANE = [[s * 8 + z for s in range(16)] for z in range(8)]
BOTH_AXES = ("tmpl", "row")
SAME_PART = [
    [t * 128 + s * 8 + ((7 - zi if part else zi) + 2 * t) % 8 for s in range(16) for zi in range(4)]
    for t in range(2)
    for part in range(2)
]
OTHER_PART = [
    (t * 128 + s * 8 + z, t * 128 + s * 8 + (7 + 4 * t - z) % 8) for t in range(2) for s in range(16) for z in range(8)
]
BY_Z = [[s * 8 + z for z in range(8) for s in range(16)]]
CORES = [(0, 1), (1, 0)]
VMEM_LIMIT = 24 * 1024 * 1024


def in_vmem(*arrays):
    return [pltpu.with_memory_space_constraint(array, pltpu.VMEM) for array in arrays]


def in_hbm(*arrays):
    return [pltpu.with_memory_space_constraint(array, pltpu.HBM) for array in arrays]


def iota(shape, dim):
    return lax.broadcasted_iota(jnp.int32, shape, dim)


def onehot(mask):
    return jnp.where(mask, 1.0, 0.0).astype(BF)


def dot(a, b):
    return jnp.dot(a, b, preferred_element_type=F32)


def dot_nt(a, b):
    return lax.dot_general(a, b, (((1,), (1,)), ((), ())), preferred_element_type=F32)


def dot_tn(a, b):
    return lax.dot_general(a, b, (((0,), (0,)), ((), ())), preferred_element_type=F32)


def lane_token(lane):
    core, chip = lax.axis_index("tmpl"), lax.axis_index("row")
    part = (lane // 512) ^ (((chip % 8 + 8 - 2 * core) % 8) // 4)
    place = (lane // 8) % 4
    z = (jnp.where(part == 0, place, 7 - place) + 2 * core) % 8
    return (lane % 8) * 128 + z * 16 + (lane // 32) % 16


def tables_kernel(final_ref, wf_ref, prow_ref, pj_ref):
    down = onehot(iota((512, CZ), 0) % CZ == iota((512, CZ), 1))
    across = onehot(iota((CH, 256), 0) == iota((CH, 256), 1) % CH)
    tall = dot_nt(down, final_ref[...]).astype(BF)
    block = iota((512, 256), 0) // CZ == iota((512, 256), 1) // CH
    wf_ref[...] = jnp.where(block, dot(tall, across), 0.0).astype(BF)
    r0, c0 = iota((512, 512), 0), iota((512, 512), 1)
    prow_ref[...] = onehot((r0 // 8 == c0 % CH) & (r0 % 8 == c0 // CH))
    r1, c1 = iota((CROP, CROP), 0), iota((CROP, CROP), 1)
    token = lane_token(c1)
    dest = r1 // 8
    pj_ref[...] = onehot(((dest % 16) * 8 + dest // 16) * 8 + r1 % 8 == token)


def make_tables(final_weight):
    return pl.pallas_call(
        tables_kernel,
        out_shape=[
            pltpu.VMEM((512, 256), BF), pltpu.VMEM((512, 512), BF),
            pltpu.HBM((CROP, CROP), BF),
        ],
        compiler_params=pltpu.CompilerParams(vmem_limit_bytes=40 * 1024 * 1024),
        cost_estimate=pl.CostEstimate(flops=10**9, bytes_accessed=6 * 2**20, transcendentals=0),
        name="tables",
    )(final_weight)


CROP_CHUNKS = 4


def crop_kernel(crop_ref, x_hbm, o_hbm, rows_ref, in_sems, out_sems):
    size = 16 // CROP_CHUNKS
    loads, stores = [], []
    for chunk in range(CROP_CHUNKS):
        rows = pl.ds(chunk * size, size)
        for a in range(8):
            tile = pl.ds(pl.multiple_of(crop_ref[0, a] * TILE, TILE), TILE)
            load = pltpu.make_async_copy(
                x_hbm.at[rows, :, tile], rows_ref.at[rows, :, pl.ds(a * TILE, TILE)], in_sems.at[chunk * 8 + a]
            )
            load.start()
            loads.append(load)
    for chunk in range(CROP_CHUNKS):
        rows = pl.ds(chunk * size, size)
        for load in loads[chunk * 8 : chunk * 8 + 8]:
            load.wait()
        store = pltpu.make_async_copy(rows_ref.at[rows], o_hbm.at[rows], out_sems.at[chunk])
        store.start()
        stores.append(store)
    for store in stores:
        store.wait()


def crop_columns(crop_tiles, pair):
    return pl.pallas_call(
        crop_kernel,
        grid_spec=pltpu.PrefetchScalarGridSpec(
            num_scalar_prefetch=1,
            grid=(1,),
            in_specs=[pl.BlockSpec(memory_space=pl.ANY)],
            out_specs=pl.BlockSpec(memory_space=pl.ANY),
            scratch_shapes=[
                pltpu.VMEM((16, CH, CROP), BF),
                pltpu.SemaphoreType.DMA((8 * CROP_CHUNKS,)),
                pltpu.SemaphoreType.DMA((CROP_CHUNKS,)),
            ],
        ),
        out_shape=pltpu.HBM((16, CH, CROP), BF),
        compiler_params=pltpu.CompilerParams(vmem_limit_bytes=VMEM_LIMIT),
        name="crop",
    )(crop_tiles, *in_hbm(pair))


def norm_channels(values):
    center = values - jnp.sum(values, axis=0, keepdims=True) * (1.0 / CH)
    spread = jnp.sum(center * center, axis=0, keepdims=True) * (1.0 / CH)
    return center * lax.rsqrt(spread + EPSILON)


def sigmoid(values):
    return 0.5 * jnp.tanh(0.5 * values) + 0.5


def side_by_side(values):
    return jnp.concatenate([values[a * CH : (a + 1) * CH] for a in range(ROWS)], axis=1)


def stacked(values):
    lanes = values.shape[1] // ROWS
    return jnp.concatenate([values[:, a * lanes : (a + 1) * lanes] for a in range(ROWS)], axis=0)


def pair_mask(crop_ref, length_ref, lanes, start):
    chip = lax.axis_index("row")
    inside = (chip % 8) * 16 + chip // 8
    length = length_ref[0]
    lane = iota((1, lanes), 1) + start
    position = lane_token(lane) % TILE
    for a in range(ROWS):
        position = position + jnp.where(lane % 8 == a, crop_ref[0, a] * TILE, 0)
    parts = []
    for a in range(ROWS):
        row_position = crop_ref[0, a] * TILE + inside
        parts.append(jnp.where((position < length) & (row_position < length), 1.0, 0.0))
    return jnp.concatenate(parts, axis=1)


def project(current, w, prow, mask, both_ref):
    values = dot_tn(w[:, : 4 * CH], norm_channels(current).astype(BF))
    lanes = both_ref.shape[1] // 2
    for side in range(2):
        gate = values[side * 128 : side * 128 + CH]
        value = values[side * 128 + CH : side * 128 + 2 * CH]
        factor = (sigmoid(gate) * value * mask).astype(BF)
        both_ref[:, side * lanes : (side + 1) * lanes] = dot(prow, stacked(factor)).astype(BF)


BLOCK = 512
ANYWHERE = pl.BlockSpec(memory_space=pl.ANY)
RESIDENT = pl.BlockSpec(memory_space=pltpu.VMEM)
STEPS = CROP // BLOCK
HALF_STEPS = STEPS // 2
LAST_BLOCK = 256
LAST_STEPS = CROP // LAST_BLOCK
BOTH = pltpu.HBM((512, 2 * CROP), BF)


def first_kernel(crop_ref, length_ref, got_ref, prow_ref, w_ref, cur_ref, both_ref):
    step = pl.program_id(0)
    parts = jnp.concatenate([got_ref[crop_ref[0, a]] for a in range(ROWS)], axis=0)
    order = onehot(iota((CROP, BLOCK), 0) == lane_token(iota((1, BLOCK), 1) + step * BLOCK))
    current = dot(parts, order)
    cur_ref[...] = current.astype(BF)
    mask = pair_mask(crop_ref, length_ref, BLOCK, step * BLOCK)
    project(side_by_side(current), w_ref[0], prow_ref[...], mask, both_ref)


def full(shape):
    return pl.BlockSpec(shape, lambda step, *_: (0,) * len(shape), pipeline_mode=pl.Buffered(1))


def lanes_of(rows, lanes=BLOCK, offset=0):
    return pl.BlockSpec((rows, lanes), lambda step, *_: (0, step + offset))


def layer_weight(columns, layer):
    return pl.BlockSpec((1, CH, columns), lambda step, *_: (layer, 0, 0), pipeline_mode=pl.Buffered(1))


def first_projection(crop_tiles, full_length, got, prow, proj_weight):
    return pl.pallas_call(
        first_kernel,
        grid_spec=pltpu.PrefetchScalarGridSpec(
            num_scalar_prefetch=2,
            grid=(STEPS,),
            in_specs=[RESIDENT, RESIDENT, layer_weight(320, 0)],
            out_specs=[lanes_of(512), lanes_of(512, 2 * BLOCK)],
        ),
        out_shape=[pltpu.HBM((512, CROP), BF), BOTH],
        compiler_params=pltpu.CompilerParams(vmem_limit_bytes=VMEM_LIMIT),
        name="first",
    )(crop_tiles, full_length, *in_vmem(got, prow), proj_weight)


def update(back_ref, cur_ref, prow, w_proj, w_out):
    block = cur_ref.shape[1]
    current = side_by_side(cur_ref[...].astype(F32))
    gate = sigmoid(dot_tn(w_proj[:, 4 * CH :], norm_channels(current).astype(BF)))
    lanes = pl.ds(pl.multiple_of(pl.program_id(0) * block, block), block)
    products = side_by_side(dot_tn(prow, back_ref[:, lanes]))
    change = dot_tn(w_out, norm_channels(products).astype(BF))
    return (current + gate * change).astype(BF)


def middle_kernel(
    crop_ref, length_ref, back_ref, cur_ref, prow_ref, w_ref, w_out_ref, w_next_ref, next_ref, both_ref
):
    current = update(back_ref, cur_ref, prow_ref[...], w_ref[0], w_out_ref[0])
    next_ref[...] = stacked(current)
    mask = pair_mask(crop_ref, length_ref, BLOCK, pl.program_id(0) * BLOCK)
    project(current.astype(F32), w_next_ref[0], prow_ref[...], mask, both_ref)


def middle_layer(crop_tiles, full_length, back, current, prow, proj_weight, out_weight, layer):
    return pl.pallas_call(
        middle_kernel,
        grid_spec=pltpu.PrefetchScalarGridSpec(
            num_scalar_prefetch=2,
            grid=(STEPS,),
            in_specs=[
                RESIDENT, lanes_of(512), RESIDENT,
                layer_weight(320, layer), layer_weight(CH, layer), layer_weight(320, layer + 1),
            ],
            out_specs=[lanes_of(512), lanes_of(512, 2 * BLOCK)],
        ),
        out_shape=[pltpu.HBM((512, CROP), BF), BOTH],
        compiler_params=pltpu.CompilerParams(vmem_limit_bytes=VMEM_LIMIT),
        name="middle",
    )(
        crop_tiles, full_length, *in_vmem(back), *in_hbm(current), *in_vmem(prow), proj_weight, out_weight,
        proj_weight,
    )


def last_rows(back_ref, cur_ref, prow_ref, w_ref, w_out_ref):
    current = update(back_ref, cur_ref, prow_ref[...], w_ref[0], w_out_ref[0])
    return stacked(norm_channels(current.astype(F32)).astype(BF))


def last_kernel(back_ref, cur_ref, prow_ref, w_ref, w_out_ref, pj_hbm, mine_ref, other_ref, rows_ref, pj_ref, sem):
    step = pl.program_id(0)
    load = pltpu.make_async_copy(pj_hbm, pj_ref, sem)

    @pl.when(step == 0)
    def _():
        load.start()

    lanes = pl.ds(pl.multiple_of(step * LAST_BLOCK, LAST_BLOCK), LAST_BLOCK)
    rows_ref[:, lanes] = last_rows(back_ref, cur_ref, prow_ref, w_ref, w_out_ref)

    @pl.when(step == LAST_STEPS - 1)
    def _():
        load.wait()
        core = lax.axis_index("tmpl")
        pj = pj_ref[...]
        mine_ref[...] = dot_nt(pj, rows_ref[pl.ds(pl.multiple_of(core * 256, 256), 256), :]).astype(BF)
        other_ref[...] = dot_nt(pj, rows_ref[pl.ds(pl.multiple_of(256 - core * 256, 256), 256), :]).astype(BF)


def last_layer(back, current, prow, proj_weight, out_weight, pj, layer):
    return pl.pallas_call(
        last_kernel,
        grid=(LAST_STEPS,),
        in_specs=[
            RESIDENT, lanes_of(512, LAST_BLOCK), RESIDENT, layer_weight(320, layer), layer_weight(CH, layer), ANYWHERE
        ],
        out_specs=[full((CROP, 256))] * 2,
        out_shape=[jax.ShapeDtypeStruct((CROP, 256), BF)] * 2,
        scratch_shapes=[pltpu.VMEM((512, CROP), BF), pltpu.VMEM((CROP, CROP), BF), pltpu.SemaphoreType.DMA],
        compiler_params=pltpu.CompilerParams(vmem_limit_bytes=VMEM_LIMIT),
        name="last",
    )(*in_vmem(back), *in_hbm(current), *in_vmem(prow), proj_weight, out_weight, *in_hbm(pj))


def own_products_kernel(both_ref, out_hbm, left_hbm, right_hbm, own_ref, sems):
    copies = []
    for side, target in ((1, right_hbm), (0, left_hbm)):
        for block in range(STEPS):
            source = both_ref.at[:, pl.ds((2 * block + side) * BLOCK, BLOCK)]
            place = target.at[:, pl.ds(block * BLOCK, BLOCK)]
            copies.append(pltpu.make_async_copy(source, place, sems.at[2 * block + side]))
    for copy in copies:
        copy.start()
    starts = [2 * block * BLOCK for block in range(STEPS)]
    left = jnp.concatenate([both_ref[:, start : start + BLOCK] for start in starts], axis=1)
    right = jnp.concatenate([both_ref[:, start + BLOCK : start + 2 * BLOCK] for start in starts], axis=1)
    own_ref[...] = dot_nt(left, right).astype(BF)
    store = pltpu.make_async_copy(own_ref, out_hbm.at[:, pl.ds(0, 512)], sems.at[2 * STEPS])
    store.start()
    for copy in copies:
        copy.wait()
    store.wait()


def own_products(both):
    square = pltpu.HBM((512, CROP), BF)
    return pl.pallas_call(
        own_products_kernel,
        out_specs=[ANYWHERE] * 3,
        out_shape=[square] * 3,
        scratch_shapes=[pltpu.VMEM((512, 512), BF), pltpu.SemaphoreType.DMA((2 * STEPS + 1,))],
        compiler_params=pltpu.CompilerParams(vmem_limit_bytes=VMEM_LIMIT),
        cost_estimate=pl.CostEstimate(flops=2**29, bytes_accessed=4 * 2**20, transcendentals=0),
        name="own_products",
    )(both)


def peer_products_kernel(left_ref, right_ref, products_hbm, out_hbm, peer_ref, sem):
    del products_hbm
    left = jnp.concatenate([left_ref[:, 512:], left_ref[:, :512]], axis=1)
    peer_ref[...] = dot_nt(left, right_ref[...]).astype(BF)
    store = pltpu.make_async_copy(peer_ref, out_hbm.at[:, pl.ds(512, 512)], sem)
    store.start()
    store.wait()


def peer_products(left, right, products):
    return pl.pallas_call(
        peer_products_kernel,
        in_specs=[RESIDENT, RESIDENT, ANYWHERE],
        out_specs=ANYWHERE,
        out_shape=pltpu.HBM((512, CROP), BF),
        input_output_aliases={2: 0},
        scratch_shapes=[pltpu.VMEM((512, 512), BF), pltpu.SemaphoreType.DMA],
        compiler_params=pltpu.CompilerParams(vmem_limit_bytes=VMEM_LIMIT),
        cost_estimate=pl.CostEstimate(flops=2**29, bytes_accessed=4 * 2**20, transcendentals=0),
        name="peer_products",
    )(left, right, products)


def hidden_features(mine, peer):
    total = mine.astype(F32) + peer.astype(F32)
    return jnp.maximum(total * 0.5, 0.0).astype(BF)


def final_kernel(source, *refs):
    rows_ref, wf_ref = refs[:2]
    out_hbm, tall0_ref, tall1_ref, wide_ref, stage_ref, sems = refs[-6:]
    core = lax.axis_index("tmpl")
    half = core if source == 0 else 1 - core
    wf = wf_ref[...]
    tall0_ref[...] = rows_ref[:, :128].astype(F32)
    tall1_ref[...] = rows_ref[:, 128:].astype(F32)
    for j in range(8):
        rows = jnp.concatenate(
            [tall0_ref[pl.ds(j, 128, stride=8), :], tall1_ref[pl.ds(j, 128, stride=8), :]], axis=1
        ).astype(BF)
        result = dot_nt(wf, rows)
        for a in range(4):
            wide_ref[a, pl.ds(j, CZ, stride=8), :] = result[a * CZ : (a + 1) * CZ]
    stores = []
    for a in range(4):
        lanes = pl.ds(a * TILE, TILE)
        stage_ref[:, lanes] = wide_ref[a].astype(BF)
        place = pl.ds(pl.multiple_of(half * 512 + a * TILE, TILE), TILE)
        store = pltpu.make_async_copy(stage_ref.at[:, lanes], out_hbm.at[:, place], sems.at[a])
        store.start()
        stores.append(store)
    for store in stores:
        store.wait()


def final_projection(source, rows, wf, earlier=()):
    return pl.pallas_call(
        functools.partial(final_kernel, source),
        in_specs=[RESIDENT, RESIDENT] + [ANYWHERE] * len(earlier),
        out_specs=ANYWHERE,
        out_shape=pltpu.HBM((CZ * 8, CROP), BF),
        input_output_aliases={2 + k: 0 for k in range(len(earlier))},
        scratch_shapes=[
            pltpu.VMEM((CROP, 128), F32), pltpu.VMEM((CROP, 128), F32), pltpu.VMEM((4, CZ * 8, TILE), F32),
            pltpu.VMEM((CZ * 8, 512), BF), pltpu.SemaphoreType.DMA((4,)),
        ],
        compiler_params=pltpu.CompilerParams(vmem_limit_bytes=VMEM_LIMIT),
        cost_estimate=pl.CostEstimate(flops=2**28, bytes_accessed=2 * 2**20, transcendentals=0),
        name="final" + str(source),
    )(rows, wf, *earlier)


def exchange(values, axes, groups, count):
    cube = values.reshape(count, -1, values.shape[-1])
    moved = lax.all_to_all(cube, axes, 0, 0, axis_index_groups=groups, tiled=True)
    return moved.reshape(values.shape)


def on_device(pair_maps, crop_tiles, full_length, proj_weight, out_weight, final_weight):
    wf, prow, pj = make_tables(final_weight)
    pair = jnp.transpose(pair_maps[0], (0, 2, 1))
    cropped = crop_columns(crop_tiles, pair)
    got = lax.all_to_all(cropped, "row", 0, 0, axis_index_groups=PLANE, tiled=True)
    current, both = first_projection(crop_tiles, full_length, got, prow, proj_weight)
    weights = (prow, proj_weight, out_weight)
    for layer in range(NLAYER):
        products, left, right = own_products(exchange(both, BOTH_AXES, SAME_PART, CH))
        right_peer = lax.ppermute(right, BOTH_AXES, OTHER_PART)
        products = peer_products(left, right_peer, products)
        back = exchange(products, BOTH_AXES, SAME_PART, CH)
        if layer + 1 < NLAYER:
            current, both = middle_layer(crop_tiles, full_length, back, current, *weights, layer)
    mine, other = last_layer(back, current, *weights, pj, NLAYER - 1)
    hidden = hidden_features(mine, lax.ppermute(other, "tmpl", CORES))
    moved = exchange(hidden, "row", BY_Z, 128)
    result = final_projection(0, moved, wf)
    result = final_projection(1, lax.ppermute(moved, "tmpl", CORES), wf, (result,))
    return result.reshape(CZ, 8, CROP)


def solution(mesh):
    placed = (P("tmpl", "row", None, None), P("tmpl", None), P(), P(), P(), P())
    return jax.shard_map(
        on_device, mesh=mesh, in_specs=placed, out_specs=P(None, "row", None), check_vma=False
    )
```

```python
import functools

import jax
import jax.numpy as jnp
from jax import lax
from jax.experimental import pallas as pl
from jax.experimental.pallas import tpu as pltpu
from jax.sharding import PartitionSpec as P

CH = 64
CZ = 128
CROP = 1024
TILE = 128
NLAYER = 2
FULL = 2048
ROWS = 8
EPSILON = 1e-05
BF = jnp.bfloat16
F32 = jnp.float32

PLANE = [[s * 8 + z for s in range(16)] for z in range(8)]
BOTH_AXES = ("tmpl", "row")
SAME_PART = [
    [t * 128 + s * 8 + ((7 - zi if part else zi) + 2 * t) % 8 for s in range(16) for zi in range(4)]
    for t in range(2)
    for part in range(2)
]
OTHER_PART = [
    (t * 128 + s * 8 + z, t * 128 + s * 8 + (7 + 4 * t - z) % 8) for t in range(2) for s in range(16) for z in range(8)
]
BY_Z = [[s * 8 + z for z in range(8) for s in range(16)]]
CORES = [(0, 1), (1, 0)]
VMEM_LIMIT = 24 * 1024 * 1024


def in_vmem(*arrays):
    return [pltpu.with_memory_space_constraint(array, pltpu.VMEM) for array in arrays]


def in_hbm(*arrays):
    return [pltpu.with_memory_space_constraint(array, pltpu.HBM) for array in arrays]


def iota(shape, dim):
    return lax.broadcasted_iota(jnp.int32, shape, dim)


def onehot(mask):
    return jnp.where(mask, 1.0, 0.0).astype(BF)


def dot(a, b):
    return jnp.dot(a, b, preferred_element_type=F32)


def dot_nt(a, b):
    return lax.dot_general(a, b, (((1,), (1,)), ((), ())), preferred_element_type=F32)


def dot_tn(a, b):
    return lax.dot_general(a, b, (((0,), (0,)), ((), ())), preferred_element_type=F32)


def lane_token(lane):
    core, chip = lax.axis_index("tmpl"), lax.axis_index("row")
    part = (lane // 512) ^ (((chip % 8 + 8 - 2 * core) % 8) // 4)
    place = (lane // 8) % 4
    z = (jnp.where(part == 0, place, 7 - place) + 2 * core) % 8
    return (lane % 8) * 128 + z * 16 + (lane // 32) % 16


def tables_kernel(final_ref, wf_ref, prow_ref, pj_ref):
    down = onehot(iota((512, CZ), 0) % CZ == iota((512, CZ), 1))
    across = onehot(iota((CH, 256), 0) == iota((CH, 256), 1) % CH)
    tall = dot_nt(down, final_ref[...]).astype(BF)
    block = iota((512, 256), 0) // CZ == iota((512, 256), 1) // CH
    wf_ref[...] = jnp.where(block, dot(tall, across), 0.0).astype(BF)
    r0, c0 = iota((512, 512), 0), iota((512, 512), 1)
    prow_ref[...] = onehot((r0 // 8 == c0 % CH) & (r0 % 8 == c0 // CH))
    r1, c1 = iota((CROP, CROP), 0), iota((CROP, CROP), 1)
    token = lane_token(c1)
    dest = r1 // 8
    pj_ref[...] = onehot(((dest % 16) * 8 + dest // 16) * 8 + r1 % 8 == token)


def make_tables(final_weight):
    return pl.pallas_call(
        tables_kernel,
        out_shape=[
            pltpu.VMEM((512, 256), BF), pltpu.VMEM((512, 512), BF),
            pltpu.HBM((CROP, CROP), BF),
        ],
        compiler_params=pltpu.CompilerParams(vmem_limit_bytes=40 * 1024 * 1024),
        cost_estimate=pl.CostEstimate(flops=10**9, bytes_accessed=6 * 2**20, transcendentals=0),
        name="tables",
    )(final_weight)


CROP_CHUNKS = 4


def crop_kernel(crop_ref, x_hbm, o_hbm, rows_ref, in_sems, out_sems):
    size = 16 // CROP_CHUNKS
    loads, stores = [], []
    for chunk in range(CROP_CHUNKS):
        rows = pl.ds(chunk * size, size)
        for a in range(8):
            tile = pl.ds(pl.multiple_of(crop_ref[0, a] * TILE, TILE), TILE)
            load = pltpu.make_async_copy(
                x_hbm.at[rows, :, tile], rows_ref.at[rows, :, pl.ds(a * TILE, TILE)], in_sems.at[chunk * 8 + a]
            )
            load.start()
            loads.append(load)
    for chunk in range(CROP_CHUNKS):
        rows = pl.ds(chunk * size, size)
        for load in loads[chunk * 8 : chunk * 8 + 8]:
            load.wait()
        store = pltpu.make_async_copy(rows_ref.at[rows], o_hbm.at[rows], out_sems.at[chunk])
        store.start()
        stores.append(store)
    for store in stores:
        store.wait()


def crop_columns(crop_tiles, pair):
    return pl.pallas_call(
        crop_kernel,
        grid_spec=pltpu.PrefetchScalarGridSpec(
            num_scalar_prefetch=1,
            grid=(1,),
            in_specs=[pl.BlockSpec(memory_space=pl.ANY)],
            out_specs=pl.BlockSpec(memory_space=pl.ANY),
            scratch_shapes=[
                pltpu.VMEM((16, CH, CROP), BF),
                pltpu.SemaphoreType.DMA((8 * CROP_CHUNKS,)),
                pltpu.SemaphoreType.DMA((CROP_CHUNKS,)),
            ],
        ),
        out_shape=pltpu.HBM((16, CH, CROP), BF),
        compiler_params=pltpu.CompilerParams(vmem_limit_bytes=VMEM_LIMIT),
        name="crop",
    )(crop_tiles, *in_hbm(pair))


def norm_channels(values):
    center = values - jnp.sum(values, axis=0, keepdims=True) * (1.0 / CH)
    spread = jnp.sum(center * center, axis=0, keepdims=True) * (1.0 / CH)
    return center * lax.rsqrt(spread + EPSILON)


def halved(weights):
    return (weights.astype(F32) * 0.5).astype(BF)


def side_by_side(values):
    return jnp.concatenate([values[a * CH : (a + 1) * CH] for a in range(ROWS)], axis=1)


def stacked(values):
    lanes = values.shape[1] // ROWS
    return jnp.concatenate([values[:, a * lanes : (a + 1) * lanes] for a in range(ROWS)], axis=0)


def pair_mask(crop_ref, length_ref, lanes, start):
    chip = lax.axis_index("row")
    inside = (chip % 8) * 16 + chip // 8
    length = length_ref[0]
    lane = iota((1, lanes), 1) + start
    position = lane_token(lane) % TILE
    for a in range(ROWS):
        position = position + jnp.where(lane % 8 == a, crop_ref[0, a] * TILE, 0)
    parts = []
    for a in range(ROWS):
        row_position = crop_ref[0, a] * TILE + inside
        parts.append(jnp.where((position < length) & (row_position < length), 1.0, 0.0))
    return jnp.concatenate(parts, axis=1)


def project(current, w, prow, mask, both_ref):
    values = dot_tn(halved(w[:, : 4 * CH]), norm_channels(current).astype(BF))
    lanes = both_ref.shape[1] // 2
    for side in range(2):
        gate = values[side * 128 : side * 128 + CH]
        value = values[side * 128 + CH : side * 128 + 2 * CH]
        factor = ((jnp.tanh(gate) + 1.0) * (value * mask)).astype(BF)
        both_ref[:, side * lanes : (side + 1) * lanes] = dot(prow, stacked(factor)).astype(BF)


BLOCK = 512
ANYWHERE = pl.BlockSpec(memory_space=pl.ANY)
RESIDENT = pl.BlockSpec(memory_space=pltpu.VMEM)
STEPS = CROP // BLOCK
HALF_STEPS = STEPS // 2
LAST_BLOCK = 256
LAST_STEPS = CROP // LAST_BLOCK
BOTH = pltpu.HBM((512, 2 * CROP), BF)


def first_kernel(crop_ref, length_ref, got_ref, prow_ref, w_ref, cur_ref, both_ref):
    step = pl.program_id(0)
    parts = jnp.concatenate([got_ref[crop_ref[0, a]] for a in range(ROWS)], axis=0)
    order = onehot(iota((CROP, BLOCK), 0) == lane_token(iota((1, BLOCK), 1) + step * BLOCK))
    current = dot(parts, order)
    cur_ref[...] = current.astype(BF)
    mask = pair_mask(crop_ref, length_ref, BLOCK, step * BLOCK)
    project(side_by_side(current), w_ref[0], prow_ref[...], mask, both_ref)


def full(shape):
    return pl.BlockSpec(shape, lambda step, *_: (0,) * len(shape), pipeline_mode=pl.Buffered(1))


def lanes_of(rows, lanes=BLOCK, offset=0):
    return pl.BlockSpec((rows, lanes), lambda step, *_: (0, step + offset))


def layer_weight(columns, layer):
    return pl.BlockSpec((1, CH, columns), lambda step, *_: (layer, 0, 0), pipeline_mode=pl.Buffered(1))


def first_projection(crop_tiles, full_length, got, prow, proj_weight):
    return pl.pallas_call(
        first_kernel,
        grid_spec=pltpu.PrefetchScalarGridSpec(
            num_scalar_prefetch=2,
            grid=(STEPS,),
            in_specs=[RESIDENT, RESIDENT, layer_weight(320, 0)],
            out_specs=[lanes_of(512), lanes_of(512, 2 * BLOCK)],
        ),
        out_shape=[pltpu.HBM((512, CROP), BF), BOTH],
        compiler_params=pltpu.CompilerParams(vmem_limit_bytes=VMEM_LIMIT),
        name="first",
    )(crop_tiles, full_length, *in_vmem(got, prow), proj_weight)


def update(back_ref, cur_ref, prow, w_proj, w_out):
    block = cur_ref.shape[1]
    current = side_by_side(cur_ref[...].astype(F32))
    gate = jnp.tanh(dot_tn(halved(w_proj[:, 4 * CH :]), norm_channels(current).astype(BF))) + 1.0
    lanes = pl.ds(pl.multiple_of(pl.program_id(0) * block, block), block)
    products = side_by_side(dot_tn(prow, back_ref[:, lanes]))
    change = dot_tn(halved(w_out), norm_channels(products).astype(BF))
    return (current + gate * change).astype(BF)


def middle_kernel(
    crop_ref, length_ref, back_ref, cur_ref, prow_ref, w_ref, w_out_ref, w_next_ref, next_ref, both_ref
):
    current = update(back_ref, cur_ref, prow_ref[...], w_ref[0], w_out_ref[0])
    next_ref[...] = stacked(current)
    mask = pair_mask(crop_ref, length_ref, BLOCK, pl.program_id(0) * BLOCK)
    project(current.astype(F32), w_next_ref[0], prow_ref[...], mask, both_ref)


def middle_layer(crop_tiles, full_length, back, current, prow, proj_weight, out_weight, layer):
    return pl.pallas_call(
        middle_kernel,
        grid_spec=pltpu.PrefetchScalarGridSpec(
            num_scalar_prefetch=2,
            grid=(STEPS,),
            in_specs=[
                RESIDENT, lanes_of(512), RESIDENT,
                layer_weight(320, layer), layer_weight(CH, layer), layer_weight(320, layer + 1),
            ],
            out_specs=[lanes_of(512), lanes_of(512, 2 * BLOCK)],
        ),
        out_shape=[pltpu.HBM((512, CROP), BF), BOTH],
        compiler_params=pltpu.CompilerParams(vmem_limit_bytes=VMEM_LIMIT),
        name="middle",
    )(
        crop_tiles, full_length, *in_vmem(back), *in_hbm(current), *in_vmem(prow), proj_weight, out_weight,
        proj_weight,
    )


def last_rows(back_ref, cur_ref, prow_ref, w_ref, w_out_ref):
    current = update(back_ref, cur_ref, prow_ref[...], w_ref[0], w_out_ref[0])
    return stacked(norm_channels(current.astype(F32)).astype(BF))


def last_kernel(back_ref, cur_ref, prow_ref, w_ref, w_out_ref, pj_hbm, mine_ref, other_ref, rows_ref, pj_ref, sem):
    step = pl.program_id(0)
    load = pltpu.make_async_copy(pj_hbm, pj_ref, sem)

    @pl.when(step == 0)
    def _():
        load.start()

    lanes = pl.ds(pl.multiple_of(step * LAST_BLOCK, LAST_BLOCK), LAST_BLOCK)
    rows_ref[:, lanes] = last_rows(back_ref, cur_ref, prow_ref, w_ref, w_out_ref)

    @pl.when(step == LAST_STEPS - 1)
    def _():
        load.wait()
        core = lax.axis_index("tmpl")
        pj = pj_ref[...]
        mine_ref[...] = dot_nt(pj, rows_ref[pl.ds(pl.multiple_of(core * 256, 256), 256), :]).astype(BF)
        other_ref[...] = dot_nt(pj, rows_ref[pl.ds(pl.multiple_of(256 - core * 256, 256), 256), :]).astype(BF)


def last_layer(back, current, prow, proj_weight, out_weight, pj, layer):
    return pl.pallas_call(
        last_kernel,
        grid=(LAST_STEPS,),
        in_specs=[
            RESIDENT, lanes_of(512, LAST_BLOCK), RESIDENT, layer_weight(320, layer), layer_weight(CH, layer), ANYWHERE
        ],
        out_specs=[full((CROP, 256))] * 2,
        out_shape=[jax.ShapeDtypeStruct((CROP, 256), BF)] * 2,
        scratch_shapes=[pltpu.VMEM((512, CROP), BF), pltpu.VMEM((CROP, CROP), BF), pltpu.SemaphoreType.DMA],
        compiler_params=pltpu.CompilerParams(vmem_limit_bytes=VMEM_LIMIT),
        name="last",
    )(*in_vmem(back), *in_hbm(current), *in_vmem(prow), proj_weight, out_weight, *in_hbm(pj))


def right_kernel(both_ref, right_hbm, sems):
    copies = []
    for block in range(STEPS):
        source = both_ref.at[:, pl.ds((2 * block + 1) * BLOCK, BLOCK)]
        place = right_hbm.at[:, pl.ds(block * BLOCK, BLOCK)]
        copies.append(pltpu.make_async_copy(source, place, sems.at[block]))
    for copy in copies:
        copy.start()
    for copy in copies:
        copy.wait()


def right_alone(both):
    return pl.pallas_call(
        right_kernel,
        in_specs=[RESIDENT],
        out_specs=ANYWHERE,
        out_shape=pltpu.HBM((512, CROP), BF),
        scratch_shapes=[pltpu.SemaphoreType.DMA((STEPS,))],
        compiler_params=pltpu.CompilerParams(vmem_limit_bytes=VMEM_LIMIT),
        cost_estimate=pl.CostEstimate(flops=0, bytes_accessed=2 * 2**20, transcendentals=0),
        name="right",
    )(both)


def lane_blocks(both_ref, side, order):
    starts = [(2 * block + side) * BLOCK for block in order]
    return jnp.concatenate([both_ref[:, start : start + BLOCK] for start in starts], axis=1)


def products_kernel(peer, *refs):
    both_ref, right_ref = refs[0], refs[1]
    out_hbm, square_ref, sem = refs[-3:]
    if peer:
        left, right = lane_blocks(both_ref, 0, [1, 0]), right_ref[...]
    else:
        left, right = lane_blocks(both_ref, 0, [0, 1]), lane_blocks(both_ref, 1, [0, 1])
    square_ref[...] = dot_nt(left, right).astype(BF)
    store = pltpu.make_async_copy(square_ref, out_hbm.at[:, pl.ds(512 * peer, 512)], sem)
    store.start()
    store.wait()


def half_products(both, *others):
    peer = len(others) // 2
    return pl.pallas_call(
        functools.partial(products_kernel, peer),
        in_specs=[RESIDENT, RESIDENT, ANYWHERE][: 1 + len(others)],
        out_specs=ANYWHERE,
        out_shape=pltpu.HBM((512, CROP), BF),
        input_output_aliases={2: 0} if peer else {},
        scratch_shapes=[pltpu.VMEM((512, 512), BF), pltpu.SemaphoreType.DMA],
        compiler_params=pltpu.CompilerParams(vmem_limit_bytes=VMEM_LIMIT),
        cost_estimate=pl.CostEstimate(flops=2**29, bytes_accessed=4 * 2**20, transcendentals=0),
        name="products" + str(peer),
    )(both, *others)


def hidden_features(mine, peer):
    total = mine.astype(F32) + peer.astype(F32)
    return jnp.maximum(total * 0.5, 0.0).astype(BF)


def final_kernel(source, *refs):
    rows_ref, wf_ref = refs[:2]
    out_hbm, tall0_ref, tall1_ref, wide_ref, stage_ref, sems = refs[-6:]
    core = lax.axis_index("tmpl")
    half = core if source == 0 else 1 - core
    wf = wf_ref[...]
    tall0_ref[...] = rows_ref[:, :128].astype(F32)
    tall1_ref[...] = rows_ref[:, 128:].astype(F32)
    for j in range(8):
        rows = jnp.concatenate(
            [tall0_ref[pl.ds(j, 128, stride=8), :], tall1_ref[pl.ds(j, 128, stride=8), :]], axis=1
        ).astype(BF)
        result = dot_nt(wf, rows)
        for a in range(4):
            wide_ref[a, pl.ds(j, CZ, stride=8), :] = result[a * CZ : (a + 1) * CZ]
    stores = []
    for a in range(4):
        lanes = pl.ds(a * TILE, TILE)
        stage_ref[:, lanes] = wide_ref[a].astype(BF)
        place = pl.ds(pl.multiple_of(half * 512 + a * TILE, TILE), TILE)
        store = pltpu.make_async_copy(stage_ref.at[:, lanes], out_hbm.at[:, place], sems.at[a])
        store.start()
        stores.append(store)
    for store in stores:
        store.wait()


def final_projection(source, rows, wf, earlier=()):
    return pl.pallas_call(
        functools.partial(final_kernel, source),
        in_specs=[RESIDENT, RESIDENT] + [ANYWHERE] * len(earlier),
        out_specs=ANYWHERE,
        out_shape=pltpu.HBM((CZ * 8, CROP), BF),
        input_output_aliases={2 + k: 0 for k in range(len(earlier))},
        scratch_shapes=[
            pltpu.VMEM((CROP, 128), F32), pltpu.VMEM((CROP, 128), F32), pltpu.VMEM((4, CZ * 8, TILE), F32),
            pltpu.VMEM((CZ * 8, 512), BF), pltpu.SemaphoreType.DMA((4,)),
        ],
        compiler_params=pltpu.CompilerParams(vmem_limit_bytes=VMEM_LIMIT),
        cost_estimate=pl.CostEstimate(flops=2**28, bytes_accessed=2 * 2**20, transcendentals=0),
        name="final" + str(source),
    )(rows, wf, *earlier)


def exchange(values, axes, groups, count):
    cube = values.reshape(count, -1, values.shape[-1])
    moved = lax.all_to_all(cube, axes, 0, 0, axis_index_groups=groups, tiled=True)
    return moved.reshape(values.shape)


def on_device(pair_maps, crop_tiles, full_length, proj_weight, out_weight, final_weight):
    wf, prow, pj = make_tables(final_weight)
    pair = jnp.transpose(pair_maps[0], (0, 2, 1))
    cropped = crop_columns(crop_tiles, pair)
    got = lax.all_to_all(cropped, "row", 0, 0, axis_index_groups=PLANE, tiled=True)
    current, both = first_projection(crop_tiles, full_length, got, prow, proj_weight)
    weights = (prow, proj_weight, out_weight)
    for layer in range(NLAYER):
        gathered = exchange(both, BOTH_AXES, SAME_PART, CH)
        right_peer = lax.ppermute(right_alone(gathered), BOTH_AXES, OTHER_PART)
        products = half_products(gathered, right_peer, half_products(gathered))
        back = exchange(products, BOTH_AXES, SAME_PART, CH)
        if layer + 1 < NLAYER:
            current, both = middle_layer(crop_tiles, full_length, back, current, *weights, layer)
    mine, other = last_layer(back, current, *weights, pj, NLAYER - 1)
    hidden = hidden_features(mine, lax.ppermute(other, "tmpl", CORES))
    moved = exchange(hidden, "row", BY_Z, 128)
    result = final_projection(0, moved, wf)
    result = final_projection(1, lax.ppermute(moved, "tmpl", CORES), wf, (result,))
    return result.reshape(CZ, 8, CROP)


def solution(mesh):
    placed = (P("tmpl", "row", None, None), P("tmpl", None), P(), P(), P(), P())
    return jax.shard_map(
        on_device, mesh=mesh, in_specs=placed, out_specs=P(None, "row", None), check_vma=False
    )
```

```python
import functools

import jax
import jax.numpy as jnp
from jax import lax
from jax.experimental import pallas as pl
from jax.experimental.pallas import tpu as pltpu
from jax.sharding import PartitionSpec as P

CH = 64
CZ = 128
CROP = 1024
TILE = 128
NLAYER = 2
FULL = 2048
ROWS = 8
EPSILON = 1e-05
BF = jnp.bfloat16
F32 = jnp.float32

PLANE = [[s * 8 + z for s in range(16)] for z in range(8)]
BOTH_AXES = ("tmpl", "row")
SAME_PART = [
    [t * 128 + s * 8 + ((7 - zi if part else zi) + 2 * t) % 8 for s in range(16) for zi in range(4)]
    for t in range(2)
    for part in range(2)
]
OTHER_PART = [
    (t * 128 + s * 8 + z, t * 128 + s * 8 + (7 + 4 * t - z) % 8) for t in range(2) for s in range(16) for z in range(8)
]
BY_Z = [[s * 8 + z for z in range(8) for s in range(16)]]
CORES = [(0, 1), (1, 0)]
VMEM_LIMIT = 24 * 1024 * 1024


def in_vmem(*arrays):
    return [pltpu.with_memory_space_constraint(array, pltpu.VMEM) for array in arrays]


def in_hbm(*arrays):
    return [pltpu.with_memory_space_constraint(array, pltpu.HBM) for array in arrays]


def iota(shape, dim):
    return lax.broadcasted_iota(jnp.int32, shape, dim)


def onehot(mask):
    return jnp.where(mask, 1.0, 0.0).astype(BF)


def dot(a, b):
    return jnp.dot(a, b, preferred_element_type=F32)


def dot_nt(a, b):
    return lax.dot_general(a, b, (((1,), (1,)), ((), ())), preferred_element_type=F32)


def dot_tn(a, b):
    return lax.dot_general(a, b, (((0,), (0,)), ((), ())), preferred_element_type=F32)


def lane_token(lane):
    core, chip = lax.axis_index("tmpl"), lax.axis_index("row")
    part = (lane // 512) ^ (((chip % 8 + 8 - 2 * core) % 8) // 4)
    place = (lane // 8) % 4
    z = (jnp.where(part == 0, place, 7 - place) + 2 * core) % 8
    return (lane % 8) * 128 + z * 16 + (lane // 32) % 16


def tables_kernel(final_ref, wf_ref, prow_ref, pj_ref):
    down = onehot(iota((512, CZ), 0) % CZ == iota((512, CZ), 1))
    across = onehot(iota((CH, 256), 0) == iota((CH, 256), 1) % CH)
    tall = dot_nt(down, final_ref[...]).astype(BF)
    block = iota((512, 256), 0) // CZ == iota((512, 256), 1) // CH
    wf_ref[...] = jnp.where(block, dot(tall, across), 0.0).astype(BF)
    r0, c0 = iota((512, 512), 0), iota((512, 512), 1)
    prow_ref[...] = onehot((r0 // 8 == c0 % CH) & (r0 % 8 == c0 // CH))
    r1, c1 = iota((CROP, CROP), 0), iota((CROP, CROP), 1)
    token = lane_token(c1)
    dest = r1 // 8
    pj_ref[...] = onehot(((dest % 16) * 8 + dest // 16) * 8 + r1 % 8 == token)


def make_tables(final_weight):
    return pl.pallas_call(
        tables_kernel,
        out_shape=[
            pltpu.VMEM((512, 256), BF), pltpu.VMEM((512, 512), BF),
            pltpu.HBM((CROP, CROP), BF),
        ],
        compiler_params=pltpu.CompilerParams(vmem_limit_bytes=40 * 1024 * 1024),
        cost_estimate=pl.CostEstimate(flops=10**9, bytes_accessed=6 * 2**20, transcendentals=0),
        name="tables",
    )(final_weight)


CROP_CHUNKS = 4


def crop_kernel(crop_ref, x_hbm, o_hbm, rows_ref, in_sems, out_sems):
    size = 16 // CROP_CHUNKS
    loads, stores = [], []
    for chunk in range(CROP_CHUNKS):
        rows = pl.ds(chunk * size, size)
        for a in range(8):
            tile = pl.ds(pl.multiple_of(crop_ref[0, a] * TILE, TILE), TILE)
            load = pltpu.make_async_copy(
                x_hbm.at[rows, :, tile], rows_ref.at[rows, :, pl.ds(a * TILE, TILE)], in_sems.at[chunk * 8 + a]
            )
            load.start()
            loads.append(load)
    for chunk in range(CROP_CHUNKS):
        rows = pl.ds(chunk * size, size)
        for load in loads[chunk * 8 : chunk * 8 + 8]:
            load.wait()
        store = pltpu.make_async_copy(rows_ref.at[rows], o_hbm.at[rows], out_sems.at[chunk])
        store.start()
        stores.append(store)
    for store in stores:
        store.wait()


def crop_columns(crop_tiles, pair):
    return pl.pallas_call(
        crop_kernel,
        grid_spec=pltpu.PrefetchScalarGridSpec(
            num_scalar_prefetch=1,
            grid=(1,),
            in_specs=[pl.BlockSpec(memory_space=pl.ANY)],
            out_specs=pl.BlockSpec(memory_space=pl.ANY),
            scratch_shapes=[
                pltpu.VMEM((16, CH, CROP), BF),
                pltpu.SemaphoreType.DMA((8 * CROP_CHUNKS,)),
                pltpu.SemaphoreType.DMA((CROP_CHUNKS,)),
            ],
        ),
        out_shape=pltpu.HBM((16, CH, CROP), BF),
        compiler_params=pltpu.CompilerParams(vmem_limit_bytes=VMEM_LIMIT),
        name="crop",
    )(crop_tiles, *in_hbm(pair))


def norm_channels(values):
    center = values - jnp.sum(values, axis=0, keepdims=True) * (1.0 / CH)
    spread = jnp.sum(center * center, axis=0, keepdims=True) * (1.0 / CH)
    return center * lax.rsqrt(spread + EPSILON)


def halved(weights):
    return (weights.astype(F32) * 0.5).astype(BF)


def side_by_side(values):
    return jnp.concatenate([values[a * CH : (a + 1) * CH] for a in range(ROWS)], axis=1)


def stacked(values):
    lanes = values.shape[1] // ROWS
    return jnp.concatenate([values[:, a * lanes : (a + 1) * lanes] for a in range(ROWS)], axis=0)


def pair_mask(crop_ref, length_ref, lanes, start):
    chip = lax.axis_index("row")
    inside = (chip % 8) * 16 + chip // 8
    length = length_ref[0]
    lane = iota((1, lanes), 1) + start
    position = lane_token(lane) % TILE
    for a in range(ROWS):
        position = position + jnp.where(lane % 8 == a, crop_ref[0, a] * TILE, 0)
    parts = []
    for a in range(ROWS):
        row_position = crop_ref[0, a] * TILE + inside
        parts.append(jnp.where((position < length) & (row_position < length), 1.0, 0.0))
    return jnp.concatenate(parts, axis=1)


def project(current, w, prow, mask, both_ref):
    values = dot_tn(halved(w[:, : 4 * CH]), norm_channels(current).astype(BF))
    lanes = both_ref.shape[1] // 2
    for side in range(2):
        gate = values[side * 128 : side * 128 + CH]
        value = values[side * 128 + CH : side * 128 + 2 * CH]
        factor = ((jnp.tanh(gate) + 1.0) * (value * mask)).astype(BF)
        both_ref[:, side * lanes : (side + 1) * lanes] = dot(prow, stacked(factor)).astype(BF)


BLOCK = 512
ANYWHERE = pl.BlockSpec(memory_space=pl.ANY)
RESIDENT = pl.BlockSpec(memory_space=pltpu.VMEM)
STEPS = CROP // BLOCK
HALF_STEPS = STEPS // 2
LAST_BLOCK = 512
LAST_STEPS = CROP // LAST_BLOCK
BOTH = pltpu.VMEM((512, 2 * CROP), BF)


def first_kernel(crop_ref, length_ref, got_ref, prow_ref, w_ref, cur_ref, both_ref):
    step = pl.program_id(0)
    parts = jnp.concatenate([got_ref[crop_ref[0, a]] for a in range(ROWS)], axis=0)
    order = onehot(iota((CROP, BLOCK), 0) == lane_token(iota((1, BLOCK), 1) + step * BLOCK))
    current = dot(parts, order)
    cur_ref[...] = current.astype(BF)
    mask = pair_mask(crop_ref, length_ref, BLOCK, step * BLOCK)
    project(side_by_side(current), w_ref[0], prow_ref[...], mask, both_ref)


def full(shape):
    return pl.BlockSpec(shape, lambda step, *_: (0,) * len(shape), pipeline_mode=pl.Buffered(1))


def lanes_of(rows, lanes=BLOCK, offset=0):
    return pl.BlockSpec((rows, lanes), lambda step, *_: (0, step + offset))


def layer_weight(columns, layer):
    return pl.BlockSpec((1, CH, columns), lambda step, *_: (layer, 0, 0), pipeline_mode=pl.Buffered(1))


def first_projection(crop_tiles, full_length, got, prow, proj_weight):
    return pl.pallas_call(
        first_kernel,
        grid_spec=pltpu.PrefetchScalarGridSpec(
            num_scalar_prefetch=2,
            grid=(STEPS,),
            in_specs=[RESIDENT, RESIDENT, layer_weight(320, 0)],
            out_specs=[lanes_of(512), lanes_of(512, 2 * BLOCK)],
        ),
        out_shape=[pltpu.HBM((512, CROP), BF), BOTH],
        compiler_params=pltpu.CompilerParams(vmem_limit_bytes=VMEM_LIMIT),
        name="first",
    )(crop_tiles, full_length, *in_vmem(got, prow), proj_weight)


def update(back_ref, cur_ref, prow, w_proj, w_out):
    block = cur_ref.shape[1]
    current = side_by_side(cur_ref[...].astype(F32))
    gate = jnp.tanh(dot_tn(halved(w_proj[:, 4 * CH :]), norm_channels(current).astype(BF))) + 1.0
    lanes = pl.ds(pl.multiple_of(pl.program_id(0) * block, block), block)
    products = side_by_side(dot_tn(prow, back_ref[:, lanes]))
    change = dot_tn(halved(w_out), norm_channels(products).astype(BF))
    return (current + gate * change).astype(BF)


def middle_kernel(
    crop_ref, length_ref, back_ref, cur_ref, prow_ref, w_ref, w_out_ref, w_next_ref, next_ref, both_ref
):
    current = update(back_ref, cur_ref, prow_ref[...], w_ref[0], w_out_ref[0])
    next_ref[...] = stacked(current)
    mask = pair_mask(crop_ref, length_ref, BLOCK, pl.program_id(0) * BLOCK)
    project(current.astype(F32), w_next_ref[0], prow_ref[...], mask, both_ref)


def middle_layer(crop_tiles, full_length, back, current, prow, proj_weight, out_weight, layer):
    return pl.pallas_call(
        middle_kernel,
        grid_spec=pltpu.PrefetchScalarGridSpec(
            num_scalar_prefetch=2,
            grid=(STEPS,),
            in_specs=[
                RESIDENT, lanes_of(512), RESIDENT,
                layer_weight(320, layer), layer_weight(CH, layer), layer_weight(320, layer + 1),
            ],
            out_specs=[lanes_of(512), lanes_of(512, 2 * BLOCK)],
        ),
        out_shape=[pltpu.HBM((512, CROP), BF), BOTH],
        compiler_params=pltpu.CompilerParams(vmem_limit_bytes=VMEM_LIMIT),
        name="middle",
    )(
        crop_tiles, full_length, *in_vmem(back), *in_hbm(current), *in_vmem(prow), proj_weight, out_weight,
        proj_weight,
    )


def last_rows(back_ref, cur_ref, prow_ref, w_ref, w_out_ref):
    current = update(back_ref, cur_ref, prow_ref[...], w_ref[0], w_out_ref[0])
    return stacked(norm_channels(current.astype(F32)).astype(BF))


def last_kernel(back_ref, cur_ref, prow_ref, w_ref, w_out_ref, pj_hbm, mine_ref, other_ref, rows_ref, pj_ref, sem):
    step = pl.program_id(0)
    load = pltpu.make_async_copy(pj_hbm, pj_ref, sem)

    @pl.when(step == 0)
    def _():
        load.start()

    lanes = pl.ds(pl.multiple_of(step * LAST_BLOCK, LAST_BLOCK), LAST_BLOCK)
    rows_ref[:, lanes] = last_rows(back_ref, cur_ref, prow_ref, w_ref, w_out_ref)

    @pl.when(step == LAST_STEPS - 1)
    def _():
        load.wait()
        core = lax.axis_index("tmpl")
        pj = pj_ref[...]
        mine_ref[...] = dot_nt(pj, rows_ref[pl.ds(pl.multiple_of(core * 256, 256), 256), :]).astype(BF)
        other_ref[...] = dot_nt(pj, rows_ref[pl.ds(pl.multiple_of(256 - core * 256, 256), 256), :]).astype(BF)


def last_layer(back, current, prow, proj_weight, out_weight, pj, layer):
    return pl.pallas_call(
        last_kernel,
        grid=(LAST_STEPS,),
        in_specs=[
            RESIDENT, lanes_of(512, LAST_BLOCK), RESIDENT, layer_weight(320, layer), layer_weight(CH, layer), ANYWHERE
        ],
        out_specs=[full((CROP, 256))] * 2,
        out_shape=[jax.ShapeDtypeStruct((CROP, 256), BF)] * 2,
        scratch_shapes=[pltpu.VMEM((512, CROP), BF), pltpu.VMEM((CROP, CROP), BF), pltpu.SemaphoreType.DMA],
        compiler_params=pltpu.CompilerParams(vmem_limit_bytes=VMEM_LIMIT),
        name="last",
    )(*in_vmem(back), *in_hbm(current), *in_vmem(prow), proj_weight, out_weight, *in_hbm(pj))


def right_kernel(both_ref, right_hbm, sems):
    copies = []
    for block in range(STEPS):
        source = both_ref.at[:, pl.ds((2 * block + 1) * BLOCK, BLOCK)]
        place = right_hbm.at[:, pl.ds(block * BLOCK, BLOCK)]
        copies.append(pltpu.make_async_copy(source, place, sems.at[block]))
    for copy in copies:
        copy.start()
    for copy in copies:
        copy.wait()


def right_alone(both):
    return pl.pallas_call(
        right_kernel,
        in_specs=[RESIDENT],
        out_specs=ANYWHERE,
        out_shape=pltpu.HBM((512, CROP), BF),
        scratch_shapes=[pltpu.SemaphoreType.DMA((STEPS,))],
        compiler_params=pltpu.CompilerParams(vmem_limit_bytes=VMEM_LIMIT),
        cost_estimate=pl.CostEstimate(flops=0, bytes_accessed=2 * 2**20, transcendentals=0),
        name="right",
    )(both)


def lane_blocks(both_ref, side, order):
    starts = [(2 * block + side) * BLOCK for block in order]
    return jnp.concatenate([both_ref[:, start : start + BLOCK] for start in starts], axis=1)


def products_kernel(peer, *refs):
    both_ref, right_ref = refs[0], refs[1]
    out_hbm, square_ref, sem = refs[-3:]
    if peer:
        left, right = lane_blocks(both_ref, 0, [1, 0]), right_ref[...]
    else:
        left, right = lane_blocks(both_ref, 0, [0, 1]), lane_blocks(both_ref, 1, [0, 1])
    square_ref[...] = dot_nt(left, right).astype(BF)
    store = pltpu.make_async_copy(square_ref, out_hbm.at[:, pl.ds(512 * peer, 512)], sem)
    store.start()
    store.wait()


def half_products(both, *others):
    peer = len(others) // 2
    return pl.pallas_call(
        functools.partial(products_kernel, peer),
        in_specs=[RESIDENT, RESIDENT, ANYWHERE][: 1 + len(others)],
        out_specs=ANYWHERE,
        out_shape=pltpu.HBM((512, CROP), BF),
        input_output_aliases={2: 0} if peer else {},
        scratch_shapes=[pltpu.VMEM((512, 512), BF), pltpu.SemaphoreType.DMA],
        compiler_params=pltpu.CompilerParams(vmem_limit_bytes=VMEM_LIMIT),
        cost_estimate=pl.CostEstimate(flops=2**29, bytes_accessed=4 * 2**20, transcendentals=0),
        name="products" + str(peer),
    )(both, *others)


def hidden_features(mine, peer):
    total = mine.astype(F32) + peer.astype(F32)
    return jnp.maximum(total * 0.5, 0.0).astype(BF)


def final_kernel(source, *refs):
    rows_ref, wf_ref = refs[:2]
    out_hbm, tall0_ref, tall1_ref, wide_ref, stage_ref, sems = refs[-6:]
    core = lax.axis_index("tmpl")
    half = core if source == 0 else 1 - core
    wf = wf_ref[...]
    tall0_ref[...] = rows_ref[:, :128].astype(F32)
    tall1_ref[...] = rows_ref[:, 128:].astype(F32)
    for j in range(8):
        rows = jnp.concatenate(
            [tall0_ref[pl.ds(j, 128, stride=8), :], tall1_ref[pl.ds(j, 128, stride=8), :]], axis=1
        ).astype(BF)
        result = dot_nt(wf, rows)
        for a in range(4):
            wide_ref[a, pl.ds(j, CZ, stride=8), :] = result[a * CZ : (a + 1) * CZ]
    stores = []
    for a in range(4):
        lanes = pl.ds(a * TILE, TILE)
        stage_ref[:, lanes] = wide_ref[a].astype(BF)
        place = pl.ds(pl.multiple_of(half * 512 + a * TILE, TILE), TILE)
        store = pltpu.make_async_copy(stage_ref.at[:, lanes], out_hbm.at[:, place], sems.at[a])
        store.start()
        stores.append(store)
    for store in stores:
        store.wait()


def final_projection(source, rows, wf, earlier=()):
    return pl.pallas_call(
        functools.partial(final_kernel, source),
        in_specs=[RESIDENT, RESIDENT] + [ANYWHERE] * len(earlier),
        out_specs=ANYWHERE,
        out_shape=pltpu.HBM((CZ * 8, CROP), BF),
        input_output_aliases={2 + k: 0 for k in range(len(earlier))},
        scratch_shapes=[
            pltpu.VMEM((CROP, 128), F32), pltpu.VMEM((CROP, 128), F32), pltpu.VMEM((4, CZ * 8, TILE), F32),
            pltpu.VMEM((CZ * 8, 512), BF), pltpu.SemaphoreType.DMA((4,)),
        ],
        compiler_params=pltpu.CompilerParams(vmem_limit_bytes=VMEM_LIMIT),
        cost_estimate=pl.CostEstimate(flops=2**28, bytes_accessed=2 * 2**20, transcendentals=0),
        name="final" + str(source),
    )(rows, wf, *earlier)


def exchange(values, axes, groups, count):
    cube = values.reshape(count, -1, values.shape[-1])
    moved = lax.all_to_all(cube, axes, 0, 0, axis_index_groups=groups, tiled=True)
    return moved.reshape(values.shape)


def on_device(pair_maps, crop_tiles, full_length, proj_weight, out_weight, final_weight):
    wf, prow, pj = make_tables(final_weight)
    pair = jnp.transpose(pair_maps[0], (0, 2, 1))
    cropped = crop_columns(crop_tiles, pair)
    got = lax.all_to_all(cropped, "row", 0, 0, axis_index_groups=PLANE, tiled=True)
    current, both = first_projection(crop_tiles, full_length, got, prow, proj_weight)
    weights = (prow, proj_weight, out_weight)
    for layer in range(NLAYER):
        gathered = exchange(both, BOTH_AXES, SAME_PART, CH)
        right_peer = lax.ppermute(right_alone(gathered), BOTH_AXES, OTHER_PART)
        products = half_products(gathered, right_peer, half_products(gathered))
        back = exchange(products, BOTH_AXES, SAME_PART, CH)
        if layer + 1 < NLAYER:
            current, both = middle_layer(crop_tiles, full_length, back, current, *weights, layer)
    mine, other = last_layer(back, current, *weights, pj, NLAYER - 1)
    hidden = hidden_features(mine, lax.ppermute(other, "tmpl", CORES))
    moved = exchange(hidden, "row", BY_Z, 128)
    result = final_projection(0, moved, wf)
    result = final_projection(1, lax.ppermute(moved, "tmpl", CORES), wf, (result,))
    return result.reshape(CZ, 8, CROP)


def solution(mesh):
    placed = (P("tmpl", "row", None, None), P("tmpl", None), P(), P(), P(), P())
    return jax.shard_map(
        on_device, mesh=mesh, in_specs=placed, out_specs=P(None, "row", None), check_vma=False
    )
```

```python
import functools

import jax
import jax.numpy as jnp
from jax import lax
from jax.experimental import pallas as pl
from jax.experimental.pallas import tpu as pltpu
from jax.sharding import PartitionSpec as P

CH = 64
CZ = 128
CROP = 1024
TILE = 128
NLAYER = 2
FULL = 2048
ROWS = 8
EPSILON = 1e-05
BF = jnp.bfloat16
F32 = jnp.float32

PLANE = [[s * 8 + z for s in range(16)] for z in range(8)]
BOTH_AXES = ("tmpl", "row")
SAME_PART = [
    [t * 128 + s * 8 + ((7 - zi if part else zi) + 2 * t) % 8 for s in range(16) for zi in range(4)]
    for t in range(2)
    for part in range(2)
]
OTHER_PART = [
    (t * 128 + s * 8 + z, t * 128 + s * 8 + (7 + 4 * t - z) % 8) for t in range(2) for s in range(16) for z in range(8)
]
BY_Z = [[s * 8 + z for z in range(8) for s in range(16)]]
CORES = [(0, 1), (1, 0)]
VMEM_LIMIT = 24 * 1024 * 1024


def in_vmem(*arrays):
    return [pltpu.with_memory_space_constraint(array, pltpu.VMEM) for array in arrays]


def in_hbm(*arrays):
    return [pltpu.with_memory_space_constraint(array, pltpu.HBM) for array in arrays]


def iota(shape, dim):
    return lax.broadcasted_iota(jnp.int32, shape, dim)


def onehot(mask):
    return jnp.where(mask, 1.0, 0.0).astype(BF)


def dot(a, b):
    return jnp.dot(a, b, preferred_element_type=F32)


def dot_nt(a, b):
    return lax.dot_general(a, b, (((1,), (1,)), ((), ())), preferred_element_type=F32)


def dot_tn(a, b):
    return lax.dot_general(a, b, (((0,), (0,)), ((), ())), preferred_element_type=F32)


def lane_token(lane):
    core, chip = lax.axis_index("tmpl"), lax.axis_index("row")
    part = (lane // 512) ^ (((chip % 8 + 8 - 2 * core) % 8) // 4)
    place = (lane // 8) % 4
    z = (jnp.where(part == 0, place, 7 - place) + 2 * core) % 8
    return (lane % 8) * 128 + z * 16 + (lane // 32) % 16


def tables_kernel(final_ref, wf_ref, prow_ref, pj_ref):
    down = onehot(iota((512, CZ), 0) % CZ == iota((512, CZ), 1))
    across = onehot(iota((CH, 256), 0) == iota((CH, 256), 1) % CH)
    tall = dot_nt(down, final_ref[...]).astype(BF)
    block = iota((512, 256), 0) // CZ == iota((512, 256), 1) // CH
    wf_ref[...] = jnp.where(block, dot(tall, across), 0.0).astype(BF)
    r0, c0 = iota((512, 512), 0), iota((512, 512), 1)
    prow_ref[...] = onehot((r0 // 8 == c0 % CH) & (r0 % 8 == c0 // CH))
    r1, c1 = iota((CROP, CROP), 0), iota((CROP, CROP), 1)
    token = lane_token(c1)
    dest = r1 // 8
    pj_ref[...] = onehot(((dest % 16) * 8 + dest // 16) * 8 + r1 % 8 == token)


def make_tables(final_weight):
    return pl.pallas_call(
        tables_kernel,
        out_shape=[
            pltpu.VMEM((512, 256), BF), pltpu.VMEM((512, 512), BF),
            pltpu.HBM((CROP, CROP), BF),
        ],
        compiler_params=pltpu.CompilerParams(vmem_limit_bytes=40 * 1024 * 1024),
        cost_estimate=pl.CostEstimate(flops=10**9, bytes_accessed=6 * 2**20, transcendentals=0),
        name="tables",
    )(final_weight)


CROP_CHUNKS = 4


def crop_kernel(crop_ref, x_hbm, o_hbm, rows_ref, in_sems, out_sems):
    size = 16 // CROP_CHUNKS
    loads, stores = [], []
    for chunk in range(CROP_CHUNKS):
        rows = pl.ds(chunk * size, size)
        for a in range(8):
            tile = pl.ds(pl.multiple_of(crop_ref[0, a] * TILE, TILE), TILE)
            load = pltpu.make_async_copy(
                x_hbm.at[rows, :, tile], rows_ref.at[rows, :, pl.ds(a * TILE, TILE)], in_sems.at[chunk * 8 + a]
            )
            load.start()
            loads.append(load)
    for chunk in range(CROP_CHUNKS):
        rows = pl.ds(chunk * size, size)
        for load in loads[chunk * 8 : chunk * 8 + 8]:
            load.wait()
        store = pltpu.make_async_copy(rows_ref.at[rows], o_hbm.at[rows], out_sems.at[chunk])
        store.start()
        stores.append(store)
    for store in stores:
        store.wait()


def crop_columns(crop_tiles, pair):
    return pl.pallas_call(
        crop_kernel,
        grid_spec=pltpu.PrefetchScalarGridSpec(
            num_scalar_prefetch=1,
            grid=(1,),
            in_specs=[pl.BlockSpec(memory_space=pl.ANY)],
            out_specs=pl.BlockSpec(memory_space=pl.ANY),
            scratch_shapes=[
                pltpu.VMEM((16, CH, CROP), BF),
                pltpu.SemaphoreType.DMA((8 * CROP_CHUNKS,)),
                pltpu.SemaphoreType.DMA((CROP_CHUNKS,)),
            ],
        ),
        out_shape=pltpu.HBM((16, CH, CROP), BF),
        compiler_params=pltpu.CompilerParams(vmem_limit_bytes=VMEM_LIMIT),
        name="crop",
    )(crop_tiles, *in_hbm(pair))


def norm_channels(values):
    center = values - jnp.sum(values, axis=0, keepdims=True) * (1.0 / CH)
    spread = jnp.sum(center * center, axis=0, keepdims=True) * (1.0 / CH)
    return center * lax.rsqrt(spread + EPSILON)


def halved(weights):
    return (weights.astype(F32) * 0.5).astype(BF)


def side_by_side(values):
    return jnp.concatenate([values[a * CH : (a + 1) * CH] for a in range(ROWS)], axis=1)


def stacked(values):
    lanes = values.shape[1] // ROWS
    return jnp.concatenate([values[:, a * lanes : (a + 1) * lanes] for a in range(ROWS)], axis=0)


def pair_mask(crop_ref, length_ref, lanes, start):
    chip = lax.axis_index("row")
    inside = (chip % 8) * 16 + chip // 8
    length = length_ref[0]
    lane = iota((1, lanes), 1) + start
    position = lane_token(lane) % TILE
    for a in range(ROWS):
        position = position + jnp.where(lane % 8 == a, crop_ref[0, a] * TILE, 0)
    parts = []
    for a in range(ROWS):
        row_position = crop_ref[0, a] * TILE + inside
        parts.append(jnp.where((position < length) & (row_position < length), 1.0, 0.0))
    return jnp.concatenate(parts, axis=1)


def project(current, w, prow, mask, both_ref):
    values = dot_tn(halved(w[:, : 4 * CH]), norm_channels(current).astype(BF))
    lanes = both_ref.shape[1] // 2
    for side in range(2):
        gate = values[side * 128 : side * 128 + CH]
        value = values[side * 128 + CH : side * 128 + 2 * CH]
        factor = ((jnp.tanh(gate) + 1.0) * (value * mask)).astype(BF)
        both_ref[:, side * lanes : (side + 1) * lanes] = dot(prow, stacked(factor)).astype(BF)


BLOCK = 512
ANYWHERE = pl.BlockSpec(memory_space=pl.ANY)
RESIDENT = pl.BlockSpec(memory_space=pltpu.VMEM)
STEPS = CROP // BLOCK
HALF_STEPS = STEPS // 2
LAST_BLOCK = 512
LAST_STEPS = CROP // LAST_BLOCK
BOTH = pltpu.VMEM((512, 2 * CROP), BF)


def first_kernel(crop_ref, length_ref, got_ref, prow_ref, w_ref, cur_ref, both_ref):
    step = pl.program_id(0)
    parts = jnp.concatenate([got_ref[crop_ref[0, a]] for a in range(ROWS)], axis=0)
    order = onehot(iota((CROP, BLOCK), 0) == lane_token(iota((1, BLOCK), 1) + step * BLOCK))
    current = dot(parts, order)
    cur_ref[...] = current.astype(BF)
    mask = pair_mask(crop_ref, length_ref, BLOCK, step * BLOCK)
    project(side_by_side(current), w_ref[0], prow_ref[...], mask, both_ref)


def full(shape):
    return pl.BlockSpec(shape, lambda step, *_: (0,) * len(shape), pipeline_mode=pl.Buffered(1))


def lanes_of(rows, lanes=BLOCK, offset=0):
    return pl.BlockSpec((rows, lanes), lambda step, *_: (0, step + offset))


def layer_weight(columns, layer):
    return pl.BlockSpec((1, CH, columns), lambda step, *_: (layer, 0, 0), pipeline_mode=pl.Buffered(1))


def first_projection(crop_tiles, full_length, got, prow, proj_weight):
    return pl.pallas_call(
        first_kernel,
        grid_spec=pltpu.PrefetchScalarGridSpec(
            num_scalar_prefetch=2,
            grid=(STEPS,),
            in_specs=[RESIDENT, RESIDENT, layer_weight(320, 0)],
            out_specs=[lanes_of(512), lanes_of(512, 2 * BLOCK)],
        ),
        out_shape=[pltpu.VMEM((512, CROP), BF), BOTH],
        compiler_params=pltpu.CompilerParams(vmem_limit_bytes=VMEM_LIMIT),
        name="first",
    )(crop_tiles, full_length, *in_vmem(got, prow), proj_weight)


def update(back_ref, cur_ref, prow, w_proj, w_out):
    block = cur_ref.shape[1]
    current = side_by_side(cur_ref[...].astype(F32))
    gate = jnp.tanh(dot_tn(halved(w_proj[:, 4 * CH :]), norm_channels(current).astype(BF))) + 1.0
    lanes = pl.ds(pl.multiple_of(pl.program_id(0) * block, block), block)
    products = side_by_side(dot_tn(prow, back_ref[:, lanes]))
    change = dot_tn(halved(w_out), norm_channels(products).astype(BF))
    return (current + gate * change).astype(BF)


def middle_kernel(
    crop_ref, length_ref, back_ref, cur_ref, prow_ref, w_ref, w_out_ref, w_next_ref, next_ref, both_ref
):
    current = update(back_ref, cur_ref, prow_ref[...], w_ref[0], w_out_ref[0])
    next_ref[...] = stacked(current)
    mask = pair_mask(crop_ref, length_ref, BLOCK, pl.program_id(0) * BLOCK)
    project(current.astype(F32), w_next_ref[0], prow_ref[...], mask, both_ref)


def middle_layer(crop_tiles, full_length, back, current, prow, proj_weight, out_weight, layer):
    return pl.pallas_call(
        middle_kernel,
        grid_spec=pltpu.PrefetchScalarGridSpec(
            num_scalar_prefetch=2,
            grid=(STEPS,),
            in_specs=[
                RESIDENT, lanes_of(512), RESIDENT,
                layer_weight(320, layer), layer_weight(CH, layer), layer_weight(320, layer + 1),
            ],
            out_specs=[lanes_of(512), lanes_of(512, 2 * BLOCK)],
        ),
        out_shape=[pltpu.VMEM((512, CROP), BF), BOTH],
        compiler_params=pltpu.CompilerParams(vmem_limit_bytes=VMEM_LIMIT),
        name="middle",
    )(
        crop_tiles, full_length, *in_vmem(back, current, prow), proj_weight, out_weight,
        proj_weight,
    )


def last_rows(back_ref, cur_ref, prow_ref, w_ref, w_out_ref):
    current = update(back_ref, cur_ref, prow_ref[...], w_ref[0], w_out_ref[0])
    return stacked(norm_channels(current.astype(F32)).astype(BF))


def last_kernel(back_ref, cur_ref, prow_ref, w_ref, w_out_ref, pj_hbm, mine_ref, other_ref, rows_ref, pj_ref, sem):
    step = pl.program_id(0)
    load = pltpu.make_async_copy(pj_hbm, pj_ref, sem)

    @pl.when(step == 0)
    def _():
        load.start()

    lanes = pl.ds(pl.multiple_of(step * LAST_BLOCK, LAST_BLOCK), LAST_BLOCK)
    rows_ref[:, lanes] = last_rows(back_ref, cur_ref, prow_ref, w_ref, w_out_ref)

    @pl.when(step == LAST_STEPS - 1)
    def _():
        load.wait()
        core = lax.axis_index("tmpl")
        pj = pj_ref[...]
        mine_ref[...] = dot_nt(pj, rows_ref[pl.ds(pl.multiple_of(core * 256, 256), 256), :]).astype(BF)
        other_ref[...] = dot_nt(pj, rows_ref[pl.ds(pl.multiple_of(256 - core * 256, 256), 256), :]).astype(BF)


def last_layer(back, current, prow, proj_weight, out_weight, pj, layer):
    return pl.pallas_call(
        last_kernel,
        grid=(LAST_STEPS,),
        in_specs=[
            RESIDENT, lanes_of(512, LAST_BLOCK), RESIDENT, layer_weight(320, layer), layer_weight(CH, layer), ANYWHERE
        ],
        out_specs=[full((CROP, 256))] * 2,
        out_shape=[jax.ShapeDtypeStruct((CROP, 256), BF)] * 2,
        scratch_shapes=[pltpu.VMEM((512, CROP), BF), pltpu.VMEM((CROP, CROP), BF), pltpu.SemaphoreType.DMA],
        compiler_params=pltpu.CompilerParams(vmem_limit_bytes=VMEM_LIMIT),
        name="last",
    )(*in_vmem(back, current, prow), proj_weight, out_weight, *in_hbm(pj))


def right_kernel(both_ref, right_hbm, sems):
    copies = []
    for block in range(STEPS):
        source = both_ref.at[:, pl.ds((2 * block + 1) * BLOCK, BLOCK)]
        place = right_hbm.at[:, pl.ds(block * BLOCK, BLOCK)]
        copies.append(pltpu.make_async_copy(source, place, sems.at[block]))
    for copy in copies:
        copy.start()
    for copy in copies:
        copy.wait()


def right_alone(both):
    return pl.pallas_call(
        right_kernel,
        in_specs=[RESIDENT],
        out_specs=ANYWHERE,
        out_shape=pltpu.HBM((512, CROP), BF),
        scratch_shapes=[pltpu.SemaphoreType.DMA((STEPS,))],
        compiler_params=pltpu.CompilerParams(vmem_limit_bytes=VMEM_LIMIT),
        cost_estimate=pl.CostEstimate(flops=0, bytes_accessed=2 * 2**20, transcendentals=0),
        name="right",
    )(both)


def lane_blocks(both_ref, side, order):
    starts = [(2 * block + side) * BLOCK for block in order]
    return jnp.concatenate([both_ref[:, start : start + BLOCK] for start in starts], axis=1)


def own_products_kernel(both_ref, out_ref):
    out_ref[...] = dot_nt(lane_blocks(both_ref, 0, [0, 1]), lane_blocks(both_ref, 1, [0, 1])).astype(BF)


def all_products_kernel(both_ref, right_ref, own_ref, out_ref):
    out_ref[:, :512] = own_ref[...]
    out_ref[:, 512:] = dot_nt(lane_blocks(both_ref, 0, [1, 0]), right_ref[...]).astype(BF)


def products_call(kernel, lanes, *operands):
    return pl.pallas_call(
        kernel,
        in_specs=[RESIDENT] * len(operands),
        out_specs=RESIDENT,
        out_shape=pltpu.VMEM((512, lanes), BF),
        compiler_params=pltpu.CompilerParams(vmem_limit_bytes=VMEM_LIMIT),
        cost_estimate=pl.CostEstimate(flops=2**29, bytes_accessed=4 * 2**20, transcendentals=0),
        name="products" + str(lanes),
    )(*operands)


def hidden_features(mine, peer):
    total = mine.astype(F32) + peer.astype(F32)
    return jnp.maximum(total * 0.5, 0.0).astype(BF)


def final_kernel(source, *refs):
    rows_ref, wf_ref = refs[:2]
    out_hbm, tall0_ref, tall1_ref, wide_ref, stage_ref, sems = refs[-6:]
    core = lax.axis_index("tmpl")
    half = core if source == 0 else 1 - core
    wf = wf_ref[...]
    tall0_ref[...] = rows_ref[:, :128].astype(F32)
    tall1_ref[...] = rows_ref[:, 128:].astype(F32)
    for j in range(8):
        rows = jnp.concatenate(
            [tall0_ref[pl.ds(j, 128, stride=8), :], tall1_ref[pl.ds(j, 128, stride=8), :]], axis=1
        ).astype(BF)
        result = dot_nt(wf, rows)
        for a in range(4):
            wide_ref[a, pl.ds(j, CZ, stride=8), :] = result[a * CZ : (a + 1) * CZ]
    stores = []
    for a in range(4):
        lanes = pl.ds(a * TILE, TILE)
        stage_ref[:, lanes] = wide_ref[a].astype(BF)
        place = pl.ds(pl.multiple_of(half * 512 + a * TILE, TILE), TILE)
        store = pltpu.make_async_copy(stage_ref.at[:, lanes], out_hbm.at[:, place], sems.at[a])
        store.start()
        stores.append(store)
    for store in stores:
        store.wait()


def final_projection(source, rows, wf, earlier=()):
    return pl.pallas_call(
        functools.partial(final_kernel, source),
        in_specs=[RESIDENT, RESIDENT] + [ANYWHERE] * len(earlier),
        out_specs=ANYWHERE,
        out_shape=pltpu.HBM((CZ * 8, CROP), BF),
        input_output_aliases={2 + k: 0 for k in range(len(earlier))},
        scratch_shapes=[
            pltpu.VMEM((CROP, 128), F32), pltpu.VMEM((CROP, 128), F32), pltpu.VMEM((4, CZ * 8, TILE), F32),
            pltpu.VMEM((CZ * 8, 512), BF), pltpu.SemaphoreType.DMA((4,)),
        ],
        compiler_params=pltpu.CompilerParams(vmem_limit_bytes=VMEM_LIMIT),
        cost_estimate=pl.CostEstimate(flops=2**28, bytes_accessed=2 * 2**20, transcendentals=0),
        name="final" + str(source),
    )(rows, wf, *earlier)


def exchange(values, axes, groups, count):
    cube = values.reshape(count, -1, values.shape[-1])
    moved = lax.all_to_all(cube, axes, 0, 0, axis_index_groups=groups, tiled=True)
    return moved.reshape(values.shape)


def on_device(pair_maps, crop_tiles, full_length, proj_weight, out_weight, final_weight):
    wf, prow, pj = make_tables(final_weight)
    pair = jnp.transpose(pair_maps[0], (0, 2, 1))
    cropped = crop_columns(crop_tiles, pair)
    got = lax.all_to_all(cropped, "row", 0, 0, axis_index_groups=PLANE, tiled=True)
    current, both = first_projection(crop_tiles, full_length, got, prow, proj_weight)
    weights = (prow, proj_weight, out_weight)
    for layer in range(NLAYER):
        gathered = exchange(both, BOTH_AXES, SAME_PART, CH)
        right_peer = lax.ppermute(right_alone(gathered), BOTH_AXES, OTHER_PART)
        own = products_call(own_products_kernel, 512, gathered)
        products = products_call(all_products_kernel, CROP, gathered, right_peer, own)
        back = exchange(products, BOTH_AXES, SAME_PART, CH)
        if layer + 1 < NLAYER:
            current, both = middle_layer(crop_tiles, full_length, back, current, *weights, layer)
    mine, other = last_layer(back, current, *weights, pj, NLAYER - 1)
    hidden = hidden_features(mine, lax.ppermute(other, "tmpl", CORES))
    moved = exchange(hidden, "row", BY_Z, 128)
    result = final_projection(0, moved, wf)
    result = final_projection(1, lax.ppermute(moved, "tmpl", CORES), wf, (result,))
    return result.reshape(CZ, 8, CROP)


def solution(mesh):
    placed = (P("tmpl", "row", None, None), P("tmpl", None), P(), P(), P(), P())
    return jax.shard_map(
        on_device, mesh=mesh, in_specs=placed, out_specs=P(None, "row", None), check_vma=False
    )
```

```python
import functools

import jax
import jax.numpy as jnp
from jax import lax
from jax.experimental import pallas as pl
from jax.experimental.pallas import tpu as pltpu
from jax.sharding import PartitionSpec as P

CH = 64
CZ = 128
CROP = 1024
TILE = 128
NLAYER = 2
FULL = 2048
ROWS = 8
EPSILON = 1e-05
BF = jnp.bfloat16
F32 = jnp.float32

PLANE = [[s * 8 + z for s in range(16)] for z in range(8)]
BOTH_AXES = ("tmpl", "row")
SAME_PART = [
    [t * 128 + s * 8 + ((zi ^ 6 if part else zi) + 2 * t) % 8 for s in range(16) for zi in range(4)]
    for t in range(2)
    for part in range(2)
]
OTHER_PART = [
    (t * 128 + s * 8 + z, t * 128 + s * 8 + (((z - 2 * t) % 8 ^ 6) + 2 * t) % 8) for t in range(2) for s in range(16) for z in range(8)
]
BY_Z = [[s * 8 + z for z in range(8) for s in range(16)]]
CORES = [(0, 1), (1, 0)]
VMEM_LIMIT = 24 * 1024 * 1024


def in_vmem(*arrays):
    return [pltpu.with_memory_space_constraint(array, pltpu.VMEM) for array in arrays]


def in_hbm(*arrays):
    return [pltpu.with_memory_space_constraint(array, pltpu.HBM) for array in arrays]


def iota(shape, dim):
    return lax.broadcasted_iota(jnp.int32, shape, dim)


def onehot(mask):
    return jnp.where(mask, 1.0, 0.0).astype(BF)


def dot(a, b):
    return jnp.dot(a, b, preferred_element_type=F32)


def dot_nt(a, b):
    return lax.dot_general(a, b, (((1,), (1,)), ((), ())), preferred_element_type=F32)


def dot_tn(a, b):
    return lax.dot_general(a, b, (((0,), (0,)), ((), ())), preferred_element_type=F32)


def lane_token(lane):
    core, chip = lax.axis_index("tmpl"), lax.axis_index("row")
    part = (lane // 512) ^ (((chip % 8 + 8 - 2 * core) % 8) // 4)
    place = (lane // 8) % 4
    z = (jnp.where(part == 0, place, place ^ 6) + 2 * core) % 8
    return (lane % 8) * 128 + z * 16 + (lane // 32) % 16


def tables_kernel(final_ref, wf_ref, prow_ref, pj_ref):
    down = onehot(iota((512, CZ), 0) % CZ == iota((512, CZ), 1))
    across = onehot(iota((CH, 256), 0) == iota((CH, 256), 1) % CH)
    tall = dot_nt(down, final_ref[...]).astype(BF)
    block = iota((512, 256), 0) // CZ == iota((512, 256), 1) // CH
    wf_ref[...] = jnp.where(block, dot(tall, across), 0.0).astype(BF)
    r0, c0 = iota((512, 512), 0), iota((512, 512), 1)
    prow_ref[...] = onehot((r0 // 8 == c0 % CH) & (r0 % 8 == c0 // CH))
    r1, c1 = iota((CROP, CROP), 0), iota((CROP, CROP), 1)
    token = lane_token(c1)
    dest = r1 // 8
    pj_ref[...] = onehot(((dest % 16) * 8 + dest // 16) * 8 + r1 % 8 == token)


def make_tables(final_weight):
    return pl.pallas_call(
        tables_kernel,
        out_shape=[
            pltpu.VMEM((512, 256), BF), pltpu.VMEM((512, 512), BF),
            pltpu.HBM((CROP, CROP), BF),
        ],
        compiler_params=pltpu.CompilerParams(vmem_limit_bytes=40 * 1024 * 1024),
        cost_estimate=pl.CostEstimate(flops=10**9, bytes_accessed=6 * 2**20, transcendentals=0),
        name="tables",
    )(final_weight)


CROP_CHUNKS = 4


def crop_kernel(crop_ref, x_hbm, o_hbm, rows_ref, in_sems, out_sems):
    size = 16 // CROP_CHUNKS
    loads, stores = [], []
    for chunk in range(CROP_CHUNKS):
        rows = pl.ds(chunk * size, size)
        for a in range(8):
            tile = pl.ds(pl.multiple_of(crop_ref[0, a] * TILE, TILE), TILE)
            load = pltpu.make_async_copy(
                x_hbm.at[rows, :, tile], rows_ref.at[rows, :, pl.ds(a * TILE, TILE)], in_sems.at[chunk * 8 + a]
            )
            load.start()
            loads.append(load)
    for chunk in range(CROP_CHUNKS):
        rows = pl.ds(chunk * size, size)
        for load in loads[chunk * 8 : chunk * 8 + 8]:
            load.wait()
        store = pltpu.make_async_copy(rows_ref.at[rows], o_hbm.at[rows], out_sems.at[chunk])
        store.start()
        stores.append(store)
    for store in stores:
        store.wait()


def crop_columns(crop_tiles, pair):
    return pl.pallas_call(
        crop_kernel,
        grid_spec=pltpu.PrefetchScalarGridSpec(
            num_scalar_prefetch=1,
            grid=(1,),
            in_specs=[pl.BlockSpec(memory_space=pl.ANY)],
            out_specs=pl.BlockSpec(memory_space=pl.ANY),
            scratch_shapes=[
                pltpu.VMEM((16, CH, CROP), BF),
                pltpu.SemaphoreType.DMA((8 * CROP_CHUNKS,)),
                pltpu.SemaphoreType.DMA((CROP_CHUNKS,)),
            ],
        ),
        out_shape=pltpu.HBM((16, CH, CROP), BF),
        compiler_params=pltpu.CompilerParams(vmem_limit_bytes=VMEM_LIMIT),
        name="crop",
    )(crop_tiles, *in_hbm(pair))


def norm_channels(values):
    center = values - jnp.sum(values, axis=0, keepdims=True) * (1.0 / CH)
    spread = jnp.sum(center * center, axis=0, keepdims=True) * (1.0 / CH)
    return center * lax.rsqrt(spread + EPSILON)


def halved(weights):
    return (weights.astype(F32) * 0.5).astype(BF)


def side_by_side(values):
    return jnp.concatenate([values[a * CH : (a + 1) * CH] for a in range(ROWS)], axis=1)


def stacked(values):
    lanes = values.shape[1] // ROWS
    return jnp.concatenate([values[:, a * lanes : (a + 1) * lanes] for a in range(ROWS)], axis=0)


def pair_mask(crop_ref, length_ref, lanes, start):
    chip = lax.axis_index("row")
    inside = (chip % 8) * 16 + chip // 8
    length = length_ref[0]
    lane = iota((1, lanes), 1) + start
    position = lane_token(lane) % TILE
    for a in range(ROWS):
        position = position + jnp.where(lane % 8 == a, crop_ref[0, a] * TILE, 0)
    parts = []
    for a in range(ROWS):
        row_position = crop_ref[0, a] * TILE + inside
        parts.append(jnp.where((position < length) & (row_position < length), 1.0, 0.0))
    return jnp.concatenate(parts, axis=1)


def project(current, w, prow, mask, both_ref):
    values = dot_tn(halved(w[:, : 4 * CH]), norm_channels(current).astype(BF))
    lanes = both_ref.shape[1] // 2
    for side in range(2):
        gate = values[side * 128 : side * 128 + CH]
        value = values[side * 128 + CH : side * 128 + 2 * CH]
        factor = ((jnp.tanh(gate) + 1.0) * (value * mask)).astype(BF)
        both_ref[:, side * lanes : (side + 1) * lanes] = dot(prow, stacked(factor)).astype(BF)


BLOCK = 512
ANYWHERE = pl.BlockSpec(memory_space=pl.ANY)
RESIDENT = pl.BlockSpec(memory_space=pltpu.VMEM)
STEPS = CROP // BLOCK
HALF_STEPS = STEPS // 2
LAST_BLOCK = 512
LAST_STEPS = CROP // LAST_BLOCK
BOTH = pltpu.VMEM((512, 2 * CROP), BF)


def first_kernel(crop_ref, length_ref, got_ref, prow_ref, w_ref, cur_ref, both_ref):
    step = pl.program_id(0)
    parts = jnp.concatenate([got_ref[crop_ref[0, a]] for a in range(ROWS)], axis=0)
    order = onehot(iota((CROP, BLOCK), 0) == lane_token(iota((1, BLOCK), 1) + step * BLOCK))
    current = dot(parts, order)
    cur_ref[...] = current.astype(BF)
    mask = pair_mask(crop_ref, length_ref, BLOCK, step * BLOCK)
    project(side_by_side(current), w_ref[0], prow_ref[...], mask, both_ref)


def full(shape):
    return pl.BlockSpec(shape, lambda step, *_: (0,) * len(shape), pipeline_mode=pl.Buffered(1))


def lanes_of(rows, lanes=BLOCK, offset=0):
    return pl.BlockSpec((rows, lanes), lambda step, *_: (0, step + offset))


def layer_weight(columns, layer):
    return pl.BlockSpec((1, CH, columns), lambda step, *_: (layer, 0, 0), pipeline_mode=pl.Buffered(1))


def first_projection(crop_tiles, full_length, got, prow, proj_weight):
    return pl.pallas_call(
        first_kernel,
        grid_spec=pltpu.PrefetchScalarGridSpec(
            num_scalar_prefetch=2,
            grid=(STEPS,),
            in_specs=[RESIDENT, RESIDENT, layer_weight(320, 0)],
            out_specs=[lanes_of(512), lanes_of(512, 2 * BLOCK)],
        ),
        out_shape=[pltpu.VMEM((512, CROP), BF), BOTH],
        compiler_params=pltpu.CompilerParams(vmem_limit_bytes=VMEM_LIMIT),
        name="first",
    )(crop_tiles, full_length, *in_vmem(got, prow), proj_weight)


def update(back_ref, cur_ref, prow, w_proj, w_out):
    block = cur_ref.shape[1]
    current = side_by_side(cur_ref[...].astype(F32))
    gate = jnp.tanh(dot_tn(halved(w_proj[:, 4 * CH :]), norm_channels(current).astype(BF))) + 1.0
    lanes = pl.ds(pl.multiple_of(pl.program_id(0) * block, block), block)
    products = side_by_side(dot_tn(prow, back_ref[:, lanes]))
    change = dot_tn(halved(w_out), norm_channels(products).astype(BF))
    return (current + gate * change).astype(BF)


def middle_kernel(
    crop_ref, length_ref, back_ref, cur_ref, prow_ref, w_ref, w_out_ref, w_next_ref, next_ref, both_ref
):
    current = update(back_ref, cur_ref, prow_ref[...], w_ref[0], w_out_ref[0])
    next_ref[...] = stacked(current)
    mask = pair_mask(crop_ref, length_ref, BLOCK, pl.program_id(0) * BLOCK)
    project(current.astype(F32), w_next_ref[0], prow_ref[...], mask, both_ref)


def middle_layer(crop_tiles, full_length, back, current, prow, proj_weight, out_weight, layer):
    return pl.pallas_call(
        middle_kernel,
        grid_spec=pltpu.PrefetchScalarGridSpec(
            num_scalar_prefetch=2,
            grid=(STEPS,),
            in_specs=[
                RESIDENT, lanes_of(512), RESIDENT,
                layer_weight(320, layer), layer_weight(CH, layer), layer_weight(320, layer + 1),
            ],
            out_specs=[lanes_of(512), lanes_of(512, 2 * BLOCK)],
        ),
        out_shape=[pltpu.VMEM((512, CROP), BF), BOTH],
        compiler_params=pltpu.CompilerParams(vmem_limit_bytes=VMEM_LIMIT),
        name="middle",
    )(
        crop_tiles, full_length, *in_vmem(back, current, prow), proj_weight, out_weight,
        proj_weight,
    )


def last_rows(back_ref, cur_ref, prow_ref, w_ref, w_out_ref):
    current = update(back_ref, cur_ref, prow_ref[...], w_ref[0], w_out_ref[0])
    return stacked(norm_channels(current.astype(F32)).astype(BF))


def last_kernel(back_ref, cur_ref, prow_ref, w_ref, w_out_ref, pj_hbm, mine_ref, other_ref, rows_ref, pj_ref, sem):
    step = pl.program_id(0)
    load = pltpu.make_async_copy(pj_hbm, pj_ref, sem)

    @pl.when(step == 0)
    def _():
        load.start()

    lanes = pl.ds(pl.multiple_of(step * LAST_BLOCK, LAST_BLOCK), LAST_BLOCK)
    rows_ref[:, lanes] = last_rows(back_ref, cur_ref, prow_ref, w_ref, w_out_ref)

    @pl.when(step == LAST_STEPS - 1)
    def _():
        load.wait()
        core = lax.axis_index("tmpl")
        pj = pj_ref[...]
        mine_ref[...] = dot_nt(pj, rows_ref[pl.ds(pl.multiple_of(core * 256, 256), 256), :]).astype(BF)
        other_ref[...] = dot_nt(pj, rows_ref[pl.ds(pl.multiple_of(256 - core * 256, 256), 256), :]).astype(BF)


def last_layer(back, current, prow, proj_weight, out_weight, pj, layer):
    return pl.pallas_call(
        last_kernel,
        grid=(LAST_STEPS,),
        in_specs=[
            RESIDENT, lanes_of(512, LAST_BLOCK), RESIDENT, layer_weight(320, layer), layer_weight(CH, layer), ANYWHERE
        ],
        out_specs=[full((CROP, 256))] * 2,
        out_shape=[jax.ShapeDtypeStruct((CROP, 256), BF)] * 2,
        scratch_shapes=[pltpu.VMEM((512, CROP), BF), pltpu.VMEM((CROP, CROP), BF), pltpu.SemaphoreType.DMA],
        compiler_params=pltpu.CompilerParams(vmem_limit_bytes=VMEM_LIMIT),
        name="last",
    )(*in_vmem(back, current, prow), proj_weight, out_weight, *in_hbm(pj))


def right_kernel(both_ref, right_hbm, sems):
    copies = []
    for block in range(STEPS):
        source = both_ref.at[:, pl.ds((2 * block + 1) * BLOCK, BLOCK)]
        place = right_hbm.at[:, pl.ds(block * BLOCK, BLOCK)]
        copies.append(pltpu.make_async_copy(source, place, sems.at[block]))
    for copy in copies:
        copy.start()
    for copy in copies:
        copy.wait()


def right_alone(both):
    return pl.pallas_call(
        right_kernel,
        in_specs=[RESIDENT],
        out_specs=ANYWHERE,
        out_shape=pltpu.HBM((512, CROP), BF),
        scratch_shapes=[pltpu.SemaphoreType.DMA((STEPS,))],
        compiler_params=pltpu.CompilerParams(vmem_limit_bytes=VMEM_LIMIT),
        cost_estimate=pl.CostEstimate(flops=0, bytes_accessed=2 * 2**20, transcendentals=0),
        name="right",
    )(both)


def lane_blocks(both_ref, side, order):
    starts = [(2 * block + side) * BLOCK for block in order]
    return jnp.concatenate([both_ref[:, start : start + BLOCK] for start in starts], axis=1)


def own_products_kernel(both_ref, out_ref):
    out_ref[...] = dot_nt(lane_blocks(both_ref, 0, [0, 1]), lane_blocks(both_ref, 1, [0, 1])).astype(BF)


def all_products_kernel(both_ref, right_ref, own_ref, out_ref):
    out_ref[:, :512] = own_ref[...]
    out_ref[:, 512:] = dot_nt(lane_blocks(both_ref, 0, [1, 0]), right_ref[...]).astype(BF)


def products_call(kernel, lanes, *operands):
    return pl.pallas_call(
        kernel,
        in_specs=[RESIDENT] * len(operands),
        out_specs=RESIDENT,
        out_shape=pltpu.VMEM((512, lanes), BF),
        compiler_params=pltpu.CompilerParams(vmem_limit_bytes=VMEM_LIMIT),
        cost_estimate=pl.CostEstimate(flops=2**29, bytes_accessed=4 * 2**20, transcendentals=0),
        name="products" + str(lanes),
    )(*operands)


def hidden_features(mine, peer):
    total = mine.astype(F32) + peer.astype(F32)
    return jnp.maximum(total * 0.5, 0.0).astype(BF)


def final_kernel(source, *refs):
    rows_ref, wf_ref = refs[:2]
    out_hbm, tall0_ref, tall1_ref, wide_ref, stage_ref, sems = refs[-6:]
    core = lax.axis_index("tmpl")
    half = core if source == 0 else 1 - core
    wf = wf_ref[...]
    tall0_ref[...] = rows_ref[:, :128].astype(F32)
    tall1_ref[...] = rows_ref[:, 128:].astype(F32)
    for j in range(8):
        rows = jnp.concatenate(
            [tall0_ref[pl.ds(j, 128, stride=8), :], tall1_ref[pl.ds(j, 128, stride=8), :]], axis=1
        ).astype(BF)
        result = dot_nt(wf, rows)
        for a in range(4):
            wide_ref[a, pl.ds(j, CZ, stride=8), :] = result[a * CZ : (a + 1) * CZ]
    stores = []
    for a in range(4):
        lanes = pl.ds(a * TILE, TILE)
        stage_ref[:, lanes] = wide_ref[a].astype(BF)
        place = pl.ds(pl.multiple_of(half * 512 + a * TILE, TILE), TILE)
        store = pltpu.make_async_copy(stage_ref.at[:, lanes], out_hbm.at[:, place], sems.at[a])
        store.start()
        stores.append(store)
    for store in stores:
        store.wait()


def final_projection(source, rows, wf, earlier=()):
    return pl.pallas_call(
        functools.partial(final_kernel, source),
        in_specs=[RESIDENT, RESIDENT] + [ANYWHERE] * len(earlier),
        out_specs=ANYWHERE,
        out_shape=pltpu.HBM((CZ * 8, CROP), BF),
        input_output_aliases={2 + k: 0 for k in range(len(earlier))},
        scratch_shapes=[
            pltpu.VMEM((CROP, 128), F32), pltpu.VMEM((CROP, 128), F32), pltpu.VMEM((4, CZ * 8, TILE), F32),
            pltpu.VMEM((CZ * 8, 512), BF), pltpu.SemaphoreType.DMA((4,)),
        ],
        compiler_params=pltpu.CompilerParams(vmem_limit_bytes=VMEM_LIMIT),
        cost_estimate=pl.CostEstimate(flops=2**28, bytes_accessed=2 * 2**20, transcendentals=0),
        name="final" + str(source),
    )(rows, wf, *earlier)


def exchange(values, axes, groups, count):
    cube = values.reshape(count, -1, values.shape[-1])
    moved = lax.all_to_all(cube, axes, 0, 0, axis_index_groups=groups, tiled=True)
    return moved.reshape(values.shape)


def on_device(pair_maps, crop_tiles, full_length, proj_weight, out_weight, final_weight):
    wf, prow, pj = make_tables(final_weight)
    pair = jnp.transpose(pair_maps[0], (0, 2, 1))
    cropped = crop_columns(crop_tiles, pair)
    got = lax.all_to_all(cropped, "row", 0, 0, axis_index_groups=PLANE, tiled=True)
    current, both = first_projection(crop_tiles, full_length, got, prow, proj_weight)
    weights = (prow, proj_weight, out_weight)
    for layer in range(NLAYER):
        gathered = exchange(both, BOTH_AXES, SAME_PART, CH)
        right_peer = lax.ppermute(right_alone(gathered), BOTH_AXES, OTHER_PART)
        own = products_call(own_products_kernel, 512, gathered)
        products = products_call(all_products_kernel, CROP, gathered, right_peer, own)
        back = exchange(products, BOTH_AXES, SAME_PART, CH)
        if layer + 1 < NLAYER:
            current, both = middle_layer(crop_tiles, full_length, back, current, *weights, layer)
    mine, other = last_layer(back, current, *weights, pj, NLAYER - 1)
    hidden = hidden_features(mine, lax.ppermute(other, "tmpl", CORES))
    moved = exchange(hidden, "row", BY_Z, 128)
    result = final_projection(0, moved, wf)
    result = final_projection(1, lax.ppermute(moved, "tmpl", CORES), wf, (result,))
    return result.reshape(CZ, 8, CROP)


def solution(mesh):
    placed = (P("tmpl", "row", None, None), P("tmpl", None), P(), P(), P(), P())
    return jax.shard_map(
        on_device, mesh=mesh, in_specs=placed, out_specs=P(None, "row", None), check_vma=False
    )
```

```python
import functools

import jax
import jax.numpy as jnp
from jax import lax
from jax.experimental import pallas as pl
from jax.experimental.pallas import tpu as pltpu
from jax.sharding import PartitionSpec as P

CH = 64
CZ = 128
CROP = 1024
TILE = 128
NLAYER = 2
FULL = 2048
ROWS = 8
EPSILON = 1e-05
BF = jnp.bfloat16
F32 = jnp.float32

PLANE = [[s * 8 + z for s in range(16)] for z in range(8)]
BOTH_AXES = ("tmpl", "row")
SAME_PART = [
    [t * 128 + s * 8 + ((7 - zi if part else zi) + 2 * t) % 8 for s in range(16) for zi in range(4)]
    for t in range(2)
    for part in range(2)
]
OTHER_PART = [
    (t * 128 + s * 8 + z, t * 128 + s * 8 + (7 + 4 * t - z) % 8) for t in range(2) for s in range(16) for z in range(8)
]
BY_Z = [[s * 8 + z for z in range(8) for s in range(16)]]
CORES = [(0, 1), (1, 0)]
VMEM_LIMIT = 24 * 1024 * 1024


def in_vmem(*arrays):
    return [pltpu.with_memory_space_constraint(array, pltpu.VMEM) for array in arrays]


def in_hbm(*arrays):
    return [pltpu.with_memory_space_constraint(array, pltpu.HBM) for array in arrays]


def iota(shape, dim):
    return lax.broadcasted_iota(jnp.int32, shape, dim)


def onehot(mask):
    return jnp.where(mask, 1.0, 0.0).astype(BF)


def dot(a, b):
    return jnp.dot(a, b, preferred_element_type=F32)


def dot_nt(a, b):
    return lax.dot_general(a, b, (((1,), (1,)), ((), ())), preferred_element_type=F32)


def dot_tn(a, b):
    return lax.dot_general(a, b, (((0,), (0,)), ((), ())), preferred_element_type=F32)


def lane_token(lane):
    core, chip = lax.axis_index("tmpl"), lax.axis_index("row")
    part = (lane // 512) ^ (((chip % 8 + 8 - 2 * core) % 8) // 4)
    place = (lane // 8) % 4
    z = (jnp.where(part == 0, place, 7 - place) + 2 * core) % 8
    return (lane % 8) * 128 + z * 16 + (lane // 32) % 16


def tables_kernel(final_ref, wf_ref, prow_ref, pj_ref):
    down = onehot(iota((512, CZ), 0) % CZ == iota((512, CZ), 1))
    across = onehot(iota((CH, 256), 0) == iota((CH, 256), 1) % CH)
    tall = dot_nt(down, final_ref[...]).astype(BF)
    block = iota((512, 256), 0) // CZ == iota((512, 256), 1) // CH
    wf_ref[...] = jnp.where(block, dot(tall, across), 0.0).astype(BF)
    r0, c0 = iota((512, 512), 0), iota((512, 512), 1)
    prow_ref[...] = onehot((r0 // 8 == c0 % CH) & (r0 % 8 == c0 // CH))
    r1, c1 = iota((CROP, CROP), 0), iota((CROP, CROP), 1)
    token = lane_token(c1)
    dest = r1 // 8
    pj_ref[...] = onehot(((dest % 16) * 8 + dest // 16) * 8 + r1 % 8 == token)


def make_tables(final_weight):
    return pl.pallas_call(
        tables_kernel,
        out_shape=[
            pltpu.VMEM((512, 256), BF), pltpu.VMEM((512, 512), BF),
            pltpu.HBM((CROP, CROP), BF),
        ],
        compiler_params=pltpu.CompilerParams(vmem_limit_bytes=40 * 1024 * 1024),
        cost_estimate=pl.CostEstimate(flops=10**9, bytes_accessed=6 * 2**20, transcendentals=0),
        name="tables",
    )(final_weight)


CROP_CHUNKS = 4


def crop_kernel(crop_ref, x_hbm, o_hbm, rows_ref, in_sems, out_sems):
    size = 16 // CROP_CHUNKS
    loads, stores = [], []
    for chunk in range(CROP_CHUNKS):
        rows = pl.ds(chunk * size, size)
        for a in range(8):
            tile = pl.ds(pl.multiple_of(crop_ref[0, a] * TILE, TILE), TILE)
            load = pltpu.make_async_copy(
                x_hbm.at[rows, :, tile], rows_ref.at[rows, :, pl.ds(a * TILE, TILE)], in_sems.at[chunk * 8 + a]
            )
            load.start()
            loads.append(load)
    for chunk in range(CROP_CHUNKS):
        rows = pl.ds(chunk * size, size)
        for load in loads[chunk * 8 : chunk * 8 + 8]:
            load.wait()
        store = pltpu.make_async_copy(rows_ref.at[rows], o_hbm.at[rows], out_sems.at[chunk])
        store.start()
        stores.append(store)
    for store in stores:
        store.wait()


def crop_columns(crop_tiles, pair):
    return pl.pallas_call(
        crop_kernel,
        grid_spec=pltpu.PrefetchScalarGridSpec(
            num_scalar_prefetch=1,
            grid=(1,),
            in_specs=[pl.BlockSpec(memory_space=pl.ANY)],
            out_specs=pl.BlockSpec(memory_space=pl.ANY),
            scratch_shapes=[
                pltpu.VMEM((16, CH, CROP), BF),
                pltpu.SemaphoreType.DMA((8 * CROP_CHUNKS,)),
                pltpu.SemaphoreType.DMA((CROP_CHUNKS,)),
            ],
        ),
        out_shape=pltpu.HBM((16, CH, CROP), BF),
        compiler_params=pltpu.CompilerParams(vmem_limit_bytes=VMEM_LIMIT),
        name="crop",
    )(crop_tiles, *in_hbm(pair))


def norm_channels(values):
    center = values - jnp.sum(values, axis=0, keepdims=True) * (1.0 / CH)
    spread = jnp.sum(center * center, axis=0, keepdims=True) * (1.0 / CH)
    return center * lax.rsqrt(spread + EPSILON)


def halved(weights):
    return (weights.astype(F32) * 0.5).astype(BF)


def side_by_side(values):
    return jnp.concatenate([values[a * CH : (a + 1) * CH] for a in range(ROWS)], axis=1)


def stacked(values):
    lanes = values.shape[1] // ROWS
    return jnp.concatenate([values[:, a * lanes : (a + 1) * lanes] for a in range(ROWS)], axis=0)


def pair_mask(crop_ref, length_ref, lanes, start):
    chip = lax.axis_index("row")
    inside = (chip % 8) * 16 + chip // 8
    length = length_ref[0]
    lane = iota((1, lanes), 1) + start
    position = lane_token(lane) % TILE
    for a in range(ROWS):
        position = position + jnp.where(lane % 8 == a, crop_ref[0, a] * TILE, 0)
    parts = []
    for a in range(ROWS):
        row_position = crop_ref[0, a] * TILE + inside
        parts.append(jnp.where((position < length) & (row_position < length), 1.0, 0.0))
    return jnp.concatenate(parts, axis=1)


def project(current, w, prow, mask, both_ref):
    values = dot_tn(halved(w[:, : 4 * CH]), norm_channels(current).astype(BF))
    lanes = both_ref.shape[1] // 2
    for side in range(2):
        gate = values[side * 128 : side * 128 + CH]
        value = values[side * 128 + CH : side * 128 + 2 * CH]
        factor = ((jnp.tanh(gate) + 1.0) * (value * mask)).astype(BF)
        both_ref[:, side * lanes : (side + 1) * lanes] = dot(prow, stacked(factor)).astype(BF)


BLOCK = 512
ANYWHERE = pl.BlockSpec(memory_space=pl.ANY)
RESIDENT = pl.BlockSpec(memory_space=pltpu.VMEM)
STEPS = CROP // BLOCK
HALF_STEPS = STEPS // 2
LAST_BLOCK = 512
LAST_STEPS = CROP // LAST_BLOCK
BOTH = pltpu.VMEM((512, 2 * CROP), BF)


def first_kernel(crop_ref, length_ref, got_ref, prow_ref, w_ref, cur_ref, both_ref):
    step = pl.program_id(0)
    parts = jnp.concatenate([got_ref[crop_ref[0, a]] for a in range(ROWS)], axis=0)
    order = onehot(iota((CROP, BLOCK), 0) == lane_token(iota((1, BLOCK), 1) + step * BLOCK))
    current = dot(parts, order)
    cur_ref[...] = current.astype(BF)
    mask = pair_mask(crop_ref, length_ref, BLOCK, step * BLOCK)
    project(side_by_side(current), w_ref[0], prow_ref[...], mask, both_ref)


def full(shape):
    return pl.BlockSpec(shape, lambda step, *_: (0,) * len(shape), pipeline_mode=pl.Buffered(1))


def lanes_of(rows, lanes=BLOCK, offset=0):
    return pl.BlockSpec((rows, lanes), lambda step, *_: (0, step + offset))


def layer_weight(columns, layer):
    return pl.BlockSpec((1, CH, columns), lambda step, *_: (layer, 0, 0), pipeline_mode=pl.Buffered(1))


def first_projection(crop_tiles, full_length, got, prow, proj_weight):
    return pl.pallas_call(
        first_kernel,
        grid_spec=pltpu.PrefetchScalarGridSpec(
            num_scalar_prefetch=2,
            grid=(STEPS,),
            in_specs=[RESIDENT, RESIDENT, layer_weight(320, 0)],
            out_specs=[lanes_of(512), lanes_of(512, 2 * BLOCK)],
        ),
        out_shape=[pltpu.VMEM((512, CROP), BF), BOTH],
        compiler_params=pltpu.CompilerParams(vmem_limit_bytes=VMEM_LIMIT),
        name="first",
    )(crop_tiles, full_length, *in_vmem(got, prow), proj_weight)


def update(back_ref, cur_ref, prow, w_proj, w_out):
    block = cur_ref.shape[1]
    current = side_by_side(cur_ref[...].astype(F32))
    gate = jnp.tanh(dot_tn(halved(w_proj[:, 4 * CH :]), norm_channels(current).astype(BF))) + 1.0
    lanes = pl.ds(pl.multiple_of(pl.program_id(0) * block, block), block)
    products = side_by_side(dot_tn(prow, back_ref[:, lanes]))
    change = dot_tn(halved(w_out), norm_channels(products).astype(BF))
    return (current + gate * change).astype(BF)


def middle_kernel(
    crop_ref, length_ref, back_ref, cur_ref, prow_ref, w_ref, w_out_ref, w_next_ref, next_ref, both_ref
):
    current = update(back_ref, cur_ref, prow_ref[...], w_ref[0], w_out_ref[0])
    next_ref[...] = stacked(current)
    mask = pair_mask(crop_ref, length_ref, BLOCK, pl.program_id(0) * BLOCK)
    project(current.astype(F32), w_next_ref[0], prow_ref[...], mask, both_ref)


def middle_layer(crop_tiles, full_length, back, current, prow, proj_weight, out_weight, layer):
    return pl.pallas_call(
        middle_kernel,
        grid_spec=pltpu.PrefetchScalarGridSpec(
            num_scalar_prefetch=2,
            grid=(STEPS,),
            in_specs=[
                RESIDENT, lanes_of(512), RESIDENT,
                layer_weight(320, layer), layer_weight(CH, layer), layer_weight(320, layer + 1),
            ],
            out_specs=[lanes_of(512), lanes_of(512, 2 * BLOCK)],
        ),
        out_shape=[pltpu.VMEM((512, CROP), BF), BOTH],
        compiler_params=pltpu.CompilerParams(vmem_limit_bytes=VMEM_LIMIT),
        name="middle",
    )(
        crop_tiles, full_length, *in_vmem(back, current, prow), proj_weight, out_weight,
        proj_weight,
    )


def last_rows(back_ref, cur_ref, prow_ref, w_ref, w_out_ref):
    current = update(back_ref, cur_ref, prow_ref[...], w_ref[0], w_out_ref[0])
    return stacked(norm_channels(current.astype(F32)).astype(BF))


def last_kernel(back_ref, cur_ref, prow_ref, w_ref, w_out_ref, pj_hbm, mine_ref, other_ref, rows_ref, pj_ref, sem):
    step = pl.program_id(0)
    load = pltpu.make_async_copy(pj_hbm, pj_ref, sem)

    @pl.when(step == 0)
    def _():
        load.start()

    lanes = pl.ds(pl.multiple_of(step * LAST_BLOCK, LAST_BLOCK), LAST_BLOCK)
    rows_ref[:, lanes] = last_rows(back_ref, cur_ref, prow_ref, w_ref, w_out_ref)

    @pl.when(step == LAST_STEPS - 1)
    def _():
        load.wait()
        core = lax.axis_index("tmpl")
        pj = pj_ref[...]
        mine_ref[...] = dot_nt(pj, rows_ref[pl.ds(pl.multiple_of(core * 256, 256), 256), :]).astype(BF)
        other_ref[...] = dot_nt(pj, rows_ref[pl.ds(pl.multiple_of(256 - core * 256, 256), 256), :]).astype(BF)


def last_layer(back, current, prow, proj_weight, out_weight, pj, layer):
    return pl.pallas_call(
        last_kernel,
        grid=(LAST_STEPS,),
        in_specs=[
            RESIDENT, lanes_of(512, LAST_BLOCK), RESIDENT, layer_weight(320, layer), layer_weight(CH, layer), ANYWHERE
        ],
        out_specs=[full((CROP, 256))] * 2,
        out_shape=[jax.ShapeDtypeStruct((CROP, 256), BF)] * 2,
        scratch_shapes=[pltpu.VMEM((512, CROP), BF), pltpu.VMEM((CROP, CROP), BF), pltpu.SemaphoreType.DMA],
        compiler_params=pltpu.CompilerParams(vmem_limit_bytes=VMEM_LIMIT),
        name="last",
    )(*in_vmem(back, current, prow), proj_weight, out_weight, *in_hbm(pj))


def right_kernel(both_ref, right_ref):
    right_ref[...] = lane_blocks(both_ref, 1, [0, 1])


def right_alone(both):
    return pl.pallas_call(
        right_kernel,
        in_specs=[RESIDENT],
        out_specs=RESIDENT,
        out_shape=pltpu.VMEM((512, CROP), BF),
        compiler_params=pltpu.CompilerParams(vmem_limit_bytes=VMEM_LIMIT),
        cost_estimate=pl.CostEstimate(flops=0, bytes_accessed=2 * 2**20, transcendentals=0),
        name="right",
    )(both)


def lane_blocks(both_ref, side, order):
    starts = [(2 * block + side) * BLOCK for block in order]
    return jnp.concatenate([both_ref[:, start : start + BLOCK] for start in starts], axis=1)


def own_products_kernel(both_ref, out_ref):
    out_ref[...] = dot_nt(lane_blocks(both_ref, 0, [0, 1]), lane_blocks(both_ref, 1, [0, 1])).astype(BF)


def all_products_kernel(both_ref, right_ref, own_ref, out_ref):
    out_ref[:, :512] = own_ref[...]
    out_ref[:, 512:] = dot_nt(lane_blocks(both_ref, 0, [1, 0]), right_ref[...]).astype(BF)


def products_call(kernel, lanes, *operands):
    return pl.pallas_call(
        kernel,
        in_specs=[RESIDENT] * len(operands),
        out_specs=RESIDENT,
        out_shape=pltpu.VMEM((512, lanes), BF),
        compiler_params=pltpu.CompilerParams(vmem_limit_bytes=VMEM_LIMIT),
        cost_estimate=pl.CostEstimate(flops=2**29, bytes_accessed=4 * 2**20, transcendentals=0),
        name="products" + str(lanes),
    )(*operands)


def hidden_features(mine, peer):
    total = mine.astype(F32) + peer.astype(F32)
    return jnp.maximum(total * 0.5, 0.0).astype(BF)


def final_kernel(source, *refs):
    rows_ref, wf_ref = refs[:2]
    out_hbm, tall0_ref, tall1_ref, wide_ref, stage_ref, sems = refs[-6:]
    core = lax.axis_index("tmpl")
    half = core if source == 0 else 1 - core
    wf = wf_ref[...]
    tall0_ref[...] = rows_ref[:, :128].astype(F32)
    tall1_ref[...] = rows_ref[:, 128:].astype(F32)
    for j in range(8):
        rows = jnp.concatenate(
            [tall0_ref[pl.ds(j, 128, stride=8), :], tall1_ref[pl.ds(j, 128, stride=8), :]], axis=1
        ).astype(BF)
        result = dot_nt(wf, rows)
        for a in range(4):
            wide_ref[a, pl.ds(j, CZ, stride=8), :] = result[a * CZ : (a + 1) * CZ]
    stores = []
    for a in range(4):
        lanes = pl.ds(a * TILE, TILE)
        stage_ref[:, lanes] = wide_ref[a].astype(BF)
        place = pl.ds(pl.multiple_of(half * 512 + a * TILE, TILE), TILE)
        store = pltpu.make_async_copy(stage_ref.at[:, lanes], out_hbm.at[:, place], sems.at[a])
        store.start()
        stores.append(store)
    for store in stores:
        store.wait()


def final_projection(source, rows, wf, earlier=()):
    return pl.pallas_call(
        functools.partial(final_kernel, source),
        in_specs=[RESIDENT, RESIDENT] + [ANYWHERE] * len(earlier),
        out_specs=ANYWHERE,
        out_shape=pltpu.HBM((CZ * 8, CROP), BF),
        input_output_aliases={2 + k: 0 for k in range(len(earlier))},
        scratch_shapes=[
            pltpu.VMEM((CROP, 128), F32), pltpu.VMEM((CROP, 128), F32), pltpu.VMEM((4, CZ * 8, TILE), F32),
            pltpu.VMEM((CZ * 8, 512), BF), pltpu.SemaphoreType.DMA((4,)),
        ],
        compiler_params=pltpu.CompilerParams(vmem_limit_bytes=VMEM_LIMIT),
        cost_estimate=pl.CostEstimate(flops=2**28, bytes_accessed=2 * 2**20, transcendentals=0),
        name="final" + str(source),
    )(rows, wf, *earlier)


def exchange(values, axes, groups, count):
    cube = values.reshape(count, -1, values.shape[-1])
    moved = lax.all_to_all(cube, axes, 0, 0, axis_index_groups=groups, tiled=True)
    return moved.reshape(values.shape)


def on_device(pair_maps, crop_tiles, full_length, proj_weight, out_weight, final_weight):
    wf, prow, pj = make_tables(final_weight)
    pair = jnp.transpose(pair_maps[0], (0, 2, 1))
    cropped = crop_columns(crop_tiles, pair)
    got = lax.all_to_all(cropped, "row", 0, 0, axis_index_groups=PLANE, tiled=True)
    current, both = first_projection(crop_tiles, full_length, got, prow, proj_weight)
    weights = (prow, proj_weight, out_weight)
    for layer in range(NLAYER):
        gathered = exchange(both, BOTH_AXES, SAME_PART, CH)
        right_peer = lax.ppermute(right_alone(gathered), BOTH_AXES, OTHER_PART)
        own = products_call(own_products_kernel, 512, gathered)
        products = products_call(all_products_kernel, CROP, gathered, right_peer, own)
        back = exchange(products, BOTH_AXES, SAME_PART, CH)
        if layer + 1 < NLAYER:
            current, both = middle_layer(crop_tiles, full_length, back, current, *weights, layer)
    mine, other = last_layer(back, current, *weights, pj, NLAYER - 1)
    hidden = hidden_features(mine, lax.ppermute(other, "tmpl", CORES))
    moved = exchange(hidden, "row", BY_Z, 128)
    result = final_projection(0, moved, wf)
    result = final_projection(1, lax.ppermute(moved, "tmpl", CORES), wf, (result,))
    return result.reshape(CZ, 8, CROP)


def solution(mesh):
    placed = (P("tmpl", "row", None, None), P("tmpl", None), P(), P(), P(), P())
    return jax.shard_map(
        on_device, mesh=mesh, in_specs=placed, out_specs=P(None, "row", None), check_vma=False
    )
```
